32 devices in a mesh: seq: 8 (over z, y), head: 4 (over x, core).
Axes of the slice: x: 2, y: 2, z: 4, core: 2. Of those that a mesh axis runs over, the one named last changes fastest.
Arguments:
- source: bfloat16 [2, 8192, 768], P(None, ('seq', 'head')), may hold values from -6 to 6
- target: bfloat16 [2, 4096, 768], P(None, ('seq', 'head')), may hold values from -6 to 6
- cotangent: bfloat16 [2, 4096, 768], P(None, ('seq', 'head')), may hold values from -6 to 6
- src_lengths: int32 [2, 16], replicated, may hold values from 1 to 2048, 8192 in all within a row
- tgt_lengths: int32 [2, 8], replicated, may hold values from 1 to 1024, 4096 in all within a row
- retrieved: int32 [2, 1024], replicated, may hold values from 0 to 8191
- encoder_qkv: bfloat16 [768, 2304], P(('seq', 'head')), may hold values from -0.21875 to 0.21875
- encoder_out: bfloat16 [768, 768], P(('seq', 'head')), may hold values from -2.5 to 2.5
- encoder_up: bfloat16 [768, 3072], P(('seq', 'head')), may hold values from -0.21875 to 0.21875
- encoder_down: bfloat16 [3072, 768], P(('seq', 'head')), may hold values from -0.109375 to 0.109375
- encoder_gains: bfloat16 [2, 768], P(None, ('seq', 'head')), may hold values from 0.5 to 1.5
- encoder_biases: bfloat16 [10, 768], P(None, ('seq', 'head')), may hold values from -1.796875 to 1.796875
- decoder_qkv: bfloat16 [768, 2304], P(('seq', 'head')), may hold values from -0.21875 to 0.21875
- decoder_out: bfloat16 [768, 768], P(('seq', 'head')), may hold values from -2.5 to 2.5
- cross_query: bfloat16 [768, 768], P(('seq', 'head')), may hold values from -0.21875 to 0.21875
- cross_keyvalue: bfloat16 [768, 1536], P(('seq', 'head')), may hold values from -0.21875 to 0.21875
- cross_out: bfloat16 [768, 768], P(('seq', 'head')), may hold values from -3.5 to 3.5
- decoder_up: bfloat16 [768, 3072], P(('seq', 'head')), may hold values from -0.21875 to 0.21875
- decoder_down: bfloat16 [3072, 768], P(('seq', 'head')), may hold values from -0.109375 to 0.109375
- decoder_gains: bfloat16 [3, 768], P(None, ('seq', 'head')), may hold values from 0.5 to 1.5
- decoder_biases: bfloat16 [14, 768], P(None, ('seq', 'head')), may hold values from -1.796875 to 1.796875
Outputs:
- decoded: float32 [2, 4096, 768], P(None, ('seq', 'head'))
- grad_source: float32 [2, 8192, 768], P(None, ('seq', 'head'))
- grad_target: float32 [2, 4096, 768], P(None, ('seq', 'head'))
- grad_encoder_qkv: float32 [768, 2304], P(('seq', 'head'))
- grad_encoder_out: float32 [768, 768], P(('seq', 'head'))
- grad_encoder_up: float32 [768, 3072], P(('seq', 'head'))
- grad_encoder_down: float32 [3072, 768], P(('seq', 'head'))
- grad_encoder_gains: float32 [2, 768], P(None, ('seq', 'head'))
- grad_encoder_biases: float32 [10, 768], P(None, ('seq', 'head'))
- grad_decoder_qkv: float32 [768, 2304], P(('seq', 'head'))
- grad_decoder_out: float32 [768, 768], P(('seq', 'head'))
- grad_cross_query: float32 [768, 768], P(('seq', 'head'))
- grad_cross_keyvalue: float32 [768, 1536], P(('seq', 'head'))
- grad_cross_out: float32 [768, 768], P(('seq', 'head'))
- grad_decoder_up: float32 [768, 3072], P(('seq', 'head'))
- grad_decoder_down: float32 [3072, 768], P(('seq', 'head'))
- grad_decoder_gains: float32 [3, 768], P(None, ('seq', 'head'))
- grad_decoder_biases: float32 [14, 768], P(None, ('seq', 'head'))
The draws below stay inside these ranges and needn't reach their ends.
Inputs may be any that keep to these rules, and one draw needn't show every extreme that they name: `src_lengths`: each row lists the lengths of one micro-batch's source documents in order; a row sums to 8192 and its largest entry is exactly 2048. `tgt_lengths`: each row lists the lengths of one micro-batch's target documents in order; a row sums to 4096 and its largest entry is exactly 1024. `retrieved`: positions in the source stream of the same micro-batch; a position may repeat.
All inputs are finite; a program needn't handle non-finite values.
Results may differ from the reference program's by a relative error of at most 0.025.
Values may be sent and summed in bfloat16 or wider, within the bound.
A program may use at most 320 MiB of HBM per device.

```python
import math
import jax
import jax.numpy as jnp
import numpy as np
from jax import lax

D = 768
HEADS = 12
HEAD_DIM = 64
FF = 3072
TGT_ROWS = 128
MICRO = 2
STRETCH = 1024
RETRIEVED = 1024
REACH = 2
SRC_TOTAL = 8192
TGT_TOTAL = 4096
SRC_MOST = 2048
SRC_DOCS = 16
TGT_MOST = 1024
TGT_DOCS = 8
N_HEAD = 4


def plant(values, stream_key, low, largest):
    spot = [jax.random.randint(jax.random.fold_in(stream_key, axis), (), 0, length) for axis, length in enumerate(values.shape)]
    main_axis = values.shape.index(max(values.shape))
    beside = spot[:main_axis] + [(spot[main_axis] + 1) % values.shape[main_axis]] + spot[main_axis + 1:]
    return values.at[tuple(spot)].set(low).at[tuple(beside)].set(largest)


def block_scale(rng, dims, shards, low, largest):
    def one(dim, blocks):
        steps = jax.random.uniform(jax.random.fold_in(jax.random.fold_in(rng, 6), dim), (blocks,), jnp.float32, low / len(shards), largest / len(shards))
        return jnp.repeat(jnp.exp(steps), dims[dim] // blocks).reshape((-1,) + (1,) * (len(dims) - dim - 1))

    level = one(*shards[0])
    for cut in shards[1:]:
        level = level * one(*cut)
    return level


def profile(number_of, total, limit, skew):
    portions = [(1 << 20) // math.isqrt(grade ** skew) + 1 for grade in range(2, number_of + 1)]
    rest, counts = total - limit - (number_of - 1), [1] * (number_of - 1)
    while rest > 0:
        candidates = [i for i in range(number_of - 1) if counts[i] < limit]
        whole, left = sum([portions[i] for i in candidates]), rest
        for i in candidates:
            more = min(limit - counts[i], max(1, left * portions[i] // whole), rest)
            counts[i] = counts[i] + more
            rest = rest - more
    return np.array([limit] + counts)


def ragged(own_key, count, total, bound, lean):
    if count == 2:
        one = jax.random.randint(own_key, (), max(1, total - bound), min(bound, total - 1) + 1)
        return jnp.stack([one, total - one])
    sizes = jnp.asarray(profile(count, total, bound, lean), jnp.int32)
    pairs = (count - 1) // 2
    donor, receiver = sizes[1:1 + 2 * pairs:2], sizes[2:2 + 2 * pairs:2]
    margin = jnp.minimum(donor - 1, bound - receiver)
    shifted = jax.random.randint(jax.random.fold_in(own_key, 1), (pairs,), 0, 1 << 20) % (margin + 1)
    sizes = sizes.at[1:1 + 2 * pairs:2].set(donor - shifted).at[2:2 + 2 * pairs:2].set(receiver + shifted)
    return sizes[jax.random.permutation(jax.random.fold_in(own_key, 2), count)]


def scatter_about(stream_key, extent, deviation, bound, shards=(), kind=jnp.bfloat16):
    level = block_scale(stream_key, extent, shards, -0.22, 0.18) if shards else 1.0
    array = jax.random.normal(stream_key, extent, jnp.float32) * deviation * level
    return jnp.minimum(jnp.maximum(array, -bound), bound).astype(kind)


def setup_inputs(seed: int = 0) -> dict:
    seeds = jax.random.split(jax.random.key(seed), 22)
    return {
        "source": scatter_about(seeds[0], (MICRO, SRC_TOTAL, D), 1.0, 6.0, ((1, 32),)),
        "target": scatter_about(seeds[1], (MICRO, TGT_TOTAL, D), 1.0, 6.0, ((1, 32),)),
        "cotangent": scatter_about(seeds[2], (MICRO, TGT_TOTAL, D), 1.0, 6.0, ((1, 32),)),
        "src_lengths": jax.vmap(lambda own: ragged(own, SRC_DOCS, SRC_TOTAL, SRC_MOST, 2))(jax.random.split(seeds[3], MICRO)).reshape((MICRO, SRC_DOCS)).astype(jnp.int32),
        "tgt_lengths": jax.vmap(lambda own: ragged(own, TGT_DOCS, TGT_TOTAL, TGT_MOST, 1))(jax.random.split(seeds[4], MICRO)).reshape((MICRO, TGT_DOCS)).astype(jnp.int32),
        "retrieved": plant(jax.random.randint(seeds[5], (MICRO, RETRIEVED), 0, SRC_TOTAL), jax.random.fold_in(seeds[5], 1), 0, SRC_TOTAL - 1).astype(jnp.int32),
        "encoder_qkv": scatter_about(seeds[6], (D, 3 * D), D ** -0.5, 0.21875, ((0, 32),)),
        "encoder_out": scatter_about(seeds[7], (D, D), (D // 128) ** -0.5, 2.5, ((0, 32),)),
        "encoder_up": scatter_about(seeds[8], (D, FF), D ** -0.5, 0.21875, ((0, 32),)),
        "encoder_down": scatter_about(seeds[9], (FF, D), FF ** -0.5, 0.109375, ((0, 32),)),
        "encoder_gains": jnp.clip(1.0 + 0.1 * jax.random.normal(seeds[10], (2, D), jnp.float32), 0.5, 1.5).astype(jnp.bfloat16),
        "encoder_biases": scatter_about(seeds[11], (10, D), 0.3, 1.796875, ((1, 32),)),
        "decoder_qkv": scatter_about(seeds[12], (D, 3 * D), D ** -0.5, 0.21875, ((0, 32),)),
        "decoder_out": scatter_about(seeds[13], (D, D), (D // 128) ** -0.5, 2.5, ((0, 32),)),
        "cross_query": scatter_about(seeds[14], (D, D), D ** -0.5, 0.21875, ((0, 32),)),
        "cross_keyvalue": scatter_about(seeds[15], (D, 2 * D), D ** -0.5, 0.21875, ((0, 32),)),
        "cross_out": scatter_about(seeds[16], (D, D), (D // 256) ** -0.5, 3.5, ((0, 32),)),
        "decoder_up": scatter_about(seeds[17], (D, FF), D ** -0.5, 0.21875, ((0, 32),)),
        "decoder_down": scatter_about(seeds[18], (FF, D), FF ** -0.5, 0.109375, ((0, 32),)),
        "decoder_gains": jnp.clip(1.0 + 0.1 * jax.random.normal(seeds[19], (3, D), jnp.float32), 0.5, 1.5).astype(jnp.bfloat16),
        "decoder_biases": scatter_about(seeds[20], (14, D), 0.3, 1.796875, ((1, 32),)),
    }


@jax.custom_vjp
def low(v):
    return lax.optimization_barrier(v.astype(jnp.bfloat16)).astype(jnp.float32)

@jax.custom_vjp
def low_back(v):
    return v

def low_keep(v):
    return (low(v), None)

def low_pass(kept, grad):
    return (grad,)

def back_keep(v):
    return (v, None)

def back_low(kept, grad):
    return (low(grad),)
low.defvjp(low_keep, low_pass)
low_back.defvjp(back_keep, back_low)
EPSILON = 1e-05
NEGATIVE = -1e+30
PRECISE = lax.Precision.HIGHEST

def layer_norm(resid, gain, shift):
    center = resid - lax.optimization_barrier(jnp.mean(resid, axis=-1, keepdims=True))
    spread = lax.optimization_barrier(jnp.mean(center * center, axis=-1, keepdims=True))
    return center * lax.rsqrt(spread + EPSILON) * gain + shift

def gelu_exact(value):
    return jax.nn.gelu(value, approximate=False)

def matmul(left, right):
    return jnp.dot(left, right, precision=PRECISE)

def both_ways(value):
    return low(low_back(value))

def doc_ids(lengths, positions):
    starts = (jnp.cumsum(lengths) - lengths).astype(jnp.int32)
    inside = (starts[None, :] <= positions[:, None]).astype(jnp.int32)
    return (lax.optimization_barrier(jnp.sum(inside, axis=1)) - 1).astype(jnp.int32)

def joined_bias(biases):
    query_part = biases[0].reshape(HEADS, HEAD_DIM)
    value_part = biases[1].reshape(HEADS, HEAD_DIM)
    return jnp.stack([query_part, jnp.zeros_like(query_part), value_part], axis=1).reshape(3 * D)

def softmax_rows(scores):
    peak = lax.optimization_barrier(jnp.max(scores, axis=-1, keepdims=True))
    weights = jnp.exp(scores - peak)
    return weights / lax.optimization_barrier(jnp.sum(weights, axis=-1, keepdims=True))

def attend(query, keys, values, allowed):
    scores = jnp.einsum('qhd,khd->hqk', query, keys, precision=PRECISE) * 0.125
    scores = low_back(jnp.where(allowed[None], scores, NEGATIVE))
    probs = low(softmax_rows(scores))
    return jnp.einsum('hqk,khd->qhd', probs, values, precision=PRECISE)

def encoder(rows_in, params, lengths):
    qkv_weight, out_weight, up_weight, down_weight, gains, biases = params
    total = rows_in.shape[0]
    count = total // STRETCH
    joined = both_ways(matmul(rows_in, qkv_weight) + joined_bias(biases))
    joined = joined.reshape(count, STRETCH, HEADS, 3, HEAD_DIM)
    documents = doc_ids(lengths, jnp.arange(total, dtype=jnp.int32)).reshape(count, STRETCH)

    def one_stretch(items):
        block, docs_here = items
        allowed = docs_here[:, None] == docs_here[None, :]
        return attend(block[:, :, 0], block[:, :, 1], block[:, :, 2], allowed)
    attended = lax.map(jax.checkpoint(one_stretch), (joined, documents))
    attended = both_ways(attended.reshape(total, D))
    branch = low_back(matmul(attended, out_weight) + biases[2])
    first = layer_norm(rows_in + branch, gains[0], biases[3])
    hidden = low_back(matmul(low(first), up_weight) + biases[4:8].reshape(FF))
    active = low(gelu_exact(hidden))
    second = low_back(matmul(active, down_weight) + biases[8])
    return layer_norm(first + second, gains[1], biases[9])

def decoder(rows_in, encoded, chosen, params, lengths):
    qkv_weight, out_weight, query_weight, keyvalue_weight, cross_weight, up_weight, down_weight, gains, biases = params
    total = rows_in.shape[0]
    group = N_HEAD * TGT_ROWS
    window = REACH * group
    count = total // group
    joined = both_ways(matmul(rows_in, qkv_weight) + joined_bias(biases)).reshape(total, HEADS, 3, HEAD_DIM)
    queries = joined[:, :, 0]
    padded = jnp.concatenate([jnp.zeros((window, HEADS, 2, HEAD_DIM), jnp.float32), joined[:, :, 1:]], axis=0)

    def self_block(index):
        first = index * group
        query = lax.dynamic_slice_in_dim(queries, first, group, 0)
        keyset = lax.dynamic_slice_in_dim(padded, first, window + group, 0)
        query_pos = first + jnp.arange(group, dtype=jnp.int32)
        key_pos = first - window + jnp.arange(window + group, dtype=jnp.int32)
        same = doc_ids(lengths, key_pos)[None, :] == doc_ids(lengths, query_pos)[:, None]
        allowed = (key_pos[None, :] <= query_pos[:, None]) & same
        return attend(query, keyset[:, :, 0], keyset[:, :, 1], allowed)
    attended = lax.map(jax.checkpoint(self_block), jnp.arange(count, dtype=jnp.int32))
    attended = both_ways(attended.reshape(total, D))
    branch = low_back(matmul(attended, out_weight) + biases[2])
    first_norm = layer_norm(rows_in + branch, gains[0], biases[3])
    fetched = low(encoded[chosen])
    cross_queries = both_ways(matmul(low(first_norm), query_weight) + biases[4])
    cross_queries = cross_queries.reshape(count, group, HEADS, HEAD_DIM)
    keyvalue = matmul(fetched, keyvalue_weight) + jnp.concatenate([jnp.zeros((D,), jnp.float32), biases[5]])
    cross_keys = low(keyvalue[:, :D]).reshape(RETRIEVED, HEADS, HEAD_DIM)
    cross_values = low(keyvalue[:, D:]).reshape(RETRIEVED, HEADS, HEAD_DIM)
    every = jnp.ones((group, RETRIEVED), jnp.bool_)

    def cross_block(query):
        return attend(query, cross_keys, cross_values, every)
    crossed = lax.map(jax.checkpoint(cross_block), cross_queries)
    crossed = both_ways(crossed.reshape(total, D))
    branch_cross = low_back(matmul(crossed, cross_weight) + biases[6])
    second_norm = layer_norm(first_norm + branch_cross, gains[1], biases[7])
    hidden = low_back(matmul(low(second_norm), up_weight) + biases[8:12].reshape(FF))
    active = low(gelu_exact(hidden))
    third = low_back(matmul(active, down_weight) + biases[12])
    return layer_norm(second_norm + third, gains[2], biases[13])

def reference(source, target, cotangent, src_lengths, tgt_lengths, retrieved, encoder_qkv, encoder_out, encoder_up, encoder_down, encoder_gains, encoder_biases, decoder_qkv, decoder_out, cross_query, cross_keyvalue, cross_out, decoder_up, decoder_down, decoder_gains, decoder_biases):
    encoder_set = tuple((item.astype(jnp.float32) for item in (encoder_qkv, encoder_out, encoder_up, encoder_down, encoder_gains, encoder_biases)))
    decoder_set = tuple((item.astype(jnp.float32) for item in (decoder_qkv, decoder_out, cross_query, cross_keyvalue, cross_out, decoder_up, decoder_down, decoder_gains, decoder_biases)))
    decoded_rows = []
    source_grads = []
    target_grads = []
    grad_totals = None
    for micro in range(MICRO):

        def forward(rows_source, rows_target, encoder_params, decoder_params):
            encoded = encoder(rows_source, encoder_params, src_lengths[micro])
            return decoder(rows_target, encoded, retrieved[micro], decoder_params, tgt_lengths[micro])
        result, pullback = jax.vjp(forward, source[micro].astype(jnp.float32), target[micro].astype(jnp.float32), encoder_set, decoder_set)
        grad_rows_source, grad_rows_target, grad_encoder, grad_decoder = pullback(cotangent[micro].astype(jnp.float32))
        decoded_rows.append(result)
        source_grads.append(grad_rows_source)
        target_grads.append(grad_rows_target)
        here = tuple(grad_encoder) + tuple(grad_decoder)
        if grad_totals is None:
            grad_totals = here
        else:
            grad_totals = tuple((left + right for left, right in zip(grad_totals, here)))
    return (jnp.stack(decoded_rows), jnp.stack(source_grads), jnp.stack(target_grads), grad_totals[0], grad_totals[1], grad_totals[2], grad_totals[3], grad_totals[4], grad_totals[5], grad_totals[6], grad_totals[7], grad_totals[8], grad_totals[9], grad_totals[10], grad_totals[11], grad_totals[12], grad_totals[13], grad_totals[14])
```

```python
import functools

import jax
import jax.numpy as jnp
from jax import lax
from jax.experimental import pallas as pl
from jax.experimental.pallas import tpu as pltpu
from jax.sharding import PartitionSpec as P

D = 768
HEADS = 12
HEAD_DIM = 64
FF = 3072
MICRO = 2
STRETCH = 1024
REACH = 2
EVERY = ("seq", "head")

EPSILON = 1e-05
NEGATIVE = -1e30
MESH = pl.DeviceIdType.MESH
F32 = jnp.float32
BF16 = jnp.bfloat16


def place():
    seq, head = lax.axis_index("seq"), lax.axis_index("head")
    return seq // 2, seq % 2, head // 2, head % 2


def device(z, y, x, c):
    return (z * 2 + y, x * 2 + c)


def shard(z, y, x, c):
    return ((z * 2 + y) * 2 + x) * 2 + c


def greet(z, y, x, c):
    barrier = pltpu.get_barrier_semaphore()
    def tell(who):
        pl.semaphore_signal(barrier, inc=1, device_id=who, device_id_type=MESH)
    tell(device(z, y, x, 1 - c))
    tell(device(z, y, 1 - x, c))
    tell(device(z, 1 - y, x, c))
    @pl.when(z > 0)
    def _():
        tell(device(z - 1, y, x, c))
    @pl.when(z < 3)
    def _():
        tell(device(z + 1, y, x, c))
    pl.semaphore_wait(barrier, 3 + (z + 2) // 3 + (5 - z) // 3)


def gather_kernel(count, firsts, *refs):
    ins, outs = refs[:count], refs[count:2 * count]
    local_sem, recv_sem, send_sem = refs[2 * count:]
    z, y, x, c = place()
    greet(z, y, x, c)

    def spot(first, zo, f, l):
        return shard(zo, l, f, c) if first == "x" else shard(zo, f, l, c)

    def holder(first, zo, f, l, cc):
        return device(zo, l, f, cc) if first == "x" else device(zo, f, l, cc)

    def copy(a, src, where, who, kind, slot):
        return pltpu.make_async_remote_copy(
            src_ref=src, dst_ref=outs[a].at[where],
            send_sem=send_sem.at[a, kind, slot], recv_sem=recv_sem.at[a, where],
            device_id=who, device_id_type=MESH)

    def forward(a, zo, fo, lo, src, right, left, last):
        first = firsts[a]
        f, l = (x, y) if first == "x" else (y, x)
        where = spot(first, zo, fo, lo)
        if right:
            @pl.when((z < 3) if right is True else right & (z < 3))
            def _():
                copy(a, src, where, holder(first, z + 1, f, l, c), 1, where // 2).start()
        if left:
            @pl.when((z > 0))
            def _():
                copy(a, src, where, holder(first, z - 1, f, l, c), 2, where // 2).start()
        if last:
            copy(a, src, where, holder(first, z, f, 1 - l, c), 3, where // 2).start()
        copy(a, src, where, holder(first, z, f, l, 1 - c), 4, where // 2).start()

    def arrived(a, where):
        copy(a, outs[a].at[where], where, device(z, y, x, c), 0, 0).wait_recv()

    def axes(a):
        return (x, y) if firsts[a] == "x" else (y, x)

    locals_ = []
    for a in range(count):
        f, l = axes(a)
        first = firsts[a]
        me = spot(first, z, f, l)
        copy(a, ins[a], me, holder(first, z, 1 - f, l, c), 0, me // 2).start()
        forward(a, z, f, l, ins[a], True, True, True)
        own = pltpu.make_async_copy(ins[a], outs[a].at[me], local_sem.at[a])
        own.start()
        locals_.append(own)

    def last_arrival(zo, fsel):
        for a in range(count):
            f, l = axes(a)
            fo = f if fsel == 0 else 1 - f
            where = spot(firsts[a], zo, fo, 1 - l)
            arrived(a, where)
            forward(a, zo, fo, 1 - l, outs[a].at[where], False, False, False)

    for a in range(count):
        f, l = axes(a)
        where = spot(firsts[a], z, 1 - f, l)
        arrived(a, where)
        forward(a, z, 1 - f, l, outs[a].at[where], True, True, True)
    last_arrival(z, 0)
    last_arrival(z, 1)
    for dist in (1, 2, 3):
        for side in (0, 1):
            zo = z - dist if side == 0 else z + dist
            ok = (zo >= 0) if side == 0 else (zo <= 3)
            @pl.when(ok)
            def _():
                for fsel in (0, 1):
                    for a in range(count):
                        f, l = axes(a)
                        fo = f if fsel == 0 else 1 - f
                        where = spot(firsts[a], zo, fo, l)
                        arrived(a, where)
                        forward(a, zo, fo, l, outs[a].at[where], side == 0, side == 1, True)
        for side in (0, 1):
            zo = z - dist if side == 0 else z + dist
            ok = (zo >= 0) if side == 0 else (zo <= 3)
            @pl.when(ok)
            def _():
                last_arrival(zo, 0)
                last_arrival(zo, 1)
    def other(i, carry):
        for a in range(count):
            where = i * 2 + 1 - c
            pltpu.make_async_remote_copy(src_ref=outs[a].at[where], dst_ref=outs[a].at[where],
                send_sem=send_sem.at[a, 4, i], recv_sem=recv_sem.at[a, where],
                device_id=device(z, y, x, 1 - c), device_id_type=MESH).wait_recv()
        return carry
    lax.fori_loop(0, 16, other, 0)
    for a in range(count):
        locals_[a].wait()
        f, l = axes(a)
        first = firsts[a]
        def sent(where, kind):
            pltpu.make_async_remote_copy(src_ref=ins[a], dst_ref=outs[a].at[where],
                send_sem=send_sem.at[a, kind, where // 2], recv_sem=recv_sem.at[a, where],
                device_id=device(z, y, x, 1 - c), device_id_type=MESH).wait_send()
        sent(spot(first, z, f, l), 0)
        for zo in range(4):
            for fo in range(2):
                where = spot(first, zo, fo, l)
                sent(where, 3)
                @pl.when((zo <= z) & (z < 3))
                def _():
                    sent(where, 1)
                @pl.when((zo >= z) & (z > 0))
                def _():
                    sent(where, 2)
        def sent_core(i, carry):
            sent(i * 2 + c, 4)
            return carry
        lax.fori_loop(0, 16, sent_core, 0)


def gather_all(arrays, firsts, collective_id):
    count = len(arrays)
    return pl.pallas_call(
        functools.partial(gather_kernel, count, tuple(firsts)),
        out_shape=[jax.ShapeDtypeStruct((32,) + v.shape, v.dtype) for v in arrays],
        in_specs=[pl.BlockSpec(memory_space=pl.ANY)] * count,
        out_specs=[pl.BlockSpec(memory_space=pl.ANY)] * count,
        scratch_shapes=[pltpu.SemaphoreType.DMA((count,)), pltpu.SemaphoreType.DMA((count, 32)),
                        pltpu.SemaphoreType.DMA((count, 5, 16))],
        compiler_params=pltpu.CompilerParams(collective_id=collective_id, has_side_effects=True),
    )(*arrays)


def scatter_kernel(count, firsts, *refs):
    grads, outs = refs[:count], refs[count:2 * count]
    held, mine, near, right, left, last = [refs[(2 + k) * count:(3 + k) * count] for k in range(6)]
    mine_sem, core_sem, near_sem, right_sem, left_sem, last_sem = refs[8 * count:]
    z, y, x, c = place()
    greet(z, y, x, c)
    half = z // 2

    def axes(a):
        return (x, y) if firsts[a] == "x" else (y, x)

    def block(a, zt, f, l):
        return (zt * 2 + l) * 2 + f if firsts[a] == "x" else (zt * 2 + f) * 2 + l

    def remote(a, src, dst, sems, slot, who):
        return pltpu.make_async_remote_copy(
            src_ref=src, dst_ref=dst, send_sem=sems.at[a, 0, slot], recv_sem=sems.at[a, 1, slot],
            device_id=who, device_id_type=MESH)

    def core_copy(a, q):
        return remote(a, grads[a].at[q * 2 + 1 - c], held[a].at[q], core_sem, q, device(z, y, x, 1 - c))

    def mine_copy(a, q):
        return pltpu.make_async_copy(grads[a].at[q * 2 + c], mine[a].at[q], mine_sem.at[a, q])

    def near_copy(a, q, slot):
        who = device(z, y, 1 - x, c) if firsts[a] == "x" else device(z, 1 - y, x, c)
        return remote(a, held[a].at[q], near[a].at[slot], near_sem, slot, who)

    def right_copy(a, q, slot):
        return remote(a, held[a].at[q], right[a].at[slot], right_sem, slot, device(z + 1, y, x, c))

    def left_copy(a, q, slot):
        return remote(a, held[a].at[q], left[a].at[slot], left_sem, slot, device(z - 1, y, x, c))

    def last_copy(a, q):
        who = device(z, 1 - y, x, c) if firsts[a] == "x" else device(z, y, 1 - x, c)
        return remote(a, held[a].at[q], last[a].at[0], last_sem, 0, who)

    def far(k):
        return 3 - k + half * (2 * k - 3)

    def others(k):
        down = 3 - k - (k // 2) * z
        up = k + (k // 2) * (3 - z)
        return down + half * (up - down)

    def wide(ref, q):
        return ref[q].astype(jnp.float32)

    for side in (1, 0):
        def start(i, carry, side=side):
            for a in range(count):
                f, l = axes(a)
                q = block(a, far(i // 2), (1 - f) if side else f, i % 2)
                core_copy(a, q).start()
                mine_copy(a, q).start()
            return carry
        lax.fori_loop(0, 8, start, 0)

    def first_phase(i, carry):
        zt, lt = far(i // 2), i % 2
        for a in range(count):
            f, l = axes(a)
            q = block(a, zt, 1 - f, lt)
            core_copy(a, q).wait_recv()
            mine_copy(a, q).wait()
            held[a][q] = (wide(held[a], q) + wide(mine[a], q)).astype(jnp.bfloat16)
            near_copy(a, q, zt * 2 + lt).start()
        return carry
    lax.fori_loop(0, 8, first_phase, 0)

    def gathered(a, zt, lt):
        f, l = axes(a)
        q = block(a, zt, f, lt)
        core_copy(a, q).wait_recv()
        mine_copy(a, q).wait()
        near_copy(a, q, zt * 2 + lt).wait_recv()
        held[a][q] = (wide(held[a], q) + wide(mine[a], q) + wide(near[a], zt * 2 + lt)).astype(jnp.bfloat16)
        return q

    def z_phase(i, carry):
        zt, lt = others(i // 2), i % 2
        for a in range(count):
            q = gathered(a, zt, lt)
            @pl.when(zt > z)
            def _():
                slot = (zt - 1) * 2 + lt
                @pl.when(z > 0)
                def _():
                    right_copy(a, q, slot).wait_recv()
                    held[a][q] = (wide(held[a], q) + wide(right[a], slot)).astype(jnp.bfloat16)
                right_copy(a, q, slot).start()
            @pl.when(zt < z)
            def _():
                slot = zt * 2 + lt
                @pl.when(z < 3)
                def _():
                    left_copy(a, q, slot).wait_recv()
                    held[a][q] = (wide(held[a], q) + wide(left[a], slot)).astype(jnp.bfloat16)
                left_copy(a, q, slot).start()
        return carry
    lax.fori_loop(0, 6, z_phase, 0)

    for side in (1, 0):
        for a in range(count):
            f, l = axes(a)
            lt = (1 - l) if side else l
            q = gathered(a, z, lt)
            @pl.when(z > 0)
            def _():
                slot = (z - 1) * 2 + lt
                right_copy(a, q, slot).wait_recv()
                held[a][q] = (wide(held[a], q) + wide(right[a], slot)).astype(jnp.bfloat16)
            @pl.when(z < 3)
            def _():
                slot = z * 2 + lt
                left_copy(a, q, slot).wait_recv()
                held[a][q] = (wide(held[a], q) + wide(left[a], slot)).astype(jnp.bfloat16)
            if side:
                last_copy(a, q).start()
    for a in range(count):
        f, l = axes(a)
        q = block(a, z, f, l)
        last_copy(a, q).wait_recv()
        outs[a][...] = (wide(held[a], q) + wide(last[a], 0)).astype(outs[a].dtype)
    def sent(i, carry):
        for a in range(count):
            f, l = axes(a)
            core_copy(a, i).wait_send()
        return carry
    lax.fori_loop(0, 16, sent, 0)
    def sent_near(i, carry):
        for a in range(count):
            f, l = axes(a)
            near_copy(a, block(a, i // 2, 1 - f, i % 2), i).wait_send()
        return carry
    lax.fori_loop(0, 8, sent_near, 0)
    def sent_z(i, carry):
        zt, lt = others(i // 2), i % 2
        for a in range(count):
            f, l = axes(a)
            q = block(a, zt, f, lt)
            @pl.when(zt > z)
            def _():
                right_copy(a, q, (zt - 1) * 2 + lt).wait_send()
            @pl.when(zt < z)
            def _():
                left_copy(a, q, zt * 2 + lt).wait_send()
        return carry
    lax.fori_loop(0, 6, sent_z, 0)
    for a in range(count):
        f, l = axes(a)
        last_copy(a, block(a, z, f, 1 - l)).wait_send()


def scatter_sum(arrays, firsts, collective_id, out_dtype=jnp.float32):
    count = len(arrays)
    shapes = [v.shape[1:] for v in arrays]
    scratch = []
    for slots in (16, 16, 8, 6, 6, 1):
        scratch += [pltpu.VMEM((slots,) + s, jnp.bfloat16) for s in shapes]
    D = pltpu.SemaphoreType.DMA
    return pl.pallas_call(
        functools.partial(scatter_kernel, count, tuple(firsts)),
        out_shape=[jax.ShapeDtypeStruct(s, out_dtype) for s in shapes],
        in_specs=[pl.BlockSpec(memory_space=pl.ANY)] * count,
        out_specs=[pl.BlockSpec(memory_space=pltpu.VMEM)] * count,
        scratch_shapes=scratch + [D((count, 16)), D((count, 2, 16)), D((count, 2, 8)), D((count, 2, 6)), D((count, 2, 6)), D((count, 2, 1))],
        compiler_params=pltpu.CompilerParams(collective_id=collective_id, has_side_effects=True, vmem_limit_bytes=60 << 20),
    )(*arrays)


def known_mesh():
    return lax.axis_size("seq") == 8 and lax.axis_size("head") == 4


def gather(arrays, firsts, collective_id):
    if known_mesh():
        return gather_all(arrays, firsts, collective_id)
    return [lax.all_gather(v, EVERY, axis=0, tiled=False) for v in arrays]


def scatter(arrays, firsts, collective_id, out_dtype=F32):
    if known_mesh():
        return scatter_sum(arrays, firsts, collective_id, out_dtype)
    return [
        lax.psum_scatter(v, EVERY, scatter_dimension=0, tiled=False).astype(out_dtype)
        for v in arrays
    ]


def fill(target, refs, columns):
    at = 0
    for ref in refs:
        rows = ref.shape[2]
        for p in range(ref.shape[0]):
            target[at : at + rows] = ref[p, 0, :, columns]
            at += rows


def spill(value, refs, columns):
    at = 0
    for ref in refs:
        rows = ref.shape[2]
        for p in range(ref.shape[0]):
            ref[p, 0, :, columns] = value[at : at + rows].astype(ref.dtype)
            at += rows


def scores_of(keys, query, allowed):
    scores = lax.dot_general(keys, query, (((1,), (1,)), ((), ())), preferred_element_type=F32)
    return jnp.where(allowed, scores * 0.125, NEGATIVE)


def soft_columns(scores):
    weights = jnp.exp(scores - jnp.max(scores, axis=0, keepdims=True))
    return weights * (1.0 / jnp.sum(weights, axis=0, keepdims=True))


def allowed_pairs(key_ref, query_ref, start, tile, causal):
    doc_key, doc_query = key_ref[0, :, 0:1], query_ref[0, 0:1, pl.ds(start, tile)]
    allowed = doc_key == doc_query
    if causal:
        allowed &= key_ref[0, :, 1:2] <= query_ref[0, 1:2, pl.ds(start, tile)]
    return allowed


def attend_kernel(heads, tile, causal, *refs):
    key_ref, query_ref, own_ref = refs[:3]
    prior = refs[3:-5]
    out_ref, key_s, value_s, query_s, result_s = refs[-5:]
    group = query_s.shape[0]
    for h in range(heads):
        fill(key_s, (*prior, own_ref), slice(h * 128, h * 128 + 64))
        fill(value_s, (*prior, own_ref), slice(h * 128 + 64, h * 128 + 128))
        at = heads * 128 + h * 64
        fill(query_s, (own_ref,), slice(at, at + 64))

        def step(i, carry):
            start = pl.multiple_of(i * tile, tile)
            allowed = allowed_pairs(key_ref, query_ref, start, tile, causal)
            probs = soft_columns(scores_of(key_s[...], query_s[pl.ds(start, tile), :], allowed))
            out = lax.dot_general(
                probs.astype(BF16), value_s[...], (((0,), (0,)), ((), ())), preferred_element_type=F32
            )
            result_s[pl.ds(start, tile), :] = out.astype(BF16)
            return carry

        lax.fori_loop(0, group // tile, step, 0)
        spill(result_s[...], (out_ref,), slice(h * 64, h * 64 + 64))


def rows_spec(shape):
    return pl.BlockSpec((shape[0], 1) + shape[2:], lambda m: (0, m, 0, 0))


def whole_spec(shape):
    return pl.BlockSpec((1,) + shape[1:], lambda m: (m, 0, 0))


def attend(joined, prior, key_info, query_info, causal, tile=256):
    parts, micro, rows, columns = joined.shape
    heads, group = columns // 192, parts * rows
    keys = key_info.shape[1]
    out = (parts, micro, rows, heads * 64)
    return pl.pallas_call(
        functools.partial(attend_kernel, heads, tile, causal),
        grid=(micro,),
        out_shape=jax.ShapeDtypeStruct(out, BF16),
        in_specs=[whole_spec(key_info.shape), whole_spec(query_info.shape), rows_spec(joined.shape)]
        + [rows_spec(p.shape) for p in prior],
        out_specs=rows_spec(out),
        scratch_shapes=[
            pltpu.VMEM((keys, 64), BF16),
            pltpu.VMEM((keys, 64), BF16),
            pltpu.VMEM((group, 64), BF16),
            pltpu.VMEM((group, 64), BF16),
        ],
        compiler_params=pltpu.CompilerParams(vmem_limit_bytes=48 << 20),
        cost_estimate=pl.CostEstimate(
            flops=4 * micro * heads * group * keys * 128,
            transcendentals=micro * heads * group * keys,
            bytes_accessed=joined.size * 4,
        ),
        name="attend",
    )(key_info, query_info, joined, *prior)


def attend_back_kernel(heads, tile, causal, count, *refs):
    key_ref, query_ref, own_ref, grad_ref = refs[:4]
    prior = refs[4 : 4 + count]
    out_ref, *prior_out = refs[4 + count : 5 + 2 * count]
    key_s, value_s, query_s, grad_s, gk_s, gv_s, result_s = refs[5 + 2 * count :]
    group = query_s.shape[0]
    for h in range(heads):
        key_cut, value_cut = slice(h * 128, h * 128 + 64), slice(h * 128 + 64, h * 128 + 128)
        fill(key_s, (*prior, own_ref), key_cut)
        fill(value_s, (*prior, own_ref), value_cut)
        query_cut = slice(heads * 128 + h * 64, heads * 128 + h * 64 + 64)
        fill(query_s, (own_ref,), query_cut)
        fill(grad_s, (grad_ref,), slice(h * 64, h * 64 + 64))
        gk_s[...] = jnp.zeros_like(gk_s)
        gv_s[...] = jnp.zeros_like(gv_s)

        def step(i, carry):
            start = pl.multiple_of(i * tile, tile)
            here = pl.ds(start, tile)
            allowed = allowed_pairs(key_ref, query_ref, start, tile, causal)
            query, grad_out = query_s[here, :], grad_s[here, :]
            probs = soft_columns(scores_of(key_s[...], query, allowed))
            grad_probs = lax.dot_general(
                value_s[...], grad_out, (((1,), (1,)), ((), ())), preferred_element_type=F32
            )
            delta = jnp.sum(probs * grad_probs, axis=0, keepdims=True)
            grad_scores = (probs * (grad_probs - delta)).astype(BF16)
            gv_s[...] += jnp.dot(probs.astype(BF16), grad_out, preferred_element_type=F32)
            gk_s[...] += jnp.dot(grad_scores, query, preferred_element_type=F32)
            grad_query = lax.dot_general(
                grad_scores, key_s[...], (((0,), (0,)), ((), ())), preferred_element_type=F32
            )
            result_s[here, :] = grad_query * 0.125
            return carry

        lax.fori_loop(0, group // tile, step, 0)
        spill(result_s[...], (out_ref,), query_cut)
        spill(gk_s[...] * 0.125, (*prior_out, out_ref), key_cut)
        spill(gv_s[...], (*prior_out, out_ref), value_cut)


def attend_back(joined, prior, key_info, query_info, grad, causal, out_dtype, tile=256):
    parts, micro, rows, columns = joined.shape
    heads, group = columns // 192, parts * rows
    keys = key_info.shape[1]
    return pl.pallas_call(
        functools.partial(attend_back_kernel, heads, tile, causal, len(prior)),
        grid=(micro,),
        out_shape=[jax.ShapeDtypeStruct(joined.shape, out_dtype)]
        + [jax.ShapeDtypeStruct(p.shape, BF16) for p in prior],
        in_specs=[
            whole_spec(key_info.shape),
            whole_spec(query_info.shape),
            rows_spec(joined.shape),
            rows_spec(grad.shape),
        ]
        + [rows_spec(p.shape) for p in prior],
        out_specs=[rows_spec(joined.shape)] + [rows_spec(p.shape) for p in prior],
        scratch_shapes=[
            pltpu.VMEM((keys, 64), BF16),
            pltpu.VMEM((keys, 64), BF16),
            pltpu.VMEM((group, 64), BF16),
            pltpu.VMEM((group, 64), BF16),
            pltpu.VMEM((keys, 64), F32),
            pltpu.VMEM((keys, 64), F32),
            pltpu.VMEM((group, 64), F32),
        ],
        compiler_params=pltpu.CompilerParams(vmem_limit_bytes=48 << 20),
        cost_estimate=pl.CostEstimate(
            flops=10 * micro * heads * group * keys * 128,
            transcendentals=micro * heads * group * keys,
            bytes_accessed=joined.size * 6,
        ),
        name="attend_back",
    )(key_info, query_info, joined, grad, *prior)


def cross_kernel(query_ref, pairs_ref, out_ref):
    for i in range(D // 128):
        outs = []
        for h in range(2):
            at = i * 128 + h * 64
            query, keys = query_ref[0, :, at : at + 64], pairs_ref[0, :, at : at + 64]
            values = pairs_ref[0, :, D + at : D + at + 64]
            scores = lax.dot_general(keys, query, (((1,), (1,)), ((), ())), preferred_element_type=F32)
            probs = soft_columns(scores * 0.125)
            outs.append(
                lax.dot_general(
                    probs.astype(BF16), values, (((0,), (0,)), ((), ())), preferred_element_type=F32
                )
            )
        out_ref[0, :, i * 128 : i * 128 + 128] = jnp.concatenate(outs, axis=1).astype(BF16)


def cross(query, pairs):
    micro, rows, _ = query.shape
    keys = pairs.shape[1]
    return pl.pallas_call(
        cross_kernel,
        grid=(micro,),
        out_shape=jax.ShapeDtypeStruct(query.shape, BF16),
        in_specs=[whole_spec(query.shape), whole_spec(pairs.shape)],
        out_specs=whole_spec(query.shape),
        compiler_params=pltpu.CompilerParams(vmem_limit_bytes=48 << 20),
        cost_estimate=pl.CostEstimate(
            flops=4 * micro * HEADS * rows * keys * 128,
            transcendentals=micro * HEADS * rows * keys,
            bytes_accessed=pairs.size * 2,
        ),
        name="cross",
    )(query, pairs)


def cross_back_kernel(query_ref, pairs_ref, grad_ref, grad_query_ref, grad_pairs_ref):
    for i in range(D // 128):
        query_parts, key_parts, value_parts = [], [], []
        for h in range(2):
            at = i * 128 + h * 64
            query, keys = query_ref[0, :, at : at + 64], pairs_ref[0, :, at : at + 64]
            values, grad_out = pairs_ref[0, :, D + at : D + at + 64], grad_ref[0, :, at : at + 64]
            scores = lax.dot_general(keys, query, (((1,), (1,)), ((), ())), preferred_element_type=F32)
            probs = soft_columns(scores * 0.125)
            grad_probs = lax.dot_general(
                values, grad_out, (((1,), (1,)), ((), ())), preferred_element_type=F32
            )
            delta = jnp.sum(probs * grad_probs, axis=0, keepdims=True)
            grad_scores = (probs * (grad_probs - delta)).astype(BF16)
            value_parts.append(jnp.dot(probs.astype(BF16), grad_out, preferred_element_type=F32))
            key_parts.append(jnp.dot(grad_scores, query, preferred_element_type=F32) * 0.125)
            query_parts.append(
                lax.dot_general(
                    grad_scores, keys, (((0,), (0,)), ((), ())), preferred_element_type=F32
                )
                * 0.125
            )
        cut = slice(i * 128, i * 128 + 128)
        grad_query_ref[0, :, cut] = jnp.concatenate(query_parts, axis=1).astype(BF16)
        grad_pairs_ref[0, :, cut] = jnp.concatenate(key_parts, axis=1).astype(BF16)
        cut = slice(D + i * 128, D + i * 128 + 128)
        grad_pairs_ref[0, :, cut] = jnp.concatenate(value_parts, axis=1).astype(BF16)


def cross_back(query, pairs, grad):
    micro, rows, _ = query.shape
    keys = pairs.shape[1]
    return pl.pallas_call(
        cross_back_kernel,
        grid=(micro,),
        out_shape=[jax.ShapeDtypeStruct(query.shape, BF16), jax.ShapeDtypeStruct(pairs.shape, BF16)],
        in_specs=[whole_spec(query.shape), whole_spec(pairs.shape), whole_spec(grad.shape)],
        out_specs=[whole_spec(query.shape), whole_spec(pairs.shape)],
        compiler_params=pltpu.CompilerParams(vmem_limit_bytes=48 << 20),
        cost_estimate=pl.CostEstimate(
            flops=10 * micro * HEADS * rows * keys * 128,
            transcendentals=micro * HEADS * rows * keys,
            bytes_accessed=pairs.size * 4,
        ),
        name="cross_back",
    )(query, pairs, grad)


def norm(resid, gain, shift):
    center = resid - jnp.mean(resid, axis=-1, keepdims=True)
    scale = lax.rsqrt(jnp.mean(center * center, axis=-1, keepdims=True) + EPSILON)
    hat = center * scale
    return hat * gain + shift, (hat, scale)


def norm_back(grad, kept, gain):
    hat, scale = kept
    inner = grad * gain
    grad_resid = scale * (
        inner
        - jnp.mean(inner, axis=-1, keepdims=True)
        - hat * jnp.mean(inner * hat, axis=-1, keepdims=True)
    )
    return grad_resid, jnp.sum(grad * hat, axis=0), jnp.sum(grad, axis=0)


def gelu(value):
    return value * (1.0 + lax.erf(value * 0.7071067811865476)) * 0.5


def gelu_slope(value):
    bell = jnp.exp(value * value * -0.5) * 0.3989422804014327
    return 0.5 * (1.0 + lax.erf(value * 0.7071067811865476)) + value * bell


def mm(left, right):
    return jnp.dot(left, right, preferred_element_type=F32)


def mm_rows(left, right):
    return lax.dot_general(left, right, (((0,), (0,)), ((), ())), preferred_element_type=F32)


def mm_back(left, right):
    return lax.dot_general(left, right, (((1,), (1,)), ((), ())), preferred_element_type=F32)


def row_sum(value):
    return jnp.sum(value.astype(F32), axis=0)


def doc_starts(lengths):
    count = lengths.shape[1]
    before = jnp.arange(count)[None, :] < jnp.arange(count)[:, None]
    return jnp.sum(jnp.where(before[None], lengths[:, None, :], 0), axis=2)


def doc_ids(starts, positions):
    return jnp.sum((starts[:, None, :] <= positions[None, :, None]).astype(jnp.int32), axis=2) - 1


def key_and_query_info(starts, key_pos, query_pos):
    key_docs, query_docs = doc_ids(starts, key_pos), doc_ids(starts, query_pos)
    micro = starts.shape[0]
    key_info = jnp.stack(
        [key_docs, jnp.broadcast_to(key_pos, (micro,) + key_pos.shape)], axis=2
    )
    query_info = jnp.stack(
        [query_docs, jnp.broadcast_to(query_pos, (micro,) + query_pos.shape)], axis=1
    )
    return key_info, query_info


def head_columns(full, parts):
    rows = full.shape[0]
    width = full.shape[1] // parts
    mine = lax.dynamic_slice_in_dim(full, lax.axis_index("head") * width, width, 1)
    mine = mine.reshape(rows, width // 192, 3, HEAD_DIM)
    return jnp.concatenate(
        [mine[:, :, 1:].reshape(rows, -1), mine[:, :, 0].reshape(rows, -1)], axis=1
    )


def head_columns_back(grad, parts):
    rows, width = grad.shape
    heads = width // 192
    pairs = grad[:, : heads * 128].reshape(rows, heads, 2, HEAD_DIM)
    query = grad[:, heads * 128 :].reshape(rows, heads, 1, HEAD_DIM)
    mine = jnp.concatenate([query, pairs], axis=2).reshape(rows, width)
    full = jnp.zeros((rows, width * parts), grad.dtype)
    return lax.dynamic_update_slice_in_dim(full, mine, lax.axis_index("head") * width, 1)


def joined_bias(biases):
    query_part = biases[0].reshape(HEADS, HEAD_DIM)
    value_part = biases[1].reshape(HEADS, HEAD_DIM)
    return jnp.stack([query_part, jnp.zeros_like(query_part), value_part], axis=1).reshape(1, 3 * D)


def to_tokens(value):
    parts, micro, rows, columns = value.shape
    got = lax.all_to_all(value, "head", split_axis=0, concat_axis=0, tiled=True)
    return got.transpose(1, 2, 0, 3).reshape(micro * rows, parts * columns)


def to_heads(value, parts, micro):
    rows = value.shape[0] // micro
    split = value.reshape(micro, rows, parts, -1).transpose(2, 0, 1, 3)
    return lax.all_to_all(split, "head", split_axis=0, concat_axis=0, tiled=True)


def from_before(value, by):
    count = lax.axis_size("seq")
    return lax.ppermute(value, "seq", [(i, i + by) for i in range(count - by)])


def to_before(value, by):
    count = lax.axis_size("seq")
    return lax.ppermute(value, "seq", [(i + by, i) for i in range(count - by)])


def pack_rows(value, width):
    padded = jnp.pad(value, ((0, 0), (0, 8 * width - value.shape[1])))
    return padded.reshape(value.shape[0], 8, width)


def shards(
    source,
    target,
    cotangent,
    src_lengths,
    tgt_lengths,
    retrieved,
    encoder_qkv,
    encoder_out,
    encoder_up,
    encoder_down,
    encoder_gains,
    encoder_biases,
    decoder_qkv,
    decoder_out,
    cross_query,
    cross_keyvalue,
    cross_out,
    decoder_up,
    decoder_down,
    decoder_gains,
    decoder_biases,
):
    micro, src_rows, _ = source.shape
    tgt_rows = target.shape[1]
    parts = lax.axis_size("head")
    devices = parts * lax.axis_size("seq")
    seq, me = lax.axis_index("seq"), lax.axis_index(EVERY)
    src_group, tgt_group = src_rows * parts, tgt_rows * parts
    asked = retrieved.shape[1]
    source_rows = source.reshape(micro * src_rows, D)
    target_rows = target.reshape(micro * tgt_rows, D)

    source_all = lax.all_gather(source, "head", axis=0, tiled=False)
    target_all = lax.all_gather(target, "head", axis=0, tiled=False)

    small = jnp.concatenate([encoder_gains, encoder_biases, decoder_gains, decoder_biases], axis=0)
    small_rows, small_width = small.shape
    small_pack = pack_rows(small.reshape(1, small_rows * small_width), D)[0]
    encoder_full = gather(
        [encoder_qkv, encoder_out, encoder_up, encoder_down, small_pack], "xyyxx", 0
    )
    decoder_full = gather(
        [decoder_qkv, decoder_out, cross_query, cross_keyvalue, cross_out, decoder_up, decoder_down],
        "xyyxyyx",
        1,
    )
    e_qkv, e_out, e_up, e_down = [v.reshape(-1, v.shape[-1]) for v in encoder_full[:4]]
    d_qkv, d_out, c_query, c_pairs, c_out, d_up, d_down = [
        v.reshape(-1, v.shape[-1]) for v in decoder_full
    ]
    small_full = encoder_full[4].reshape(devices, -1)[:, : small_rows * small_width]
    small_full = (
        small_full.reshape(devices, small_rows, small_width).transpose(1, 0, 2).reshape(small_rows, D)
    ).astype(F32)
    e_gains, e_bias = small_full[0:2], small_full[2:12]
    d_gains, d_bias = small_full[12:15], small_full[15:29]

    src_pos = seq * src_group + jnp.arange(src_group, dtype=jnp.int32)
    src_info = key_and_query_info(doc_starts(src_lengths), src_pos, src_pos)
    tgt_pos = seq * tgt_group + jnp.arange(tgt_group, dtype=jnp.int32)
    tgt_key_pos = (seq - REACH) * tgt_group + jnp.arange((REACH + 1) * tgt_group, dtype=jnp.int32)
    tgt_info = key_and_query_info(doc_starts(tgt_lengths), tgt_key_pos, tgt_pos)

    e_qkv_here = head_columns(e_qkv, parts)
    e_joined = (
        mm(source_all.reshape(-1, D), e_qkv_here) + head_columns(joined_bias(e_bias), parts)
    ).astype(BF16)
    e_joined = e_joined.reshape(parts, micro, src_rows, -1)
    e_mixed = to_tokens(attend(e_joined, [], *src_info, False))
    e_first, e_kept_one = norm(
        source_rows.astype(F32) + mm(e_mixed, e_out) + e_bias[2], e_gains[0], e_bias[3]
    )
    e_first_low = e_first.astype(BF16)
    e_hidden = mm(e_first_low, e_up) + e_bias[4:8].reshape(FF)
    e_active = gelu(e_hidden).astype(BF16)
    e_result, e_kept_two = norm(
        e_first + mm(e_active, e_down) + e_bias[8], e_gains[1], e_bias[9]
    )

    d_qkv_here = head_columns(d_qkv, parts)
    d_joined = (
        mm(target_all.reshape(-1, D), d_qkv_here) + head_columns(joined_bias(d_bias), parts)
    ).astype(BF16)
    d_joined = d_joined.reshape(parts, micro, tgt_rows, -1)
    d_pairs = d_joined[..., : d_joined.shape[-1] // 3 * 2]
    d_prior = [from_before(d_pairs, by) for by in range(REACH, 0, -1)]
    d_mixed = to_tokens(attend(d_joined, d_prior, *tgt_info, True))
    d_first, d_kept_one = norm(
        target_rows.astype(F32) + mm(d_mixed, d_out) + d_bias[2], d_gains[0], d_bias[3]
    )
    d_first_low = d_first.astype(BF16)
    queries = (mm(d_first_low, c_query) + d_bias[4]).astype(BF16).reshape(micro, tgt_rows, D)

    src_own = me * src_rows + jnp.arange(src_rows, dtype=jnp.int32)
    select = (retrieved[:, :, None] == src_own[None, None, :]).astype(BF16)
    picked = jnp.einsum(
        "mrs,msd->mrd",
        select,
        e_result.astype(BF16).reshape(micro, src_rows, D),
        preferred_element_type=F32,
    ).astype(BF16)
    picked = [picked[m].reshape(devices, asked // devices, D) for m in range(micro)]
    fetched = gather(scatter(picked, "xy", 2, BF16), "xy", 3)
    fetched = jnp.concatenate([v.reshape(asked, D) for v in fetched], axis=0)
    pair_bias = jnp.concatenate([jnp.zeros((D,), F32), d_bias[5]])
    pairs = (mm(fetched, c_pairs) + pair_bias).astype(BF16).reshape(micro, asked, 2 * D)

    crossed = cross(queries, pairs).reshape(micro * tgt_rows, D)
    d_second, d_kept_two = norm(
        d_first + mm(crossed, c_out) + d_bias[6], d_gains[1], d_bias[7]
    )
    d_second_low = d_second.astype(BF16)
    d_hidden = mm(d_second_low, d_up) + d_bias[8:12].reshape(FF)
    d_active = gelu(d_hidden).astype(BF16)
    decoded, d_kept_three = norm(
        d_second + mm(d_active, d_down) + d_bias[12], d_gains[2], d_bias[13]
    )

    grad = cotangent.reshape(micro * tgt_rows, D).astype(F32)
    g_sum, d_gain_three, d_shift_three = norm_back(grad, d_kept_three, d_gains[2])
    g_third = g_sum.astype(BF16)
    w_d_down = mm_rows(d_active, g_third)
    g_hidden = (mm_back(g_third, d_down) * gelu_slope(d_hidden)).astype(BF16)
    w_d_up = mm_rows(d_second_low, g_hidden)
    g_second = g_sum + mm_back(g_hidden, d_up)
    g_sum_two, d_gain_two, d_shift_two = norm_back(g_second, d_kept_two, d_gains[1])
    g_branch_cross = g_sum_two.astype(BF16)
    w_c_out = mm_rows(crossed, g_branch_cross)
    g_crossed = mm_back(g_branch_cross, c_out).astype(BF16).reshape(micro, tgt_rows, D)
    g_queries, g_pairs = cross_back(queries, pairs, g_crossed)
    g_queries = g_queries.reshape(micro * tgt_rows, D)
    g_pairs = g_pairs.reshape(micro * asked, 2 * D)
    g_fetched = mm_back(g_pairs, c_pairs).astype(BF16).reshape(micro, asked, D)
    g_fetched = [g_fetched[m].reshape(devices, asked // devices, D) for m in range(micro)]
    g_fetched = gather(scatter(g_fetched, "xy", 4, BF16), "xy", 5)
    w_c_pairs = mm_rows(fetched, g_pairs)
    w_c_query = mm_rows(d_first_low, g_queries)
    g_first = g_sum_two + mm_back(g_queries, c_query)
    g_resid, d_gain_one, d_shift_one = norm_back(g_first, d_kept_one, d_gains[0])
    g_branch = g_resid.astype(BF16)
    w_d_out = mm_rows(d_mixed, g_branch)
    g_mixed = mm_back(g_branch, d_out).astype(BF16)
    g_attended = to_heads(g_mixed, parts, micro)
    g_own, *g_prior = attend_back(d_joined, d_prior, *tgt_info, g_attended, True, F32)
    width = d_pairs.shape[-1]
    g_back = sum(to_before(g, by).astype(F32) for g, by in zip(g_prior, range(REACH, 0, -1)))
    g_joined = jnp.concatenate(
        [(g_own[..., :width] + g_back).astype(BF16), g_own[..., width:].astype(BF16)], axis=-1
    ).reshape(parts * micro * tgt_rows, -1)
    w_d_qkv = mm_rows(target_all.reshape(-1, D), g_joined)
    g_target_all = mm_back(g_joined, d_qkv_here).astype(BF16)
    g_target = g_resid + lax.psum_scatter(
        g_target_all.reshape(parts, micro * tgt_rows, D), "head", scatter_dimension=0, tiled=False
    ).astype(F32)
    d_joined_sums = head_columns_back(row_sum(g_joined)[None], parts).reshape(HEADS, 3, HEAD_DIM)

    g_result = jnp.einsum(
        "mrs,mrd->msd",
        select,
        jnp.stack([v.reshape(asked, D) for v in g_fetched]),
        preferred_element_type=F32,
    ).reshape(micro * src_rows, D)
    g_sum, e_gain_two, e_shift_two = norm_back(g_result, e_kept_two, e_gains[1])
    g_second_low = g_sum.astype(BF16)
    w_e_down = mm_rows(e_active, g_second_low)
    ge_hidden = (mm_back(g_second_low, e_down) * gelu_slope(e_hidden)).astype(BF16)
    w_e_up = mm_rows(e_first_low, ge_hidden)
    g_first = g_sum + mm_back(ge_hidden, e_up)
    ge_resid, e_gain_one, e_shift_one = norm_back(g_first, e_kept_one, e_gains[0])
    ge_branch = ge_resid.astype(BF16)
    w_e_out = mm_rows(e_mixed, ge_branch)
    ge_mixed = mm_back(ge_branch, e_out).astype(BF16)
    ge_attended = to_heads(ge_mixed, parts, micro)
    (ge_joined,) = attend_back(e_joined, [], *src_info, ge_attended, False, BF16)
    ge_joined = ge_joined.reshape(parts * micro * src_rows, -1)
    w_e_qkv = mm_rows(source_all.reshape(-1, D), ge_joined)
    g_source_all = mm_back(ge_joined, e_qkv_here).astype(BF16)
    g_source = ge_resid + lax.psum_scatter(
        g_source_all.reshape(parts, micro * src_rows, D), "head", scatter_dimension=0, tiled=False
    ).astype(F32)
    e_joined_sums = head_columns_back(row_sum(ge_joined)[None], parts).reshape(HEADS, 3, HEAD_DIM)

    def pieces(value):
        return value.astype(BF16).reshape(devices, value.shape[0] // devices, value.shape[1])

    decoder_sums = scatter(
        [
            pieces(head_columns_back(w_d_qkv.astype(BF16), parts)),
            pieces(w_d_out),
            pieces(w_c_query),
            pieces(w_c_pairs),
            pieces(w_c_out),
            pieces(w_d_up),
            pieces(w_d_down),
        ],
        "xyyxyyx",
        6,
    )
    small_grads = jnp.concatenate(
        [
            e_gain_one[None],
            e_gain_two[None],
            e_joined_sums[:, 0].reshape(1, D),
            e_joined_sums[:, 2].reshape(1, D),
            row_sum(ge_branch)[None],
            e_shift_one[None],
            row_sum(ge_hidden).reshape(4, D),
            row_sum(g_second_low)[None],
            e_shift_two[None],
            d_gain_one[None],
            d_gain_two[None],
            d_gain_three[None],
            d_joined_sums[:, 0].reshape(1, D),
            d_joined_sums[:, 2].reshape(1, D),
            row_sum(g_branch)[None],
            d_shift_one[None],
            row_sum(g_queries)[None],
            row_sum(g_pairs[:, D:])[None],
            row_sum(g_branch_cross)[None],
            d_shift_two[None],
            row_sum(g_hidden).reshape(4, D),
            row_sum(g_third)[None],
            d_shift_three[None],
        ],
        axis=0,
    )
    small_pieces = (
        small_grads.astype(BF16)
        .reshape(small_rows, devices, small_width)
        .transpose(1, 0, 2)
        .reshape(devices, small_rows * small_width)
    )
    encoder_sums = scatter(
        [
            pieces(head_columns_back(w_e_qkv.astype(BF16), parts)),
            pieces(w_e_out),
            pieces(w_e_up),
            pieces(w_e_down),
            pack_rows(small_pieces, D),
        ],
        "xyyxx",
        7,
    )
    small_sums = encoder_sums[4].reshape(-1)[: small_rows * small_width]
    small_sums = small_sums.reshape(small_rows, small_width)
    return (
        decoded.reshape(micro, tgt_rows, D),
        g_source.reshape(micro, src_rows, D),
        g_target.reshape(micro, tgt_rows, D),
        *encoder_sums[:4],
        small_sums[0:2],
        small_sums[2:12],
        *decoder_sums,
        small_sums[12:15],
        small_sums[15:29],
    )


def solution(mesh):
    in_specs = (
        P(None, ("seq", "head"), None),
        P(None, ("seq", "head"), None),
        P(None, ("seq", "head"), None),
        P(),
        P(),
        P(),
        P(("seq", "head"), None),
        P(("seq", "head"), None),
        P(("seq", "head"), None),
        P(("seq", "head"), None),
        P(None, ("seq", "head")),
        P(None, ("seq", "head")),
        P(("seq", "head"), None),
        P(("seq", "head"), None),
        P(("seq", "head"), None),
        P(("seq", "head"), None),
        P(("seq", "head"), None),
        P(("seq", "head"), None),
        P(("seq", "head"), None),
        P(None, ("seq", "head")),
        P(None, ("seq", "head")),
    )
    out_specs = (
        P(None, ("seq", "head"), None),
        P(None, ("seq", "head"), None),
        P(None, ("seq", "head"), None),
        P(("seq", "head"), None),
        P(("seq", "head"), None),
        P(("seq", "head"), None),
        P(("seq", "head"), None),
        P(None, ("seq", "head")),
        P(None, ("seq", "head")),
        P(("seq", "head"), None),
        P(("seq", "head"), None),
        P(("seq", "head"), None),
        P(("seq", "head"), None),
        P(("seq", "head"), None),
        P(("seq", "head"), None),
        P(("seq", "head"), None),
        P(None, ("seq", "head")),
        P(None, ("seq", "head")),
    )
    return jax.shard_map(shards, mesh=mesh, in_specs=in_specs, out_specs=out_specs, check_vma=False)
```

```python
import functools

import jax
import jax.numpy as jnp
from jax import lax
from jax.experimental import pallas as pl
from jax.experimental.pallas import tpu as pltpu
from jax.sharding import PartitionSpec as P

D = 768
HEADS = 12
HEAD_DIM = 64
FF = 3072
MICRO = 2
STRETCH = 1024
REACH = 2
EVERY = ("seq", "head")

EPSILON = 1e-05
NEGATIVE = -1e30
MESH = pl.DeviceIdType.MESH
F32 = jnp.float32
BF16 = jnp.bfloat16


def place():
    seq, head = lax.axis_index("seq"), lax.axis_index("head")
    return seq // 2, seq % 2, head // 2, head % 2


def device(z, y, x, c):
    return (z * 2 + y, x * 2 + c)


def shard(z, y, x, c):
    return ((z * 2 + y) * 2 + x) * 2 + c


def greet(z, y, x, c):
    barrier = pltpu.get_barrier_semaphore()
    def tell(who):
        pl.semaphore_signal(barrier, inc=1, device_id=who, device_id_type=MESH)
    tell(device(z, y, x, 1 - c))
    tell(device(z, y, 1 - x, c))
    tell(device(z, 1 - y, x, c))
    @pl.when(z > 0)
    def _():
        tell(device(z - 1, y, x, c))
    @pl.when(z < 3)
    def _():
        tell(device(z + 1, y, x, c))
    pl.semaphore_wait(barrier, 3 + (z + 2) // 3 + (5 - z) // 3)


def gather_kernel(count, shared, orders, *refs):
    every = count + shared
    ins, outs = refs[:every], refs[every : 2 * every]
    own_sem, recv_sem, send_sem, group_recv, group_send = refs[2 * every :]
    z, y, x, c = place()
    greet(z, y, x, c)
    here = [(x, y) if order in "xX" else (y, x) for order in orders]

    def shard_of(a, zo, f, l):
        return shard(zo, l, f, c) if orders[a] in "xX" else shard(zo, f, l, c)

    def holder(a, zo, f, l, cc):
        return device(zo, l, f, cc) if orders[a] in "xX" else device(zo, f, l, cc)

    def copy(a, src, where, who, kind):
        return pltpu.make_async_remote_copy(
            src_ref=src,
            dst_ref=outs[a].at[where],
            send_sem=send_sem.at[a, kind, where // 2],
            recv_sem=recv_sem.at[a, where],
            device_id=who,
            device_id_type=MESH,
        )

    def forward(a, src, where, first, up, down):
        f, l = here[a]
        if first:
            copy(a, src, where, holder(a, z, 1 - f, l, c), 0).start()
        if up:

            @pl.when(z < 3)
            def _():
                copy(a, src, where, holder(a, z + 1, f, l, c), 1).start()

        if down:

            @pl.when(z > 0)
            def _():
                copy(a, src, where, holder(a, z - 1, f, l, c), 2).start()

        copy(a, src, where, holder(a, z, f, 1 - l, c), 3).start()
        copy(a, src, where, holder(a, z, f, l, 1 - c), 4).start()

    def arrived(a, where):
        copy(a, outs[a].at[where], where, device(z, y, x, 1 - c), 0).wait_recv()

    def pass_on(a, zo, fo, first, up, down):
        where = shard_of(a, zo, fo, here[a][1])
        arrived(a, where)
        forward(a, outs[a].at[where], where, first, up, down)

    def from_last(zo, other):
        for a in range(count):
            f, l = here[a]
            where = shard_of(a, zo, 1 - f if other else f, 1 - l)
            arrived(a, where)
            copy(a, outs[a].at[where], where, holder(a, z, f, l, 1 - c), 4).start()

    def group_copy(b, src, xo, co, kind, who):
        return pltpu.make_async_remote_copy(
            src_ref=src,
            dst_ref=outs[count + b].at[xo * 2 + co],
            send_sem=group_send.at[b, kind],
            recv_sem=group_recv.at[b, xo * 2 + co],
            device_id=who,
            device_id_type=MESH,
        )

    over, beside = device(z, y, 1 - x, c), device(z, y, x, 1 - c)
    kept = []
    for b in range(shared):
        group_copy(b, ins[count + b], x, c, 0, over).start()
        group_copy(b, ins[count + b], x, c, 1, beside).start()
        kept.append(
            pltpu.make_async_copy(
                ins[count + b], outs[count + b].at[x * 2 + c], own_sem.at[count + b]
            )
        )
        kept[-1].start()
    for a in range(count):
        me = shard_of(a, z, *here[a])
        forward(a, ins[a], me, True, True, True)
        kept.append(pltpu.make_async_copy(ins[a], outs[a].at[me], own_sem.at[a]))
        kept[-1].start()
    for a in range(count):
        early = orders[a] in "XY"
        pass_on(a, z, 1 - here[a][0], False, not early, not early)
    from_last(z, False)
    from_last(z, True)
    for b in range(shared):
        landed = outs[count + b].at[(1 - x) * 2 + c]
        group_copy(b, landed, 1 - x, c, 2, beside).wait_recv()
        group_copy(b, landed, 1 - x, c, 2, beside).start()
    for distance in (1, 2, 3):
        for below in (True, False):

            @pl.when((z >= distance) if below else (z + distance <= 3))
            def _():
                zo = z - distance if below else z + distance
                for a in range(count):
                    early = orders[a] in "XY"
                    pass_on(a, zo, here[a][0], early, below, not below)
                    if not early:
                        pass_on(a, zo, 1 - here[a][0], False, below, not below)

        for below in (True, False):

            @pl.when((z >= distance) if below else (z + distance <= 3))
            def _():
                zo = z - distance if below else z + distance
                for a in range(count):
                    if orders[a] in "XY":
                        pass_on(a, zo, 1 - here[a][0], False, False, False)
                from_last(zo, False)
                from_last(zo, True)

    def sent(a, where, kind):
        copy(a, ins[a], where, device(z, y, x, 1 - c), kind).wait_send()

    def cores(i, carry):
        for a in range(count):
            arrived(a, i * 2 + 1 - c)
            sent(a, i * 2 + c, 4)
        return carry

    lax.fori_loop(0, 16, cores, 0)
    for b in range(shared):
        first, landed = ins[count + b], outs[count + b].at[(1 - x) * 2 + c]
        group_copy(b, first, x, 1 - c, 1, beside).wait_recv()
        group_copy(b, first, 1 - x, 1 - c, 1, beside).wait_recv()
        group_copy(b, first, x, c, 0, over).wait_send()
        group_copy(b, first, x, c, 1, beside).wait_send()
        group_copy(b, landed, 1 - x, c, 2, beside).wait_send()
    for copied in kept:
        copied.wait()
    for a in range(count):
        f, l = here[a]
        early = orders[a] in "XY"
        if not early:
            sent(a, shard_of(a, z, f, l), 0)
        for zo in range(4):
            if early:
                sent(a, shard_of(a, zo, f, l), 0)
            for fo in range(2):
                sent(a, shard_of(a, zo, fo, l), 3)
            for fo in [f] if early else [0, 1]:

                @pl.when((zo <= z) & (z < 3))
                def _():
                    sent(a, shard_of(a, zo, fo, l), 1)

                @pl.when((zo >= z) & (z > 0))
                def _():
                    sent(a, shard_of(a, zo, fo, l), 2)


def traffic(arrays, share):
    size = sum(v.size * v.dtype.itemsize for v in arrays)
    return pl.CostEstimate(flops=0, transcendentals=0, bytes_accessed=size * share)


def gather_all(arrays, orders, collective_id, group_arrays=()):
    count, shared = len(arrays), len(group_arrays)
    every = [*arrays, *group_arrays]
    copies = [32] * count + [4] * shared
    D = pltpu.SemaphoreType.DMA
    return pl.pallas_call(
        functools.partial(gather_kernel, count, shared, orders),
        out_shape=[jax.ShapeDtypeStruct((n,) + v.shape, v.dtype) for n, v in zip(copies, every)],
        in_specs=[pl.BlockSpec(memory_space=pl.ANY)] * len(every),
        out_specs=[pl.BlockSpec(memory_space=pl.ANY)] * len(every),
        scratch_shapes=[
            D((len(every),)),
            D((count, 32)),
            D((count, 5, 16)),
            D((max(shared, 1), 4)),
            D((max(shared, 1), 3)),
        ],
        compiler_params=pltpu.CompilerParams(collective_id=collective_id, has_side_effects=True),
        cost_estimate=traffic(arrays, 500),
        name="gather_all",
    )(*every)


def scatter_kernel(count, shared, orders, *refs):
    every = count + shared
    grads, outs, refs = refs[:every], refs[every : 2 * every], refs[2 * every :]
    held, mine, near, mid, right, left = [refs[k * count : (k + 1) * count] for k in range(6)]
    refs = refs[6 * count :]
    mine_sem, core_sem, near_sem, mid_sem, right_sem, left_sem, group_sem, refs = (
        *refs[:7],
        refs[7:],
    )
    group_held, group_mine, group_last = [refs[k * shared : (k + 1) * shared] for k in range(3)]
    z, y, x, c = place()
    greet(z, y, x, c)
    half = z // 2
    here = [(x, y) if order in "xX" else (y, x) for order in orders]
    late = [order in "XY" for order in orders]

    def block(a, zt, f, l):
        return (zt * 2 + l) * 2 + f if orders[a] in "xX" else (zt * 2 + f) * 2 + l

    def remote(a, src, dst, sems, slot, who):
        return pltpu.make_async_remote_copy(
            src_ref=src,
            dst_ref=dst,
            send_sem=sems.at[a, 0, slot],
            recv_sem=sems.at[a, 1, slot],
            device_id=who,
            device_id_type=MESH,
        )

    def core_copy(a, q):
        who = device(z, y, x, 1 - c)
        return remote(a, grads[a].at[q * 2 + 1 - c], held[a].at[q], core_sem, q, who)

    def mine_copy(a, q):
        return pltpu.make_async_copy(grads[a].at[q * 2 + c], mine[a].at[q], mine_sem.at[a, q])

    def along(a, first):
        flip_x = (orders[a] in "xX") == first
        return device(z, y, 1 - x, c) if flip_x else device(z, 1 - y, x, c)

    def near_copy(a, q, slot):
        return remote(a, held[a].at[q], near[a].at[slot], near_sem, slot, along(a, True))

    def mid_copy(a, q, slot):
        return remote(a, held[a].at[q], mid[a].at[slot], mid_sem, slot, along(a, False))

    def right_copy(a, q, slot):
        return remote(a, held[a].at[q], right[a].at[slot], right_sem, slot, device(z + 1, y, x, c))

    def left_copy(a, q, slot):
        return remote(a, held[a].at[q], left[a].at[slot], left_sem, slot, device(z - 1, y, x, c))

    def far(k):
        return 3 - k + half * (2 * k - 3)

    def others(k):
        down = 3 - k - (k // 2) * z
        up = k + (k // 2) * (3 - z)
        return down + half * (up - down)

    def add(a, q, *terms):
        total = held[a][q].astype(F32)
        for ref, slot in terms:
            total = total + ref[slot].astype(F32)
        held[a][q] = total.astype(BF16)

    for side in (True, False):

        def start(i, carry, side=side):
            for a in range(count):
                f = here[a][0]
                q = block(a, far(i // 2), 1 - f if side else f, i % 2)
                core_copy(a, q).start()
                mine_copy(a, q).start()
            return carry

        lax.fori_loop(0, 8, start, 0)

    def group_copy(b, kind):
        if kind < 2:
            xt = 1 - x if kind == 0 else x
            return pltpu.make_async_remote_copy(
                src_ref=grads[count + b].at[xt * 2 + 1 - c],
                dst_ref=group_held[b].at[kind],
                send_sem=group_sem.at[b, 0, kind],
                recv_sem=group_sem.at[b, 1, kind],
                device_id=device(z, y, x, 1 - c),
                device_id_type=MESH,
            )
        if kind < 4:
            xt = 1 - x if kind == 2 else x
            return pltpu.make_async_copy(
                grads[count + b].at[xt * 2 + c], group_mine[b].at[kind - 2], group_sem.at[b, 0, kind]
            )
        return pltpu.make_async_remote_copy(
            src_ref=group_held[b].at[0],
            dst_ref=group_last[b],
            send_sem=group_sem.at[b, 0, 4],
            recv_sem=group_sem.at[b, 1, 4],
            device_id=device(z, y, 1 - x, c),
            device_id_type=MESH,
        )

    def in_pieces(rows, step):
        piece = rows // 8

        def body(i, carry):
            step(pl.ds(pl.multiple_of(i * piece, piece), piece))
            return carry

        lax.fori_loop(0, 8, body, 0)

    for b in range(shared):
        for kind in range(4):
            group_copy(b, kind).start()

    def first_step(i, carry):
        zt, lt = far(i // 2), i % 2
        for a in range(count):
            q = block(a, zt, 1 - here[a][0], lt)
            core_copy(a, q).wait_recv()
            mine_copy(a, q).wait()
            add(a, q, (mine[a], q))
            near_copy(a, q, zt * 2 + lt).start()
        return carry

    lax.fori_loop(0, 8, first_step, 0)
    for b in range(shared):
        group_copy(b, 0).wait_recv()
        group_copy(b, 2).wait()

        def to_other(cut, b=b):
            total = group_held[b][0, cut, :].astype(F32) + group_mine[b][0, cut, :].astype(F32)
            group_held[b][0, cut, :] = total.astype(BF16)

        in_pieces(group_last[b].shape[0], to_other)
        group_copy(b, 4).start()

    def summed(a, zt, lt):
        q = block(a, zt, here[a][0], lt)
        core_copy(a, q).wait_recv()
        mine_copy(a, q).wait()
        near_copy(a, q, zt * 2 + lt).wait_recv()
        add(a, q, (mine[a], q), (near[a], zt * 2 + lt))
        return q

    if any(late):

        def mid_step(i, carry):
            zt = far(i)
            for a in range(count):
                if late[a]:
                    mid_copy(a, summed(a, zt, 1 - here[a][1]), zt).start()
            return carry

        lax.fori_loop(0, 4, mid_step, 0)

    def slots(a, zt, lt):
        return (zt - 1, zt) if late[a] else ((zt - 1) * 2 + lt, zt * 2 + lt)

    def along_z(a, zt, lt):
        q = summed(a, zt, lt)
        if late[a]:
            mid_copy(a, q, zt).wait_recv()
            add(a, q, (mid[a], zt))
        up, down = slots(a, zt, lt)

        @pl.when(zt > z)
        def _():
            @pl.when(z > 0)
            def _():
                right_copy(a, q, up).wait_recv()
                add(a, q, (right[a], up))

            right_copy(a, q, up).start()

        @pl.when(zt < z)
        def _():
            @pl.when(z < 3)
            def _():
                left_copy(a, q, down).wait_recv()
                add(a, q, (left[a], down))

            left_copy(a, q, down).start()

    def z_step(k, carry):
        for a in range(count):
            if late[a]:
                along_z(a, others(k), here[a][1])
            else:
                along_z(a, others(k), 0)
                along_z(a, others(k), 1)
        return carry

    lax.fori_loop(0, 3, z_step, 0)

    def from_z(a, q, lt):
        up, down = slots(a, z, lt)

        @pl.when(z > 0)
        def _():
            right_copy(a, q, up).wait_recv()
            add(a, q, (right[a], up))

        @pl.when(z < 3)
        def _():
            left_copy(a, q, down).wait_recv()
            add(a, q, (left[a], down))

    for a in range(count):
        if not late[a]:
            lt = 1 - here[a][1]
            q = summed(a, z, lt)
            from_z(a, q, lt)
            mid_copy(a, q, 0).start()
    for a in range(count):
        lt = here[a][1]
        q = summed(a, z, lt)
        if late[a]:
            mid_copy(a, q, z).wait_recv()
            add(a, q, (mid[a], z))
        from_z(a, q, lt)
    for a in range(count):
        q = block(a, z, *here[a])
        total = held[a][q].astype(F32)
        if not late[a]:
            mid_copy(a, q, 0).wait_recv()
            total = total + mid[a][0].astype(F32)
        outs[a][...] = total.astype(outs[a].dtype)

    for b in range(shared):
        group_copy(b, 1).wait_recv()
        group_copy(b, 3).wait()
        group_copy(b, 4).wait_recv()

        def at_home(cut, b=b):
            total = group_held[b][1, cut, :].astype(F32) + group_mine[b][1, cut, :].astype(F32)
            outs[count + b][cut, :] = total + group_last[b][cut, :].astype(F32)

        in_pieces(group_last[b].shape[0], at_home)
        for kind in (0, 1, 4):
            group_copy(b, kind).wait_send()

    def sent_core(i, carry):
        for a in range(count):
            core_copy(a, i).wait_send()
        return carry

    lax.fori_loop(0, 16, sent_core, 0)

    def sent_near(i, carry):
        for a in range(count):
            near_copy(a, block(a, i // 2, 1 - here[a][0], i % 2), i).wait_send()
        return carry

    lax.fori_loop(0, 8, sent_near, 0)

    def sent_z(k, carry):
        zt = others(k)
        for a in range(count):
            for lt in [here[a][1]] if late[a] else [0, 1]:
                q = block(a, zt, here[a][0], lt)
                up, down = slots(a, zt, lt)

                @pl.when(zt > z)
                def _():
                    right_copy(a, q, up).wait_send()

                @pl.when(zt < z)
                def _():
                    left_copy(a, q, down).wait_send()

        return carry

    lax.fori_loop(0, 3, sent_z, 0)
    for a in range(count):
        f, l = here[a]
        if late[a]:
            for zt in range(4):
                mid_copy(a, block(a, zt, f, 1 - l), zt).wait_send()
        else:
            mid_copy(a, block(a, z, f, 1 - l), 0).wait_send()


def scatter_sum(arrays, orders, collective_id, out_dtype=F32, group_arrays=()):
    count, shared = len(arrays), len(group_arrays)
    shapes = [v.shape[1:] for v in (*arrays, *group_arrays)]
    late = [order in "XY" for order in orders]
    sizes = [[16, 16, 8, 4, 3, 3] if up else [16, 16, 8, 1, 6, 6] for up in late]
    scratch = []
    for k in range(6):
        scratch += [pltpu.VMEM((size[k],) + shape, BF16) for size, shape in zip(sizes, shapes)]
    scratch += [pltpu.SemaphoreType.DMA((count, 16))]
    scratch += [pltpu.SemaphoreType.DMA((count, 2, n)) for n in (16, 8, 4, 6, 6)]
    scratch += [pltpu.SemaphoreType.DMA((max(shared, 1), 2, 5))]
    scratch += [pltpu.VMEM((2,) + shape, BF16) for shape in shapes[count:]] * 2
    scratch += [pltpu.VMEM(shape, BF16) for shape in shapes[count:]]
    return pl.pallas_call(
        functools.partial(scatter_kernel, count, shared, orders),
        out_shape=[jax.ShapeDtypeStruct(shape, out_dtype) for shape in shapes],
        in_specs=[pl.BlockSpec(memory_space=pl.ANY)] * len(shapes),
        out_specs=[pl.BlockSpec(memory_space=pltpu.VMEM)] * len(shapes),
        scratch_shapes=scratch,
        compiler_params=pltpu.CompilerParams(
            collective_id=collective_id, has_side_effects=True, vmem_limit_bytes=60 << 20
        ),
        cost_estimate=traffic(arrays, 1),
        name="scatter_sum",
    )(*arrays, *group_arrays)


def known_mesh():
    return lax.axis_size("seq") == 8 and lax.axis_size("head") == 4


def gather(arrays, orders, collective_id, group_arrays=()):
    if known_mesh():
        return gather_all(arrays, orders, collective_id, group_arrays)
    return [lax.all_gather(v, EVERY, axis=0, tiled=False) for v in arrays] + [
        lax.all_gather(v, "head", axis=0, tiled=False) for v in group_arrays
    ]


def scatter(arrays, orders, collective_id, out_dtype=F32, group_arrays=()):
    if known_mesh():
        return scatter_sum(arrays, orders, collective_id, out_dtype, group_arrays)
    return [
        lax.psum_scatter(v, axes, scatter_dimension=0, tiled=False).astype(out_dtype)
        for v, axes in [(v, EVERY) for v in arrays] + [(v, "head") for v in group_arrays]
    ]


def fill(target, refs, columns, scale=None):
    at = 0
    for ref in refs:
        rows = ref.shape[2]
        for p in range(ref.shape[0]):
            piece = ref[p, 0, :, columns]
            target[at : at + rows] = piece if scale is None else piece * scale
            at += rows


def spill(value, refs, columns):
    at = 0
    for ref in refs:
        rows = ref.shape[2]
        for p in range(ref.shape[0]):
            ref[p, 0, :, columns] = value[at : at + rows].astype(ref.dtype)
            at += rows


def across(left, right):
    return lax.dot_general(left, right, (((1,), (1,)), ((), ())), preferred_element_type=F32)


def down(left, right):
    return lax.dot_general(left, right, (((0,), (0,)), ((), ())), preferred_element_type=F32)


def soft_columns(scores):
    peak = jnp.max(scores, axis=0, keepdims=True)
    weights = jnp.exp(scores - peak)
    total = jnp.sum(weights, axis=0, keepdims=True)
    return weights * (1.0 / total), peak + jnp.log(total)


def score_grads(probs, grad_probs):
    delta = jnp.sum(probs * grad_probs, axis=0, keepdims=True)
    return (probs * (grad_probs - delta)).astype(BF16)


def allowed_pairs(key_ref, query_ref, start, tile, causal):
    doc_key, doc_query = key_ref[0, :, 0:1], query_ref[0, 0:1, pl.ds(start, tile)]
    allowed = doc_key == doc_query
    if causal:
        allowed &= key_ref[0, :, 1:2] <= query_ref[0, 1:2, pl.ds(start, tile)]
    return allowed


def attend_kernel(heads, tile, causal, *refs):
    key_ref, query_ref, own_ref = refs[:3]
    prior = refs[3:-6]
    out_ref, log_ref, key_s, value_s, query_s, result_s = refs[-6:]
    group = query_s.shape[0]
    for h in range(heads):
        fill(key_s, (*prior, own_ref), slice(h * 128, h * 128 + 64))
        fill(value_s, (*prior, own_ref), slice(h * 128 + 64, h * 128 + 128))
        at = heads * 128 + h * 64
        fill(query_s, (own_ref,), slice(at, at + 64), 0.125)

        def step(i, carry):
            start = pl.multiple_of(i * tile, tile)
            allowed = allowed_pairs(key_ref, query_ref, start, tile, causal)
            scores = across(key_s[...], query_s[pl.ds(start, tile), :])
            probs, log_total = soft_columns(jnp.where(allowed, scores, NEGATIVE))
            result_s[pl.ds(start, tile), :] = down(probs.astype(BF16), value_s[...]).astype(BF16)
            log_ref[0, h : h + 1, pl.ds(start, tile)] = log_total
            return carry

        lax.fori_loop(0, group // tile, step, 0)
        spill(result_s[...], (out_ref,), slice(h * 64, h * 64 + 64))


def rows_spec(shape):
    return pl.BlockSpec((shape[0], 1) + shape[2:], lambda m: (0, m, 0, 0))


def whole_spec(shape):
    return pl.BlockSpec((1,) + shape[1:], lambda m: (m, 0, 0))


def attend(joined, prior, key_info, query_info, heads, causal, tile=256):
    parts, micro, rows, _ = joined.shape
    group = parts * rows
    keys = key_info.shape[1]
    out, logs = (parts, micro, rows, heads * 64), (micro, heads, group)
    return pl.pallas_call(
        functools.partial(attend_kernel, heads, tile, causal),
        grid=(micro,),
        out_shape=[jax.ShapeDtypeStruct(out, BF16), jax.ShapeDtypeStruct(logs, F32)],
        in_specs=[whole_spec(key_info.shape), whole_spec(query_info.shape), rows_spec(joined.shape)]
        + [rows_spec(p.shape) for p in prior],
        out_specs=[rows_spec(out), whole_spec(logs)],
        scratch_shapes=[
            pltpu.VMEM((keys, 64), BF16),
            pltpu.VMEM((keys, 64), BF16),
            pltpu.VMEM((group, 64), BF16),
            pltpu.VMEM((group, 64), BF16),
        ],
        compiler_params=pltpu.CompilerParams(vmem_limit_bytes=48 << 20),
        cost_estimate=pl.CostEstimate(
            flops=16 * micro * heads * group * keys * 128,
            transcendentals=micro * heads * group * keys,
            bytes_accessed=joined.size * 4,
        ),
        name="attend",
    )(key_info, query_info, joined, *prior)


def attend_back_kernel(heads, tile, causal, count, *refs):
    key_ref, query_ref, own_ref, log_ref, grad_ref = refs[:5]
    prior = refs[5 : 5 + count]
    out_ref, *prior_out = refs[5 + count : 6 + 2 * count]
    key_s, value_s, query_s, grad_s, gk_s, gv_s, result_s = refs[6 + 2 * count :]
    group = query_s.shape[0]
    for h in range(heads):
        key_cut, value_cut = slice(h * 128, h * 128 + 64), slice(h * 128 + 64, h * 128 + 128)
        fill(key_s, (*prior, own_ref), key_cut)
        fill(value_s, (*prior, own_ref), value_cut)
        query_cut = slice(heads * 128 + h * 64, heads * 128 + h * 64 + 64)
        fill(query_s, (own_ref,), query_cut, 0.125)
        fill(grad_s, (grad_ref,), slice(h * 64, h * 64 + 64))
        gk_s[...] = jnp.zeros_like(gk_s)
        gv_s[...] = jnp.zeros_like(gv_s)

        def step(i, carry):
            start = pl.multiple_of(i * tile, tile)
            here = pl.ds(start, tile)
            allowed = allowed_pairs(key_ref, query_ref, start, tile, causal)
            query, grad_out = query_s[here, :], grad_s[here, :]
            scores = jnp.where(allowed, across(key_s[...], query), NEGATIVE)
            probs = jnp.exp(scores - log_ref[0, h : h + 1, here])
            grad_scores = score_grads(probs, across(value_s[...], grad_out))
            gv_s[...] += jnp.dot(probs.astype(BF16), grad_out, preferred_element_type=F32)
            gk_s[...] += jnp.dot(grad_scores, query, preferred_element_type=F32)
            result_s[here, :] = down(grad_scores, key_s[...]) * 0.125
            return carry

        lax.fori_loop(0, group // tile, step, 0)
        spill(result_s[...], (out_ref,), query_cut)
        spill(gk_s[...], (*prior_out, out_ref), key_cut)
        spill(gv_s[...], (*prior_out, out_ref), value_cut)
    for p in range(out_ref.shape[0]):
        out_ref[p, 0, :, heads * 192 :] = jnp.zeros(
            (out_ref.shape[2], out_ref.shape[3] - heads * 192), out_ref.dtype
        )


def attend_back(
    joined, prior, key_info, query_info, logs, grad, heads, causal, out_dtype, tile=256
):
    parts, micro, rows, _ = joined.shape
    group = parts * rows
    keys = key_info.shape[1]
    return pl.pallas_call(
        functools.partial(attend_back_kernel, heads, tile, causal, len(prior)),
        grid=(micro,),
        out_shape=[jax.ShapeDtypeStruct(joined.shape, out_dtype)]
        + [jax.ShapeDtypeStruct(p.shape, BF16) for p in prior],
        in_specs=[
            whole_spec(key_info.shape),
            whole_spec(query_info.shape),
            rows_spec(joined.shape),
            whole_spec(logs.shape),
            rows_spec(grad.shape),
        ]
        + [rows_spec(p.shape) for p in prior],
        out_specs=[rows_spec(joined.shape)] + [rows_spec(p.shape) for p in prior],
        scratch_shapes=[
            pltpu.VMEM((keys, 64), BF16),
            pltpu.VMEM((keys, 64), BF16),
            pltpu.VMEM((group, 64), BF16),
            pltpu.VMEM((group, 64), BF16),
            pltpu.VMEM((keys, 64), F32),
            pltpu.VMEM((keys, 64), F32),
            pltpu.VMEM((group, 64), F32),
        ],
        compiler_params=pltpu.CompilerParams(vmem_limit_bytes=48 << 20),
        cost_estimate=pl.CostEstimate(
            flops=24 * micro * heads * group * keys * 128,
            transcendentals=micro * heads * group * keys,
            bytes_accessed=joined.size * 6,
        ),
        name="attend_back",
    )(key_info, query_info, joined, logs, grad, *prior)


def cross_kernel(query_ref, pairs_ref, out_ref, log_ref):
    for i in range(D // 128):
        outs = []
        for h in range(2):
            at = i * 128 + h * 64
            query, keys = query_ref[0, :, at : at + 64] * 0.125, pairs_ref[0, :, at : at + 64]
            values = pairs_ref[0, :, D + at : D + at + 64]
            probs, log_total = soft_columns(across(keys, query))
            outs.append(down(probs.astype(BF16), values))
            log_ref[0, i * 2 + h : i * 2 + h + 1, :] = log_total
        out_ref[0, :, i * 128 : i * 128 + 128] = jnp.concatenate(outs, axis=1).astype(BF16)


def cross(query, pairs):
    micro, rows, _ = query.shape
    keys = pairs.shape[1]
    logs = (micro, HEADS, rows)
    return pl.pallas_call(
        cross_kernel,
        grid=(micro,),
        out_shape=[jax.ShapeDtypeStruct(query.shape, BF16), jax.ShapeDtypeStruct(logs, F32)],
        in_specs=[whole_spec(query.shape), whole_spec(pairs.shape)],
        out_specs=[whole_spec(query.shape), whole_spec(logs)],
        compiler_params=pltpu.CompilerParams(vmem_limit_bytes=48 << 20),
        cost_estimate=pl.CostEstimate(
            flops=16 * micro * HEADS * rows * keys * 128,
            transcendentals=micro * HEADS * rows * keys,
            bytes_accessed=pairs.size * 2,
        ),
        name="cross",
    )(query, pairs)


def cross_back_kernel(
    query_ref, pairs_ref, log_ref, grad_ref, grad_query_ref, grad_pairs_ref
):
    for i in range(D // 128):
        query_parts, key_parts, value_parts = [], [], []
        for h in range(2):
            at = i * 128 + h * 64
            cut = slice(at, at + 64)
            query, keys = query_ref[0, :, cut] * 0.125, pairs_ref[0, :, cut]
            values, grad_out = pairs_ref[0, :, D + at : D + at + 64], grad_ref[0, :, cut]
            probs = jnp.exp(across(keys, query) - log_ref[0, i * 2 + h : i * 2 + h + 1, :])
            grad_scores = score_grads(probs, across(values, grad_out))
            value_parts.append(jnp.dot(probs.astype(BF16), grad_out, preferred_element_type=F32))
            key_parts.append(jnp.dot(grad_scores, query, preferred_element_type=F32))
            query_parts.append(down(grad_scores, keys) * 0.125)
        cut = slice(i * 128, i * 128 + 128)
        grad_query_ref[0, :, cut] = jnp.concatenate(query_parts, axis=1).astype(BF16)
        grad_pairs_ref[0, :, cut] = jnp.concatenate(key_parts, axis=1).astype(BF16)
        cut = slice(D + i * 128, D + i * 128 + 128)
        grad_pairs_ref[0, :, cut] = jnp.concatenate(value_parts, axis=1).astype(BF16)


def cross_back(query, pairs, logs, grad):
    micro, rows, _ = query.shape
    keys = pairs.shape[1]
    return pl.pallas_call(
        cross_back_kernel,
        grid=(micro,),
        out_shape=[jax.ShapeDtypeStruct(query.shape, BF16), jax.ShapeDtypeStruct(pairs.shape, BF16)],
        in_specs=[whole_spec(v.shape) for v in (query, pairs, logs, grad)],
        out_specs=[whole_spec(query.shape), whole_spec(pairs.shape)],
        compiler_params=pltpu.CompilerParams(vmem_limit_bytes=48 << 20),
        cost_estimate=pl.CostEstimate(
            flops=24 * micro * HEADS * rows * keys * 128,
            transcendentals=micro * HEADS * rows * keys,
            bytes_accessed=pairs.size * 4,
        ),
        name="cross_back",
    )(query, pairs, logs, grad)


SMALL_ROWS = 29
SINGLES = (4, 0, 5, 10, 1, 11, 17, 12, 18, 19, 21, 13, 22, 27, 14, 28)


def head_places(head, heads):
    base = head // heads * joined_width(heads) + head % heads * 64
    return base + head % heads * 64 + 64, base + heads * 128


def joined_width(heads):
    return (heads * 192 + 127) // 128 * 128


def unpack_kernel(width, heads, pack_ref, *refs):
    e_joined, e_hidden, d_joined, d_hidden, pair_bias = refs[:5]
    singles, full = refs[5:-1], refs[-1]
    for d in range(pack_ref.shape[0]):
        full[:, d * width : d * width + width] = pack_ref[d, :, 0:width].astype(F32)
    for target, row in ((e_joined, 2), (d_joined, 15)):
        target[...] = jnp.zeros_like(target)
        for head in range(HEADS):
            value_at, query_at = head_places(head, heads)
            cut = slice(head * 64, head * 64 + 64)
            target[:, query_at : query_at + 64] = full[row : row + 1, cut]
            target[:, value_at : value_at + 64] = full[row + 1 : row + 2, cut]
    for target, row in ((e_hidden, 6), (d_hidden, 23)):
        for k in range(FF // D):
            target[:, k * D : k * D + D] = full[row + k : row + k + 1, :]
    pair_bias[:, 0:D] = jnp.zeros((1, D), F32)
    pair_bias[:, D:] = full[20:21, :]
    for target, row in zip(singles, SINGLES):
        target[...] = full[row : row + 1, :]


def unpack_small(packs, heads):
    devices = packs.shape[0]
    joined = joined_width(heads) * (HEADS // heads)
    widths = [joined, FF, joined, FF, 2 * D] + [D] * len(SINGLES)
    return pl.pallas_call(
        functools.partial(unpack_kernel, D // devices, heads),
        out_shape=[jax.ShapeDtypeStruct((1, w), F32) for w in widths],
        scratch_shapes=[pltpu.VMEM((32, D), F32)],
        name="unpack_small",
    )(packs)


def pack_kernel(width, heads, count, *refs):
    e_joined, e_hidden, d_joined, d_hidden, pair_sum = refs[:5]
    singles, out_ref, full = refs[5 : 5 + count], refs[-2], refs[-1]
    full[...] = jnp.zeros_like(full)
    for source, row in ((e_joined, 2), (d_joined, 15)):
        for head in range(HEADS):
            value_at, query_at = head_places(head, heads)
            cut = slice(head * 64, head * 64 + 64)
            full[row : row + 1, cut] = source[:, query_at : query_at + 64]
            full[row + 1 : row + 2, cut] = source[:, value_at : value_at + 64]
    for source, row in ((e_hidden, 6), (d_hidden, 23)):
        for k in range(FF // D):
            full[row + k : row + k + 1, :] = source[:, k * D : k * D + D]
    full[20:21, :] = pair_sum[:, D:]
    for source, row in zip(singles, SINGLES):
        full[row : row + 1, :] = source[...]
    out_ref[...] = jnp.zeros_like(out_ref)
    for d in range(out_ref.shape[0]):
        out_ref[d, :, 0:width] = full[:, d * width : d * width + width].astype(BF16)


def pack_small(vectors, devices, heads):
    return pl.pallas_call(
        functools.partial(pack_kernel, D // devices, heads, len(SINGLES)),
        out_shape=jax.ShapeDtypeStruct((devices, 32, 128), BF16),
        scratch_shapes=[pltpu.VMEM((32, D), F32)],
        name="pack_small",
    )(*vectors)


def norm(resid, gain, shift):
    center = resid - jnp.mean(resid, axis=-1, keepdims=True)
    scale = lax.rsqrt(jnp.mean(center * center, axis=-1, keepdims=True) + EPSILON)
    hat = center * scale
    return hat * gain + shift, (hat, scale)


def norm_back(grad, kept, gain):
    hat, scale = kept
    inner = grad * gain
    grad_resid = scale * (
        inner
        - jnp.mean(inner, axis=-1, keepdims=True)
        - hat * jnp.mean(inner * hat, axis=-1, keepdims=True)
    )
    gain_sum = jnp.sum(grad * hat, axis=0, keepdims=True)
    return grad_resid, gain_sum, jnp.sum(grad, axis=0, keepdims=True)


def gelu(value):
    return value * (1.0 + lax.erf(value * 0.7071067811865476)) * 0.5


def gelu_slope(value):
    bell = jnp.exp(value * value * -0.5) * 0.3989422804014327
    return 0.5 * (1.0 + lax.erf(value * 0.7071067811865476)) + value * bell


def mm(left, right):
    return jnp.dot(left, right, preferred_element_type=F32)


def mm_rows(left, right):
    return lax.dot_general(left, right, (((0,), (0,)), ((), ())), preferred_element_type=F32)


def mm_back(left, right):
    return lax.dot_general(left, right, (((1,), (1,)), ((), ())), preferred_element_type=F32)


def row_sum(value):
    return jnp.sum(value.astype(F32), axis=0, keepdims=True)


def doc_starts(lengths):
    count = lengths.shape[1]
    before = jnp.arange(count)[None, :] < jnp.arange(count)[:, None]
    return jnp.sum(jnp.where(before[None], lengths[:, None, :], 0), axis=2)


def doc_ids(starts, positions):
    return jnp.sum((starts[:, None, :] <= positions[None, :, None]).astype(jnp.int32), axis=2) - 1


def key_and_query_info(starts, key_pos, query_pos):
    key_docs, query_docs = doc_ids(starts, key_pos), doc_ids(starts, query_pos)
    micro = starts.shape[0]
    key_info = jnp.stack(
        [key_docs, jnp.broadcast_to(key_pos, (micro,) + key_pos.shape)], axis=2
    )
    query_info = jnp.stack(
        [query_docs, jnp.broadcast_to(query_pos, (micro,) + query_pos.shape)], axis=1
    )
    return key_info, query_info


def by_group(weight, parts):
    rows = weight.shape[0]
    split = weight.reshape(rows, parts, HEADS // parts, 3, HEAD_DIM)
    pairs = split[:, :, :, 1:].reshape(rows, parts, -1)
    query = split[:, :, :, 0].reshape(rows, parts, -1)
    width = joined_width(HEADS // parts)
    blank = jnp.zeros((rows, parts, width - pairs.shape[2] - query.shape[2]), weight.dtype)
    return jnp.concatenate([pairs, query, blank], axis=2).reshape(rows, parts * width)


def by_head(grad, parts):
    rows, heads = grad.shape[0], HEADS // parts
    split = grad.reshape(rows, parts, -1)
    pairs = split[:, :, : heads * 128].reshape(rows, parts, heads, 2, HEAD_DIM)
    query = split[:, :, heads * 128 : heads * 192].reshape(rows, parts, heads, 1, HEAD_DIM)
    return jnp.concatenate([query, pairs], axis=3).reshape(rows, 3 * D)


def to_beside_rows(grad, devices):
    split = grad.reshape(devices, FF // D, -1, D)
    return split.transpose(0, 2, 1, 3).reshape(D, FF)


def my_columns(full, parts):
    width = full.shape[1] // parts
    return lax.dynamic_slice_in_dim(full, lax.axis_index("head") * width, width, 1)


def all_columns(mine, parts):
    rows, width = mine.shape
    full = jnp.zeros((rows, width * parts), mine.dtype)
    return lax.dynamic_update_slice_in_dim(full, mine, lax.axis_index("head") * width, 1)


def to_tokens(value):
    parts, micro, rows, columns = value.shape
    got = lax.all_to_all(value, "head", split_axis=0, concat_axis=0, tiled=True)
    return got.transpose(1, 2, 0, 3).reshape(micro * rows, parts * columns)


def to_heads(value, parts, micro):
    rows = value.shape[0] // micro
    split = value.reshape(micro, rows, parts, -1).transpose(2, 0, 1, 3)
    return lax.all_to_all(split, "head", split_axis=0, concat_axis=0, tiled=True)


def from_before(value, by):
    count = lax.axis_size("seq")
    return lax.ppermute(value, "seq", [(i, i + by) for i in range(count - by)])


def to_before(value, by):
    count = lax.axis_size("seq")
    return lax.ppermute(value, "seq", [(i + by, i) for i in range(count - by)])


def shards(
    source,
    target,
    cotangent,
    src_lengths,
    tgt_lengths,
    retrieved,
    encoder_qkv,
    encoder_out,
    encoder_up,
    encoder_down,
    encoder_gains,
    encoder_biases,
    decoder_qkv,
    decoder_out,
    cross_query,
    cross_keyvalue,
    cross_out,
    decoder_up,
    decoder_down,
    decoder_gains,
    decoder_biases,
):
    micro, src_rows, _ = source.shape
    tgt_rows = target.shape[1]
    parts = lax.axis_size("head")
    devices = parts * lax.axis_size("seq")
    seq, me = lax.axis_index("seq"), lax.axis_index(EVERY)
    src_group, tgt_group = src_rows * parts, tgt_rows * parts
    asked = retrieved.shape[1]
    source_rows = source.reshape(micro * src_rows, D)
    target_rows = target.reshape(micro * tgt_rows, D)

    heads = HEADS // parts
    small = jnp.concatenate([encoder_gains, encoder_biases, decoder_gains, decoder_biases], axis=0)
    small = jnp.pad(small, ((0, 32 - SMALL_ROWS), (0, 128 - small.shape[1])))
    encoder_full = gather(
        [by_group(encoder_qkv, parts), encoder_out, encoder_up, encoder_down, small],
        "xyxyx",
        0,
        [source, target],
    )
    source_all, target_all = encoder_full[5:]
    decoder_parts = [
        by_group(decoder_qkv, parts),
        decoder_out,
        cross_query,
        cross_keyvalue,
        cross_out,
        decoder_up,
    ]
    decoder_pack, small_full = lax.optimization_barrier(
        (jnp.concatenate(decoder_parts, axis=1), encoder_full[4])
    )
    decoder_full = lax.all_gather(decoder_pack, EVERY, axis=0, tiled=True)
    d_down = lax.all_gather(decoder_down, EVERY, axis=0, tiled=True)
    e_qkv, e_out, e_up, e_down = [v.reshape(-1, v.shape[-1]) for v in encoder_full[:4]]
    e_bias, e_hidden_bias, d_bias, d_hidden_bias, pair_bias, *singles = unpack_small(
        small_full, heads
    )
    e_b2, e_g0, e_b3, e_b8, e_g1, e_b9 = singles[:6]
    d_b2, d_g0, d_b3, d_b4, d_b6, d_g1, d_b7, d_b12, d_g2, d_b13 = singles[6:]

    src_pos = seq * src_group + jnp.arange(src_group, dtype=jnp.int32)
    src_info = key_and_query_info(doc_starts(src_lengths), src_pos, src_pos)
    tgt_pos = seq * tgt_group + jnp.arange(tgt_group, dtype=jnp.int32)
    tgt_key_pos = (seq - REACH) * tgt_group + jnp.arange((REACH + 1) * tgt_group, dtype=jnp.int32)
    tgt_info = key_and_query_info(doc_starts(tgt_lengths), tgt_key_pos, tgt_pos)

    e_qkv_here = my_columns(e_qkv, parts)
    e_joined = (mm(source_all.reshape(-1, D), e_qkv_here) + my_columns(e_bias, parts)).astype(BF16)
    e_joined = e_joined.reshape(parts, micro, src_rows, -1)
    e_attended, e_logs = attend(e_joined, [], *src_info, heads, False)
    e_mixed = to_tokens(e_attended)
    e_first, e_kept_one = norm(
        source_rows.astype(F32) + mm(e_mixed, e_out) + e_b2, e_g0, e_b3
    )
    e_first_low = e_first.astype(BF16)
    e_hidden = mm(e_first_low, e_up) + e_hidden_bias
    e_active = gelu(e_hidden).astype(BF16)
    e_result, e_kept_two = norm(e_first + mm(e_active, e_down) + e_b8, e_g1, e_b9)

    src_own = me * src_rows + jnp.arange(src_rows, dtype=jnp.int32)
    select = (retrieved[:, :, None] == src_own[None, None, :]).astype(BF16)
    picked = jnp.einsum(
        "mrs,msd->mrd",
        select,
        e_result.astype(BF16).reshape(micro, src_rows, D),
        preferred_element_type=F32,
    ).astype(BF16)
    picked = [picked[m].reshape(devices, asked // devices, D) for m in range(micro)]
    fetched = gather(scatter(picked, "xy", 2, BF16), "xy", 3)
    fetched = jnp.concatenate([v.reshape(asked, D) for v in fetched], axis=0)
    decoder_full, fetched = lax.optimization_barrier((decoder_full, fetched))
    ends = [0]
    for part in decoder_parts:
        ends.append(ends[-1] + part.shape[1])
    d_qkv, d_out, c_query, c_pairs, c_out, d_up = [
        decoder_full[:, start:end] for start, end in zip(ends, ends[1:])
    ]

    d_qkv_here = my_columns(d_qkv, parts)
    d_joined = (mm(target_all.reshape(-1, D), d_qkv_here) + my_columns(d_bias, parts)).astype(BF16)
    d_joined = d_joined.reshape(parts, micro, tgt_rows, -1)
    d_pairs = d_joined[..., : heads * 128]
    d_prior = [from_before(d_pairs, by) for by in range(REACH, 0, -1)]
    d_attended, d_logs = attend(d_joined, d_prior, *tgt_info, heads, True)
    d_mixed = to_tokens(d_attended)
    d_first, d_kept_one = norm(
        target_rows.astype(F32) + mm(d_mixed, d_out) + d_b2, d_g0, d_b3
    )
    d_first_low = d_first.astype(BF16)
    queries = (mm(d_first_low, c_query) + d_b4).astype(BF16).reshape(micro, tgt_rows, D)

    pairs = (mm(fetched, c_pairs) + pair_bias).astype(BF16).reshape(micro, asked, 2 * D)

    crossed_rows, cross_logs = cross(queries, pairs)
    crossed = crossed_rows.reshape(micro * tgt_rows, D)
    d_second, d_kept_two = norm(d_first + mm(crossed, c_out) + d_b6, d_g1, d_b7)
    d_second_low = d_second.astype(BF16)
    d_hidden = mm(d_second_low, d_up) + d_hidden_bias
    d_active = gelu(d_hidden).astype(BF16)
    decoded, d_kept_three = norm(d_second + mm(d_active, d_down) + d_b12, d_g2, d_b13)

    grad = cotangent.reshape(micro * tgt_rows, D).astype(F32)
    g_sum, d_gain_three, d_shift_three = norm_back(grad, d_kept_three, d_g2)
    g_third = g_sum.astype(BF16)
    w_d_down = mm_rows(d_active, g_third)
    g_hidden = (mm_back(g_third, d_down) * gelu_slope(d_hidden)).astype(BF16)
    w_d_up = mm_rows(d_second_low, g_hidden)
    g_second = g_sum + mm_back(g_hidden, d_up)
    g_sum_two, d_gain_two, d_shift_two = norm_back(g_second, d_kept_two, d_g1)
    g_branch_cross = g_sum_two.astype(BF16)
    w_c_out = mm_rows(crossed, g_branch_cross)
    g_crossed = mm_back(g_branch_cross, c_out).astype(BF16).reshape(micro, tgt_rows, D)
    g_queries, g_pairs = cross_back(queries, pairs, cross_logs, g_crossed)
    g_queries = g_queries.reshape(micro * tgt_rows, D)
    g_pairs = g_pairs.reshape(micro * asked, 2 * D)
    g_fetched = mm_back(g_pairs, c_pairs).astype(BF16).reshape(micro, asked, D)
    g_fetched = [g_fetched[m].reshape(devices, asked // devices, D) for m in range(micro)]
    g_fetched = gather(scatter(g_fetched, "xy", 4, BF16), "xy", 5)
    w_c_pairs = mm_rows(fetched, g_pairs)
    w_c_query = mm_rows(d_first_low, g_queries)
    decoder_grads = [w_c_query, w_c_pairs, w_c_out, w_d_up]
    decoder_grads = [g.astype(BF16) for g in decoder_grads]
    decoder_grads.append(to_beside_rows(w_d_down.astype(BF16), devices))
    decoder_pack, *g_fetched = lax.optimization_barrier(
        (jnp.concatenate(decoder_grads, axis=1), *g_fetched)
    )
    decoder_sums = lax.psum_scatter(decoder_pack, EVERY, scatter_dimension=0, tiled=True)
    g_first = g_sum_two + mm_back(g_queries, c_query)
    g_resid, d_gain_one, d_shift_one = norm_back(g_first, d_kept_one, d_g0)
    g_branch = g_resid.astype(BF16)
    w_d_out = mm_rows(d_mixed, g_branch)
    g_mixed = mm_back(g_branch, d_out).astype(BF16)
    g_attended = to_heads(g_mixed, parts, micro)
    g_own, *g_prior = attend_back(
        d_joined, d_prior, *tgt_info, d_logs, g_attended, heads, True, F32
    )
    g_back = [to_before(g, by) for g, by in zip(g_prior, range(REACH, 0, -1))]

    g_result = jnp.einsum(
        "mrs,mrd->msd",
        select,
        jnp.stack([v.reshape(asked, D) for v in g_fetched]),
        preferred_element_type=F32,
    ).reshape(micro * src_rows, D)
    g_sum, e_gain_two, e_shift_two = norm_back(g_result, e_kept_two, e_g1)
    g_second_low = g_sum.astype(BF16)
    w_e_down = mm_rows(e_active, g_second_low)
    ge_hidden = (mm_back(g_second_low, e_down) * gelu_slope(e_hidden)).astype(BF16)
    w_e_up = mm_rows(e_first_low, ge_hidden)
    g_first = g_sum + mm_back(ge_hidden, e_up)
    ge_resid, e_gain_one, e_shift_one = norm_back(g_first, e_kept_one, e_g0)
    ge_branch = ge_resid.astype(BF16)
    w_e_out = mm_rows(e_mixed, ge_branch)
    ge_mixed = mm_back(ge_branch, e_out).astype(BF16)
    ge_attended = to_heads(ge_mixed, parts, micro)
    (ge_joined,) = attend_back(
        e_joined, [], *src_info, e_logs, ge_attended, heads, False, BF16
    )
    ge_joined = ge_joined.reshape(parts * micro * src_rows, -1)
    w_e_qkv = mm_rows(source_all.reshape(-1, D), ge_joined)
    g_source_all = mm_back(ge_joined, e_qkv_here).astype(BF16)

    *g_back, ge_joined = lax.optimization_barrier((*g_back, ge_joined))
    width = heads * 128
    g_pairs_own = g_own[..., :width] + sum(g.astype(F32) for g in g_back)
    g_joined = jnp.concatenate([g_pairs_own.astype(BF16), g_own[..., width:].astype(BF16)], axis=-1)
    g_joined = g_joined.reshape(parts * micro * tgt_rows, -1)
    w_d_qkv = mm_rows(target_all.reshape(-1, D), g_joined)
    g_target_all = mm_back(g_joined, d_qkv_here).astype(BF16)

    def pieces(value):
        return value.astype(BF16).reshape(devices, value.shape[0] // devices, value.shape[1])

    ends = [0]
    for part in decoder_grads:
        ends.append(ends[-1] + part.shape[1])
    decoder_sums = [decoder_sums[:, start:end].astype(F32) for start, end in zip(ends, ends[1:])]
    decoder_sums[4] = decoder_sums[4].reshape(-1, FF // D, D).transpose(1, 0, 2).reshape(-1, D)
    small_grads = pack_small(
        [
            all_columns(row_sum(ge_joined), parts),
            row_sum(ge_hidden),
            all_columns(row_sum(g_joined), parts),
            row_sum(g_hidden),
            row_sum(g_pairs),
            row_sum(ge_branch),
            e_gain_one,
            e_shift_one,
            row_sum(g_second_low),
            e_gain_two,
            e_shift_two,
            row_sum(g_branch),
            d_gain_one,
            d_shift_one,
            row_sum(g_queries),
            row_sum(g_branch_cross),
            d_gain_two,
            d_shift_two,
            row_sum(g_third),
            d_gain_three,
            d_shift_three,
        ],
        devices,
        heads,
    )
    encoder_sums = scatter(
        [
            pieces(all_columns(w_e_qkv.astype(BF16), parts)),
            pieces(w_e_out),
            pieces(w_e_up),
            pieces(w_e_down),
            small_grads,
            pieces(all_columns(w_d_qkv.astype(BF16), parts)),
            pieces(w_d_out),
        ],
        "xyyxxyx",
        7,
        F32,
        [v.reshape(parts, -1, D) for v in (g_source_all, g_target_all)],
    )
    g_source, g_target = ge_resid + encoder_sums[7], g_resid + encoder_sums[8]
    small_sums = encoder_sums[4][:, : encoder_gains.shape[1]]
    return (
        decoded.reshape(micro, tgt_rows, D),
        g_source.reshape(micro, src_rows, D),
        g_target.reshape(micro, tgt_rows, D),
        by_head(encoder_sums[0], parts),
        *encoder_sums[1:4],
        small_sums[0:2],
        small_sums[2:12],
        by_head(encoder_sums[5], parts),
        encoder_sums[6],
        *decoder_sums,
        small_sums[12:15],
        small_sums[15:SMALL_ROWS],
    )


def solution(mesh):
    in_specs = (
        P(None, ("seq", "head"), None),
        P(None, ("seq", "head"), None),
        P(None, ("seq", "head"), None),
        P(),
        P(),
        P(),
        P(("seq", "head"), None),
        P(("seq", "head"), None),
        P(("seq", "head"), None),
        P(("seq", "head"), None),
        P(None, ("seq", "head")),
        P(None, ("seq", "head")),
        P(("seq", "head"), None),
        P(("seq", "head"), None),
        P(("seq", "head"), None),
        P(("seq", "head"), None),
        P(("seq", "head"), None),
        P(("seq", "head"), None),
        P(("seq", "head"), None),
        P(None, ("seq", "head")),
        P(None, ("seq", "head")),
    )
    out_specs = (
        P(None, ("seq", "head"), None),
        P(None, ("seq", "head"), None),
        P(None, ("seq", "head"), None),
        P(("seq", "head"), None),
        P(("seq", "head"), None),
        P(("seq", "head"), None),
        P(("seq", "head"), None),
        P(None, ("seq", "head")),
        P(None, ("seq", "head")),
        P(("seq", "head"), None),
        P(("seq", "head"), None),
        P(("seq", "head"), None),
        P(("seq", "head"), None),
        P(("seq", "head"), None),
        P(("seq", "head"), None),
        P(("seq", "head"), None),
        P(None, ("seq", "head")),
        P(None, ("seq", "head")),
    )
    return jax.shard_map(shards, mesh=mesh, in_specs=in_specs, out_specs=out_specs, check_vma=False)
```

```python
import functools

import jax
import jax.numpy as jnp
from jax import lax
from jax.experimental import pallas as pl
from jax.experimental.pallas import tpu as pltpu
from jax.sharding import PartitionSpec as P

D = 768
HEADS = 12
HEAD_DIM = 64
FF = 3072
MICRO = 2
STRETCH = 1024
REACH = 2
EVERY = ("seq", "head")

EPSILON = 1e-05
NEGATIVE = -1e30
MESH = pl.DeviceIdType.MESH
F32 = jnp.float32
BF16 = jnp.bfloat16


def place():
    seq, head = lax.axis_index("seq"), lax.axis_index("head")
    return seq // 2, seq % 2, head // 2, head % 2


def device(z, y, x, c):
    return (z * 2 + y, x * 2 + c)


def shard(z, y, x, c):
    return ((z * 2 + y) * 2 + x) * 2 + c


def greet(z, y, x, c, ahead=False):
    barrier = pltpu.get_barrier_semaphore()
    def tell(who):
        pl.semaphore_signal(barrier, inc=1, device_id=who, device_id_type=MESH)
    tell(device(z, y, x, 1 - c))
    tell(device(z, y, 1 - x, c))
    tell(device(z, 1 - y, x, c))
    @pl.when(z > 0)
    def _():
        tell(device(z - 1, y, x, c))
    @pl.when(z < 3)
    def _():
        tell(device(z + 1, y, x, c))
    if ahead:

        @pl.when((y == 1) & (z < 3))
        def _():
            tell(device(z + 1, 0, x, c))

        @pl.when((y == 0) & (z > 0))
        def _():
            tell(device(z - 1, 1, x, c))

    below, above = (z + 2) // 3, (5 - z) // 3
    count = 3 + below + above
    if ahead:
        count = count + y * above + (1 - y) * below
    pl.semaphore_wait(barrier, count)


def gather_kernel(count, shared, reach, orders, *refs):
    every = count + shared
    ins, outs, refs = refs[:every], refs[every : 2 * every + reach], refs[2 * every + reach :]
    own_sem, recv_sem, send_sem, group_recv, group_send, ahead_send = refs
    z, y, x, c = place()
    greet(z, y, x, c, reach > 0)
    here = [(x, y) if order in "xX" else (y, x) for order in orders]

    def shard_of(a, zo, f, l):
        return shard(zo, l, f, c) if orders[a] in "xX" else shard(zo, f, l, c)

    def holder(a, zo, f, l, cc):
        return device(zo, l, f, cc) if orders[a] in "xX" else device(zo, f, l, cc)

    def copy(a, src, where, who, kind):
        return pltpu.make_async_remote_copy(
            src_ref=src,
            dst_ref=outs[a].at[where],
            send_sem=send_sem.at[a, kind, where // 2],
            recv_sem=recv_sem.at[a, where],
            device_id=who,
            device_id_type=MESH,
        )

    def forward(a, src, where, first, up, down):
        f, l = here[a]
        if first:
            copy(a, src, where, holder(a, z, 1 - f, l, c), 0).start()
        if up:

            @pl.when(z < 3)
            def _():
                copy(a, src, where, holder(a, z + 1, f, l, c), 1).start()

        if down:

            @pl.when(z > 0)
            def _():
                copy(a, src, where, holder(a, z - 1, f, l, c), 2).start()

        copy(a, src, where, holder(a, z, f, 1 - l, c), 3).start()
        copy(a, src, where, holder(a, z, f, l, 1 - c), 4).start()

    def arrived(a, where):
        copy(a, outs[a].at[where], where, device(z, y, x, 1 - c), 0).wait_recv()

    def pass_on(a, zo, fo, first, up, down):
        where = shard_of(a, zo, fo, here[a][1])
        arrived(a, where)
        forward(a, outs[a].at[where], where, first, up, down)

    def from_last(zo, other):
        for a in range(count):
            f, l = here[a]
            where = shard_of(a, zo, 1 - f if other else f, 1 - l)
            arrived(a, where)
            copy(a, outs[a].at[where], where, holder(a, z, f, l, 1 - c), 4).start()

    def group_copy(b, src, xo, co, kind, who):
        return pltpu.make_async_remote_copy(
            src_ref=src,
            dst_ref=outs[count + b].at[xo * 2 + co],
            send_sem=group_send.at[b, kind],
            recv_sem=group_recv.at[b, xo * 2 + co],
            device_id=who,
            device_id_type=MESH,
        )

    over, beside = device(z, y, 1 - x, c), device(z, y, x, 1 - c)
    seq = z * 2 + y

    def ahead_copy(by):
        return pltpu.make_async_remote_copy(
            src_ref=ins[every - 1],
            dst_ref=outs[every + by - 1].at[x * 2 + c],
            send_sem=ahead_send.at[by - 1],
            recv_sem=group_recv.at[shared + by - 1, x * 2 + c],
            device_id=(seq + by, x * 2 + c),
            device_id_type=MESH,
        )

    def spread(b, source):
        group_copy(b, source, x, c, 0, over).start()
        group_copy(b, source, x, c, 1, beside).start()

    def spread_on(b):
        landed = outs[count + b].at[(1 - x) * 2 + c]
        group_copy(b, landed, 1 - x, c, 2, beside).wait_recv()
        group_copy(b, landed, 1 - x, c, 2, beside).start()

    def spread_done(b, source):
        landed = outs[count + b].at[(1 - x) * 2 + c]
        group_copy(b, source, x, 1 - c, 1, beside).wait_recv()
        group_copy(b, source, 1 - x, 1 - c, 1, beside).wait_recv()
        group_copy(b, source, x, c, 0, over).wait_send()
        group_copy(b, source, x, c, 1, beside).wait_send()
        group_copy(b, landed, 1 - x, c, 2, beside).wait_send()

    for by in range(1, reach + 1):

        @pl.when(seq + by <= 7)
        def _():
            ahead_copy(by).start()

    kept = []
    for b in range(shared):
        spread(b, ins[count + b])
        kept.append(
            pltpu.make_async_copy(
                ins[count + b], outs[count + b].at[x * 2 + c], own_sem.at[count + b]
            )
        )
        kept[-1].start()
    for a in range(count):
        me = shard_of(a, z, *here[a])
        forward(a, ins[a], me, True, True, True)
        kept.append(pltpu.make_async_copy(ins[a], outs[a].at[me], own_sem.at[a]))
        kept[-1].start()
    for a in range(count):
        early = orders[a] in "XY"
        pass_on(a, z, 1 - here[a][0], False, not early, not early)
    from_last(z, False)
    from_last(z, True)
    for b in range(shared):
        spread_on(b)
    for by in range(1, reach + 1):

        @pl.when(seq >= by)
        def _():
            ahead_copy(by).wait_recv()
            spread(shared + by - 1, outs[every + by - 1].at[x * 2 + c])

    for distance in (1, 2, 3):
        for below in (True, False):

            @pl.when((z >= distance) if below else (z + distance <= 3))
            def _():
                zo = z - distance if below else z + distance
                for a in range(count):
                    early = orders[a] in "XY"
                    pass_on(a, zo, here[a][0], early, below, not below)
                    if not early:
                        pass_on(a, zo, 1 - here[a][0], False, below, not below)

        for below in (True, False):

            @pl.when((z >= distance) if below else (z + distance <= 3))
            def _():
                zo = z - distance if below else z + distance
                for a in range(count):
                    if orders[a] in "XY":
                        pass_on(a, zo, 1 - here[a][0], False, False, False)
                from_last(zo, False)
                from_last(zo, True)

    def sent(a, where, kind):
        copy(a, ins[a], where, device(z, y, x, 1 - c), kind).wait_send()

    def cores(i, carry):
        for a in range(count):
            arrived(a, i * 2 + 1 - c)
            sent(a, i * 2 + c, 4)
        return carry

    lax.fori_loop(0, 16, cores, 0)
    for by in range(1, reach + 1):

        @pl.when(seq >= by)
        def _():
            spread_on(shared + by - 1)
            spread_done(shared + by - 1, outs[every + by - 1].at[x * 2 + c])

        @pl.when(seq + by <= 7)
        def _():
            ahead_copy(by).wait_send()

    for b in range(shared):
        spread_done(b, ins[count + b])
    for copied in kept:
        copied.wait()
    for a in range(count):
        f, l = here[a]
        early = orders[a] in "XY"
        if not early:
            sent(a, shard_of(a, z, f, l), 0)
        for zo in range(4):
            if early:
                sent(a, shard_of(a, zo, f, l), 0)
            for fo in range(2):
                sent(a, shard_of(a, zo, fo, l), 3)
            for fo in [f] if early else [0, 1]:

                @pl.when((zo <= z) & (z < 3))
                def _():
                    sent(a, shard_of(a, zo, fo, l), 1)

                @pl.when((zo >= z) & (z > 0))
                def _():
                    sent(a, shard_of(a, zo, fo, l), 2)


def traffic(arrays, share):
    size = sum(v.size * v.dtype.itemsize for v in arrays)
    return pl.CostEstimate(flops=0, transcendentals=0, bytes_accessed=size * share)


def gather_all(arrays, orders, collective_id, group_arrays=(), reach=0):
    count, shared = len(arrays), len(group_arrays)
    every = [*arrays, *group_arrays]
    results = [(32, v) for v in arrays] + [(4, v) for v in group_arrays]
    results += [(4, v) for v in every[-1:] * reach]
    spreads = max(shared + reach, 1)
    D = pltpu.SemaphoreType.DMA
    return pl.pallas_call(
        functools.partial(gather_kernel, count, shared, reach, orders),
        out_shape=[jax.ShapeDtypeStruct((n,) + v.shape, v.dtype) for n, v in results],
        in_specs=[pl.BlockSpec(memory_space=pl.ANY)] * len(every),
        out_specs=[pl.BlockSpec(memory_space=pl.ANY)] * len(results),
        scratch_shapes=[
            D((len(every),)),
            D((count, 32)),
            D((count, 5, 16)),
            D((spreads, 4)),
            D((spreads, 3)),
            D((max(reach, 1),)),
        ],
        compiler_params=pltpu.CompilerParams(collective_id=collective_id, has_side_effects=True),
        cost_estimate=traffic(arrays, 500),
        name="gather_all",
    )(*every)


def scatter_kernel(count, shared, orders, *refs):
    every = count + shared
    grads, outs, refs = refs[:every], refs[every : 2 * every], refs[2 * every :]
    held, mine, near, mid, right, left = [refs[k * count : (k + 1) * count] for k in range(6)]
    refs = refs[6 * count :]
    mine_sem, core_sem, near_sem, mid_sem, right_sem, left_sem, group_sem, refs = (
        *refs[:7],
        refs[7:],
    )
    group_held, group_mine, group_last = [refs[k * shared : (k + 1) * shared] for k in range(3)]
    z, y, x, c = place()
    greet(z, y, x, c)
    half = z // 2
    here = [(x, y) if order in "xX" else (y, x) for order in orders]
    late = [order in "XY" for order in orders]

    def block(a, zt, f, l):
        return (zt * 2 + l) * 2 + f if orders[a] in "xX" else (zt * 2 + f) * 2 + l

    def remote(a, src, dst, sems, slot, who):
        return pltpu.make_async_remote_copy(
            src_ref=src,
            dst_ref=dst,
            send_sem=sems.at[a, 0, slot],
            recv_sem=sems.at[a, 1, slot],
            device_id=who,
            device_id_type=MESH,
        )

    def core_copy(a, q):
        who = device(z, y, x, 1 - c)
        return remote(a, grads[a].at[q * 2 + 1 - c], held[a].at[q], core_sem, q, who)

    def mine_copy(a, q):
        return pltpu.make_async_copy(grads[a].at[q * 2 + c], mine[a].at[q], mine_sem.at[a, q])

    def along(a, first):
        flip_x = (orders[a] in "xX") == first
        return device(z, y, 1 - x, c) if flip_x else device(z, 1 - y, x, c)

    def near_copy(a, q, slot):
        return remote(a, held[a].at[q], near[a].at[slot], near_sem, slot, along(a, True))

    def mid_copy(a, q, slot):
        return remote(a, held[a].at[q], mid[a].at[slot], mid_sem, slot, along(a, False))

    def right_copy(a, q, slot):
        return remote(a, held[a].at[q], right[a].at[slot], right_sem, slot, device(z + 1, y, x, c))

    def left_copy(a, q, slot):
        return remote(a, held[a].at[q], left[a].at[slot], left_sem, slot, device(z - 1, y, x, c))

    def far(k):
        return 3 - k + half * (2 * k - 3)

    def others(k):
        down = 3 - k - (k // 2) * z
        up = k + (k // 2) * (3 - z)
        return down + half * (up - down)

    def add(a, q, *terms):
        total = held[a][q].astype(F32)
        for ref, slot in terms:
            total = total + ref[slot].astype(F32)
        held[a][q] = total.astype(BF16)

    for side in (True, False):

        def start(i, carry, side=side):
            for a in range(count):
                f = here[a][0]
                q = block(a, far(i // 2), 1 - f if side else f, i % 2)
                core_copy(a, q).start()
                mine_copy(a, q).start()
            return carry

        lax.fori_loop(0, 8, start, 0)

    def group_copy(b, kind):
        if kind < 2:
            xt = 1 - x if kind == 0 else x
            return pltpu.make_async_remote_copy(
                src_ref=grads[count + b].at[xt * 2 + 1 - c],
                dst_ref=group_held[b].at[kind],
                send_sem=group_sem.at[b, 0, kind],
                recv_sem=group_sem.at[b, 1, kind],
                device_id=device(z, y, x, 1 - c),
                device_id_type=MESH,
            )
        if kind < 4:
            xt = 1 - x if kind == 2 else x
            return pltpu.make_async_copy(
                grads[count + b].at[xt * 2 + c], group_mine[b].at[kind - 2], group_sem.at[b, 0, kind]
            )
        return pltpu.make_async_remote_copy(
            src_ref=group_held[b].at[0],
            dst_ref=group_last[b],
            send_sem=group_sem.at[b, 0, 4],
            recv_sem=group_sem.at[b, 1, 4],
            device_id=device(z, y, 1 - x, c),
            device_id_type=MESH,
        )

    def in_pieces(rows, step):
        piece = rows // 8

        def body(i, carry):
            step(pl.ds(pl.multiple_of(i * piece, piece), piece))
            return carry

        lax.fori_loop(0, 8, body, 0)

    for b in range(shared):
        for kind in range(4):
            group_copy(b, kind).start()

    def first_step(i, carry):
        zt, lt = far(i // 2), i % 2
        for a in range(count):
            q = block(a, zt, 1 - here[a][0], lt)
            core_copy(a, q).wait_recv()
            mine_copy(a, q).wait()
            add(a, q, (mine[a], q))
            near_copy(a, q, zt * 2 + lt).start()
        return carry

    lax.fori_loop(0, 8, first_step, 0)
    for b in range(shared):
        group_copy(b, 0).wait_recv()
        group_copy(b, 2).wait()

        def to_other(cut, b=b):
            total = group_held[b][0, cut, :].astype(F32) + group_mine[b][0, cut, :].astype(F32)
            group_held[b][0, cut, :] = total.astype(BF16)

        in_pieces(group_last[b].shape[0], to_other)
        group_copy(b, 4).start()

    def summed(a, zt, lt):
        q = block(a, zt, here[a][0], lt)
        core_copy(a, q).wait_recv()
        mine_copy(a, q).wait()
        near_copy(a, q, zt * 2 + lt).wait_recv()
        add(a, q, (mine[a], q), (near[a], zt * 2 + lt))
        return q

    if any(late):

        def mid_step(i, carry):
            zt = far(i)
            for a in range(count):
                if late[a]:
                    mid_copy(a, summed(a, zt, 1 - here[a][1]), zt).start()
            return carry

        lax.fori_loop(0, 4, mid_step, 0)

    def slots(a, zt, lt):
        return (zt - 1, zt) if late[a] else ((zt - 1) * 2 + lt, zt * 2 + lt)

    def along_z(a, zt, lt):
        q = summed(a, zt, lt)
        if late[a]:
            mid_copy(a, q, zt).wait_recv()
            add(a, q, (mid[a], zt))
        up, down = slots(a, zt, lt)

        @pl.when(zt > z)
        def _():
            @pl.when(z > 0)
            def _():
                right_copy(a, q, up).wait_recv()
                add(a, q, (right[a], up))

            right_copy(a, q, up).start()

        @pl.when(zt < z)
        def _():
            @pl.when(z < 3)
            def _():
                left_copy(a, q, down).wait_recv()
                add(a, q, (left[a], down))

            left_copy(a, q, down).start()

    def z_step(k, carry):
        for a in range(count):
            if late[a]:
                along_z(a, others(k), here[a][1])
            else:
                along_z(a, others(k), 0)
                along_z(a, others(k), 1)
        return carry

    lax.fori_loop(0, 3, z_step, 0)

    def from_z(a, q, lt):
        up, down = slots(a, z, lt)

        @pl.when(z > 0)
        def _():
            right_copy(a, q, up).wait_recv()
            add(a, q, (right[a], up))

        @pl.when(z < 3)
        def _():
            left_copy(a, q, down).wait_recv()
            add(a, q, (left[a], down))

    for a in range(count):
        if not late[a]:
            lt = 1 - here[a][1]
            q = summed(a, z, lt)
            from_z(a, q, lt)
            mid_copy(a, q, 0).start()
    for a in range(count):
        lt = here[a][1]
        q = summed(a, z, lt)
        if late[a]:
            mid_copy(a, q, z).wait_recv()
            add(a, q, (mid[a], z))
        from_z(a, q, lt)
    for a in range(count):
        q = block(a, z, *here[a])
        total = held[a][q].astype(F32)
        if not late[a]:
            mid_copy(a, q, 0).wait_recv()
            total = total + mid[a][0].astype(F32)
        outs[a][...] = total.astype(outs[a].dtype)

    for b in range(shared):
        group_copy(b, 1).wait_recv()
        group_copy(b, 3).wait()
        group_copy(b, 4).wait_recv()

        def at_home(cut, b=b):
            total = group_held[b][1, cut, :].astype(F32) + group_mine[b][1, cut, :].astype(F32)
            outs[count + b][cut, :] = total + group_last[b][cut, :].astype(F32)

        in_pieces(group_last[b].shape[0], at_home)
        for kind in (0, 1, 4):
            group_copy(b, kind).wait_send()

    def sent_core(i, carry):
        for a in range(count):
            core_copy(a, i).wait_send()
        return carry

    lax.fori_loop(0, 16, sent_core, 0)

    def sent_near(i, carry):
        for a in range(count):
            near_copy(a, block(a, i // 2, 1 - here[a][0], i % 2), i).wait_send()
        return carry

    lax.fori_loop(0, 8, sent_near, 0)

    def sent_z(k, carry):
        zt = others(k)
        for a in range(count):
            for lt in [here[a][1]] if late[a] else [0, 1]:
                q = block(a, zt, here[a][0], lt)
                up, down = slots(a, zt, lt)

                @pl.when(zt > z)
                def _():
                    right_copy(a, q, up).wait_send()

                @pl.when(zt < z)
                def _():
                    left_copy(a, q, down).wait_send()

        return carry

    lax.fori_loop(0, 3, sent_z, 0)
    for a in range(count):
        f, l = here[a]
        if late[a]:
            for zt in range(4):
                mid_copy(a, block(a, zt, f, 1 - l), zt).wait_send()
        else:
            mid_copy(a, block(a, z, f, 1 - l), 0).wait_send()


def scatter_sum(arrays, orders, collective_id, out_dtype=F32, group_arrays=()):
    count, shared = len(arrays), len(group_arrays)
    shapes = [v.shape[1:] for v in (*arrays, *group_arrays)]
    late = [order in "XY" for order in orders]
    sizes = [[16, 16, 8, 4, 3, 3] if up else [16, 16, 8, 1, 6, 6] for up in late]
    scratch = []
    for k in range(6):
        scratch += [pltpu.VMEM((size[k],) + shape, BF16) for size, shape in zip(sizes, shapes)]
    scratch += [pltpu.SemaphoreType.DMA((count, 16))]
    scratch += [pltpu.SemaphoreType.DMA((count, 2, n)) for n in (16, 8, 4, 6, 6)]
    scratch += [pltpu.SemaphoreType.DMA((max(shared, 1), 2, 5))]
    scratch += [pltpu.VMEM((2,) + shape, BF16) for shape in shapes[count:]] * 2
    scratch += [pltpu.VMEM(shape, BF16) for shape in shapes[count:]]
    return pl.pallas_call(
        functools.partial(scatter_kernel, count, shared, orders),
        out_shape=[jax.ShapeDtypeStruct(shape, out_dtype) for shape in shapes],
        in_specs=[pl.BlockSpec(memory_space=pl.ANY)] * len(shapes),
        out_specs=[pl.BlockSpec(memory_space=pltpu.VMEM)] * len(shapes),
        scratch_shapes=scratch,
        compiler_params=pltpu.CompilerParams(
            collective_id=collective_id, has_side_effects=True, vmem_limit_bytes=60 << 20
        ),
        cost_estimate=traffic(arrays, 1),
        name="scatter_sum",
    )(*arrays, *group_arrays)


def known_mesh():
    return lax.axis_size("seq") == 8 and lax.axis_size("head") == 4


def gather(arrays, orders, collective_id, group_arrays=(), reach=0):
    if known_mesh():
        return gather_all(arrays, orders, collective_id, group_arrays, reach)
    every = [lax.all_gather(v, EVERY, axis=0, tiled=False) for v in arrays]
    group = [lax.all_gather(v, "head", axis=0, tiled=False) for v in group_arrays]
    return every + group + [from_before(group[-1], by) for by in range(1, reach + 1)]


def scatter(arrays, orders, collective_id, out_dtype=F32, group_arrays=()):
    if known_mesh():
        return scatter_sum(arrays, orders, collective_id, out_dtype, group_arrays)
    return [
        lax.psum_scatter(v, axes, scatter_dimension=0, tiled=False).astype(out_dtype)
        for v, axes in [(v, EVERY) for v in arrays] + [(v, "head") for v in group_arrays]
    ]


def fill(target, refs, columns, scale=None):
    at = 0
    for ref in refs:
        rows = ref.shape[2]
        for p in range(ref.shape[0]):
            piece = ref[p, 0, :, columns]
            target[at : at + rows] = piece if scale is None else piece * scale
            at += rows


def spill(value, refs, columns):
    at = 0
    for ref in refs:
        rows = ref.shape[2]
        for p in range(ref.shape[0]):
            ref[p, 0, :, columns] = value[at : at + rows].astype(ref.dtype)
            at += rows


def across(left, right):
    return lax.dot_general(left, right, (((1,), (1,)), ((), ())), preferred_element_type=F32)


def down(left, right):
    return lax.dot_general(left, right, (((0,), (0,)), ((), ())), preferred_element_type=F32)


def soft_columns(scores):
    peak = jnp.max(scores, axis=0, keepdims=True)
    weights = jnp.exp(scores - peak)
    total = jnp.sum(weights, axis=0, keepdims=True)
    return weights * (1.0 / total), peak + jnp.log(total)


def score_grads(probs, grad_probs):
    delta = jnp.sum(probs * grad_probs, axis=0, keepdims=True)
    return (probs * (grad_probs - delta)).astype(BF16)


def allowed_pairs(key_ref, query_ref, start, tile, causal):
    doc_key, doc_query = key_ref[0, :, 0:1], query_ref[0, 0:1, pl.ds(start, tile)]
    allowed = doc_key == doc_query
    if causal:
        allowed &= key_ref[0, :, 1:2] <= query_ref[0, 1:2, pl.ds(start, tile)]
    return allowed


def attend_kernel(heads, tile, causal, *refs):
    key_ref, query_ref, own_ref = refs[:3]
    prior = refs[3:-6]
    out_ref, log_ref, key_s, value_s, query_s, result_s = refs[-6:]
    group = query_s.shape[0]
    for h in range(heads):
        fill(key_s, (*prior, own_ref), slice(h * 128, h * 128 + 64))
        fill(value_s, (*prior, own_ref), slice(h * 128 + 64, h * 128 + 128))
        at = heads * 128 + h * 64
        fill(query_s, (own_ref,), slice(at, at + 64), 0.125)
        values = value_s[...].T

        def step(i, carry):
            start = pl.multiple_of(i * tile, tile)
            allowed = allowed_pairs(key_ref, query_ref, start, tile, causal)
            scores = across(key_s[...], query_s[pl.ds(start, tile), :])
            probs, log_total = soft_columns(jnp.where(allowed, scores, NEGATIVE))
            made = jnp.dot(values, probs.astype(BF16), preferred_element_type=F32)
            result_s[pl.ds(start, tile), :] = made.astype(BF16).T
            log_ref[0, h : h + 1, pl.ds(start, tile)] = log_total
            return carry

        lax.fori_loop(0, group // tile, step, 0)
        spill(result_s[...], (out_ref,), slice(h * 64, h * 64 + 64))


def rows_spec(shape):
    return pl.BlockSpec((shape[0], 1) + shape[2:], lambda m: (0, m, 0, 0))


def whole_spec(shape):
    return pl.BlockSpec((1,) + shape[1:], lambda m: (m, 0, 0))


def attend(joined, prior, key_info, query_info, heads, causal, tile=256):
    parts, micro, rows, _ = joined.shape
    group = parts * rows
    keys = key_info.shape[1]
    out, logs = (parts, micro, rows, heads * 64), (micro, heads, group)
    return pl.pallas_call(
        functools.partial(attend_kernel, heads, tile, causal),
        grid=(micro,),
        out_shape=[jax.ShapeDtypeStruct(out, BF16), jax.ShapeDtypeStruct(logs, F32)],
        in_specs=[whole_spec(key_info.shape), whole_spec(query_info.shape), rows_spec(joined.shape)]
        + [rows_spec(p.shape) for p in prior],
        out_specs=[rows_spec(out), whole_spec(logs)],
        scratch_shapes=[
            pltpu.VMEM((keys, 64), BF16),
            pltpu.VMEM((keys, 64), BF16),
            pltpu.VMEM((group, 64), BF16),
            pltpu.VMEM((group, 64), BF16),
        ],
        compiler_params=pltpu.CompilerParams(vmem_limit_bytes=48 << 20),
        cost_estimate=pl.CostEstimate(
            flops=16 * micro * heads * group * keys * 128,
            transcendentals=micro * heads * group * keys,
            bytes_accessed=joined.size * 4,
        ),
        name="attend",
    )(key_info, query_info, joined, *prior)


def attend_back_kernel(heads, tile, causal, count, *refs):
    key_ref, query_ref, own_ref, log_ref, grad_ref = refs[:5]
    prior = refs[5 : 5 + count]
    out_ref, *prior_out = refs[5 + count : 6 + 2 * count]
    key_s, value_s, query_s, grad_s, gk_s, gv_s, result_s = refs[6 + 2 * count :]
    group = query_s.shape[0]
    for h in range(heads):
        key_cut, value_cut = slice(h * 128, h * 128 + 64), slice(h * 128 + 64, h * 128 + 128)
        fill(key_s, (*prior, own_ref), key_cut)
        fill(value_s, (*prior, own_ref), value_cut)
        query_cut = slice(heads * 128 + h * 64, heads * 128 + h * 64 + 64)
        fill(query_s, (own_ref,), query_cut, 0.125)
        fill(grad_s, (grad_ref,), slice(h * 64, h * 64 + 64))
        gk_s[...] = jnp.zeros_like(gk_s)
        gv_s[...] = jnp.zeros_like(gv_s)
        keys = key_s[...].T

        def step(i, carry):
            start = pl.multiple_of(i * tile, tile)
            here = pl.ds(start, tile)
            allowed = allowed_pairs(key_ref, query_ref, start, tile, causal)
            query, grad_out = query_s[here, :], grad_s[here, :]
            scores = jnp.where(allowed, across(key_s[...], query), NEGATIVE)
            probs = jnp.exp(scores - log_ref[0, h : h + 1, here])
            grad_scores = score_grads(probs, across(value_s[...], grad_out))
            gv_s[...] += jnp.dot(probs.astype(BF16), grad_out, preferred_element_type=F32)
            gk_s[...] += jnp.dot(grad_scores, query, preferred_element_type=F32)
            made = jnp.dot(keys, grad_scores, preferred_element_type=F32)
            result_s[here, :] = made.T * 0.125
            return carry

        lax.fori_loop(0, group // tile, step, 0)
        spill(result_s[...], (out_ref,), query_cut)
        spill(gk_s[...], (*prior_out, out_ref), key_cut)
        spill(gv_s[...], (*prior_out, out_ref), value_cut)
    for p in range(out_ref.shape[0]):
        out_ref[p, 0, :, heads * 192 :] = jnp.zeros(
            (out_ref.shape[2], out_ref.shape[3] - heads * 192), out_ref.dtype
        )


def attend_back(
    joined, prior, key_info, query_info, logs, grad, heads, causal, out_dtype, tile=256
):
    parts, micro, rows, _ = joined.shape
    group = parts * rows
    keys = key_info.shape[1]
    return pl.pallas_call(
        functools.partial(attend_back_kernel, heads, tile, causal, len(prior)),
        grid=(micro,),
        out_shape=[jax.ShapeDtypeStruct(joined.shape, out_dtype)]
        + [jax.ShapeDtypeStruct(p.shape, BF16) for p in prior],
        in_specs=[
            whole_spec(key_info.shape),
            whole_spec(query_info.shape),
            rows_spec(joined.shape),
            whole_spec(logs.shape),
            rows_spec(grad.shape),
        ]
        + [rows_spec(p.shape) for p in prior],
        out_specs=[rows_spec(joined.shape)] + [rows_spec(p.shape) for p in prior],
        scratch_shapes=[
            pltpu.VMEM((keys, 64), BF16),
            pltpu.VMEM((keys, 64), BF16),
            pltpu.VMEM((group, 64), BF16),
            pltpu.VMEM((group, 64), BF16),
            pltpu.VMEM((keys, 64), F32),
            pltpu.VMEM((keys, 64), F32),
            pltpu.VMEM((group, 64), F32),
        ],
        compiler_params=pltpu.CompilerParams(vmem_limit_bytes=48 << 20),
        cost_estimate=pl.CostEstimate(
            flops=24 * micro * heads * group * keys * 128,
            transcendentals=micro * heads * group * keys,
            bytes_accessed=joined.size * 6,
        ),
        name="attend_back",
    )(key_info, query_info, joined, logs, grad, *prior)


def cross_kernel(query_ref, pairs_ref, out_ref, log_ref):
    for i in range(D // 128):
        outs = []
        for h in range(2):
            at = i * 128 + h * 64
            query, keys = query_ref[0, :, at : at + 64] * 0.125, pairs_ref[0, :, at : at + 64]
            values = pairs_ref[0, :, D + at : D + at + 64]
            probs, log_total = soft_columns(across(keys, query))
            outs.append(down(probs.astype(BF16), values))
            log_ref[0, i * 2 + h : i * 2 + h + 1, :] = log_total
        out_ref[0, :, i * 128 : i * 128 + 128] = jnp.concatenate(outs, axis=1).astype(BF16)


def cross(query, pairs):
    micro, rows, _ = query.shape
    keys = pairs.shape[1]
    logs = (micro, HEADS, rows)
    return pl.pallas_call(
        cross_kernel,
        grid=(micro,),
        out_shape=[jax.ShapeDtypeStruct(query.shape, BF16), jax.ShapeDtypeStruct(logs, F32)],
        in_specs=[whole_spec(query.shape), whole_spec(pairs.shape)],
        out_specs=[whole_spec(query.shape), whole_spec(logs)],
        compiler_params=pltpu.CompilerParams(vmem_limit_bytes=48 << 20),
        cost_estimate=pl.CostEstimate(
            flops=16 * micro * HEADS * rows * keys * 128,
            transcendentals=micro * HEADS * rows * keys,
            bytes_accessed=pairs.size * 2,
        ),
        name="cross",
    )(query, pairs)


def cross_back_kernel(
    query_ref, pairs_ref, log_ref, grad_ref, grad_query_ref, grad_pairs_ref
):
    for i in range(D // 128):
        query_parts, key_parts, value_parts = [], [], []
        for h in range(2):
            at = i * 128 + h * 64
            cut = slice(at, at + 64)
            query, keys = query_ref[0, :, cut] * 0.125, pairs_ref[0, :, cut]
            values, grad_out = pairs_ref[0, :, D + at : D + at + 64], grad_ref[0, :, cut]
            probs = jnp.exp(across(keys, query) - log_ref[0, i * 2 + h : i * 2 + h + 1, :])
            grad_scores = score_grads(probs, across(values, grad_out))
            value_parts.append(jnp.dot(probs.astype(BF16), grad_out, preferred_element_type=F32))
            key_parts.append(jnp.dot(grad_scores, query, preferred_element_type=F32))
            query_parts.append(jnp.dot(keys.T, grad_scores, preferred_element_type=F32))
        cut = slice(i * 128, i * 128 + 128)
        made = jnp.concatenate(query_parts, axis=0).T * 0.125
        grad_query_ref[0, :, cut] = made.astype(BF16)
        grad_pairs_ref[0, :, cut] = jnp.concatenate(key_parts, axis=1).astype(BF16)
        cut = slice(D + i * 128, D + i * 128 + 128)
        grad_pairs_ref[0, :, cut] = jnp.concatenate(value_parts, axis=1).astype(BF16)


def cross_back(query, pairs, logs, grad):
    micro, rows, _ = query.shape
    keys = pairs.shape[1]
    return pl.pallas_call(
        cross_back_kernel,
        grid=(micro,),
        out_shape=[jax.ShapeDtypeStruct(query.shape, BF16), jax.ShapeDtypeStruct(pairs.shape, BF16)],
        in_specs=[whole_spec(v.shape) for v in (query, pairs, logs, grad)],
        out_specs=[whole_spec(query.shape), whole_spec(pairs.shape)],
        compiler_params=pltpu.CompilerParams(vmem_limit_bytes=48 << 20),
        cost_estimate=pl.CostEstimate(
            flops=24 * micro * HEADS * rows * keys * 128,
            transcendentals=micro * HEADS * rows * keys,
            bytes_accessed=pairs.size * 4,
        ),
        name="cross_back",
    )(query, pairs, logs, grad)


SMALL_ROWS = 29
SINGLES = (4, 0, 5, 10, 1, 11, 17, 12, 18, 19, 21, 13, 22, 27, 14, 28)


def head_places(head, heads):
    base = head // heads * joined_width(heads) + head % heads * 64
    return base + head % heads * 64 + 64, base + heads * 128


def joined_width(heads):
    return (heads * 192 + 127) // 128 * 128


def unpack_kernel(width, heads, pack_ref, *refs):
    e_joined, e_hidden, d_joined, d_hidden, pair_bias = refs[:5]
    singles, full = refs[5:-1], refs[-1]
    for d in range(pack_ref.shape[0]):
        full[:, d * width : d * width + width] = pack_ref[d, :, 0:width].astype(F32)
    for target, row in ((e_joined, 2), (d_joined, 15)):
        target[...] = jnp.zeros_like(target)
        for head in range(HEADS):
            value_at, query_at = head_places(head, heads)
            cut = slice(head * 64, head * 64 + 64)
            target[:, query_at : query_at + 64] = full[row : row + 1, cut]
            target[:, value_at : value_at + 64] = full[row + 1 : row + 2, cut]
    for target, row in ((e_hidden, 6), (d_hidden, 23)):
        for k in range(FF // D):
            target[:, k * D : k * D + D] = full[row + k : row + k + 1, :]
    pair_bias[:, 0:D] = jnp.zeros((1, D), F32)
    pair_bias[:, D:] = full[20:21, :]
    for target, row in zip(singles, SINGLES):
        target[...] = full[row : row + 1, :]


def unpack_small(packs, heads):
    devices = packs.shape[0]
    joined = joined_width(heads) * (HEADS // heads)
    widths = [joined, FF, joined, FF, 2 * D] + [D] * len(SINGLES)
    return pl.pallas_call(
        functools.partial(unpack_kernel, D // devices, heads),
        out_shape=[jax.ShapeDtypeStruct((1, w), F32) for w in widths],
        scratch_shapes=[pltpu.VMEM((32, D), F32)],
        name="unpack_small",
    )(packs)


def pack_kernel(width, heads, count, *refs):
    e_joined, e_hidden, d_joined, d_hidden, pair_sum = refs[:5]
    singles, out_ref, full = refs[5 : 5 + count], refs[-2], refs[-1]
    full[...] = jnp.zeros_like(full)
    for source, row in ((e_joined, 2), (d_joined, 15)):
        for head in range(HEADS):
            value_at, query_at = head_places(head, heads)
            cut = slice(head * 64, head * 64 + 64)
            full[row : row + 1, cut] = source[:, query_at : query_at + 64]
            full[row + 1 : row + 2, cut] = source[:, value_at : value_at + 64]
    for source, row in ((e_hidden, 6), (d_hidden, 23)):
        for k in range(FF // D):
            full[row + k : row + k + 1, :] = source[k * D : k * D + D].reshape(1, D)
    full[20:21, :] = pair_sum[D:].reshape(1, D)
    for source, row in zip(singles, SINGLES):
        full[row : row + 1, :] = source[...].reshape(1, D)
    out_ref[...] = jnp.zeros_like(out_ref)
    for d in range(out_ref.shape[0]):
        out_ref[d, :, 0:width] = full[:, d * width : d * width + width].astype(BF16)


def pack_small(vectors, devices, heads):
    return pl.pallas_call(
        functools.partial(pack_kernel, D // devices, heads, len(SINGLES)),
        out_shape=jax.ShapeDtypeStruct((devices, 32, 128), BF16),
        scratch_shapes=[pltpu.VMEM((32, D), F32)],
        name="pack_small",
    )(*vectors)


def finish_kernel(heads, *refs):
    late, pack, outs = refs[:7], refs[7], refs[8:]
    for k in (0, 4):
        for head in range(HEADS):
            value_at, query_at = head_places(head, heads)
            for n, at in enumerate((query_at, value_at - 64, value_at)):
                start = head * 192 + n * 64
                outs[k][:, start : start + 64] = late[k][:, at : at + 64]
    for k in (1, 2, 3, 5, 6):
        outs[k][...] = late[k][...]
    at = 0
    for target in outs[7:]:
        width = target.shape[1]
        target[...] = pack[:, at : at + width].astype(F32)
        at += width


def finish(late, early, heads):
    rows = late[0].shape[0]
    shapes = [v.shape for v in late]
    shapes[0] = shapes[4] = (rows, 3 * D)
    shapes += [(rows, width) for width in (D, 2 * D, D, FF, FF)]
    return pl.pallas_call(
        functools.partial(finish_kernel, heads),
        out_shape=[jax.ShapeDtypeStruct(shape, F32) for shape in shapes],
        compiler_params=pltpu.CompilerParams(vmem_limit_bytes=48 << 20),
        name="finish",
    )(*late, early)


def norm(resid, gain, shift):
    center = resid - jnp.mean(resid, axis=-1, keepdims=True)
    scale = lax.rsqrt(jnp.mean(center * center, axis=-1, keepdims=True) + EPSILON)
    hat = center * scale
    return hat * gain + shift, (hat, scale)


def norm_back(grad, kept, gain):
    hat, scale = kept
    inner = grad * gain
    grad_resid = scale * (
        inner
        - jnp.mean(inner, axis=-1, keepdims=True)
        - hat * jnp.mean(inner * hat, axis=-1, keepdims=True)
    )
    return grad_resid, jnp.sum(grad * hat, axis=0), jnp.sum(grad, axis=0)


def gelu(value):
    return value * (1.0 + lax.erf(value * 0.7071067811865476)) * 0.5


def gelu_slope(value):
    bell = jnp.exp(value * value * -0.5) * 0.3989422804014327
    return 0.5 * (1.0 + lax.erf(value * 0.7071067811865476)) + value * bell


def mm(left, right):
    return jnp.dot(left, right, preferred_element_type=F32)


def mm_rows(left, right):
    return lax.dot_general(left, right, (((0,), (0,)), ((), ())), preferred_element_type=F32)


def mm_back(left, right):
    return lax.dot_general(left, right, (((1,), (1,)), ((), ())), preferred_element_type=F32)


def row_sum(value):
    return jnp.sum(value.astype(F32), axis=0)


def doc_starts(lengths):
    count = lengths.shape[1]
    before = jnp.arange(count)[None, :] < jnp.arange(count)[:, None]
    return jnp.sum(jnp.where(before[None], lengths[:, None, :], 0), axis=2)


def doc_ids(starts, positions):
    return jnp.sum((starts[:, None, :] <= positions[None, :, None]).astype(jnp.int32), axis=2) - 1


def key_and_query_info(starts, key_pos, query_pos):
    key_docs, query_docs = doc_ids(starts, key_pos), doc_ids(starts, query_pos)
    micro = starts.shape[0]
    key_info = jnp.stack(
        [key_docs, jnp.broadcast_to(key_pos, (micro,) + key_pos.shape)], axis=2
    )
    query_info = jnp.stack(
        [query_docs, jnp.broadcast_to(query_pos, (micro,) + query_pos.shape)], axis=1
    )
    return key_info, query_info


def by_group(weight, parts):
    rows = weight.shape[0]
    split = weight.reshape(rows, parts, HEADS // parts, 3, HEAD_DIM)
    pairs = split[:, :, :, 1:].reshape(rows, parts, -1)
    query = split[:, :, :, 0].reshape(rows, parts, -1)
    width = joined_width(HEADS // parts)
    blank = jnp.zeros((rows, parts, width - pairs.shape[2] - query.shape[2]), weight.dtype)
    return jnp.concatenate([pairs, query, blank], axis=2).reshape(rows, parts * width)


def by_head(grad, parts):
    rows, heads = grad.shape[0], HEADS // parts
    split = grad.reshape(rows, parts, -1)
    pairs = split[:, :, : heads * 128].reshape(rows, parts, heads, 2, HEAD_DIM)
    query = split[:, :, heads * 128 : heads * 192].reshape(rows, parts, heads, 1, HEAD_DIM)
    return jnp.concatenate([query, pairs], axis=3).reshape(rows, 3 * D)


def my_columns(full, parts):
    width = full.shape[1] // parts
    return lax.dynamic_slice_in_dim(full, lax.axis_index("head") * width, width, 1)


def all_columns(mine, parts):
    rows, width = mine.shape
    full = jnp.zeros((rows, width * parts), mine.dtype)
    return lax.dynamic_update_slice_in_dim(full, mine, lax.axis_index("head") * width, 1)


def to_tokens(value):
    parts, micro, rows, columns = value.shape
    got = lax.all_to_all(value, "head", split_axis=0, concat_axis=0, tiled=True)
    return got.transpose(1, 2, 0, 3).reshape(micro * rows, parts * columns)


def to_heads(value, parts, micro):
    rows = value.shape[0] // micro
    split = value.reshape(micro, rows, parts, -1).transpose(2, 0, 1, 3)
    return lax.all_to_all(split, "head", split_axis=0, concat_axis=0, tiled=True)


def from_before(value, by):
    count = lax.axis_size("seq")
    return lax.ppermute(value, "seq", [(i, i + by) for i in range(count - by)])


def to_before(value, by):
    count = lax.axis_size("seq")
    return lax.ppermute(value, "seq", [(i + by, i) for i in range(count - by)])


def shards(
    source,
    target,
    cotangent,
    src_lengths,
    tgt_lengths,
    retrieved,
    encoder_qkv,
    encoder_out,
    encoder_up,
    encoder_down,
    encoder_gains,
    encoder_biases,
    decoder_qkv,
    decoder_out,
    cross_query,
    cross_keyvalue,
    cross_out,
    decoder_up,
    decoder_down,
    decoder_gains,
    decoder_biases,
):
    micro, src_rows, _ = source.shape
    tgt_rows = target.shape[1]
    parts = lax.axis_size("head")
    devices = parts * lax.axis_size("seq")
    seq, me = lax.axis_index("seq"), lax.axis_index(EVERY)
    src_group, tgt_group = src_rows * parts, tgt_rows * parts
    asked = retrieved.shape[1]
    source_rows = source.reshape(micro * src_rows, D)
    target_rows = target.reshape(micro * tgt_rows, D)

    heads = HEADS // parts
    small = jnp.concatenate([encoder_gains, encoder_biases, decoder_gains, decoder_biases], axis=0)
    small = jnp.pad(small, ((0, 32 - SMALL_ROWS), (0, 128 - small.shape[1])))
    encoder_full = gather(
        [by_group(encoder_qkv, parts), encoder_out, encoder_up, encoder_down, small],
        "yxxxx",
        0,
        [source, target],
        REACH,
    )
    source_all, target_all, *target_before = encoder_full[5:]
    decoder_parts = [
        by_group(decoder_qkv, parts),
        decoder_out,
        cross_query,
        cross_keyvalue,
        cross_out,
        decoder_up,
    ]
    decoder_pack, small_full = lax.optimization_barrier(
        (jnp.concatenate(decoder_parts, axis=1), encoder_full[4])
    )
    decoder_full = lax.all_gather(decoder_pack, EVERY, axis=0, tiled=True)
    d_down = lax.all_gather(decoder_down, EVERY, axis=0, tiled=True)
    e_qkv, e_out, e_up, e_down = [v.reshape(-1, v.shape[-1]) for v in encoder_full[:4]]
    e_bias, e_hidden_bias, d_bias, d_hidden_bias, pair_bias, *singles = unpack_small(
        small_full, heads
    )
    e_b2, e_g0, e_b3, e_b8, e_g1, e_b9 = singles[:6]
    d_b2, d_g0, d_b3, d_b4, d_b6, d_g1, d_b7, d_b12, d_g2, d_b13 = singles[6:]

    src_pos = seq * src_group + jnp.arange(src_group, dtype=jnp.int32)
    src_info = key_and_query_info(doc_starts(src_lengths), src_pos, src_pos)
    tgt_pos = seq * tgt_group + jnp.arange(tgt_group, dtype=jnp.int32)
    tgt_key_pos = (seq - REACH) * tgt_group + jnp.arange((REACH + 1) * tgt_group, dtype=jnp.int32)
    tgt_info = key_and_query_info(doc_starts(tgt_lengths), tgt_key_pos, tgt_pos)

    e_qkv_here = my_columns(e_qkv, parts)
    e_joined = (mm(source_all.reshape(-1, D), e_qkv_here) + my_columns(e_bias, parts)).astype(BF16)
    e_joined = e_joined.reshape(parts, micro, src_rows, -1)
    e_attended, e_logs = attend(e_joined, [], *src_info, heads, False)
    e_mixed = to_tokens(e_attended)
    e_first, e_kept_one = norm(
        source_rows.astype(F32) + mm(e_mixed, e_out) + e_b2, e_g0, e_b3
    )
    e_first_low = e_first.astype(BF16)
    e_hidden = mm(e_first_low, e_up) + e_hidden_bias
    e_active = gelu(e_hidden).astype(BF16)
    e_result, e_kept_two = norm(e_first + mm(e_active, e_down) + e_b8, e_g1, e_b9)

    src_own = me * src_rows + jnp.arange(src_rows, dtype=jnp.int32)
    select = (retrieved[:, :, None] == src_own[None, None, :]).astype(BF16)
    picked = jnp.einsum(
        "mrs,msd->mrd",
        select,
        e_result.astype(BF16).reshape(micro, src_rows, D),
        preferred_element_type=F32,
    ).astype(BF16)
    picked = [picked[m].reshape(devices, asked // devices, D) for m in range(micro)]
    fetched = gather(scatter(picked, "xy", 2, BF16), "xy", 3)
    fetched = jnp.concatenate([v.reshape(asked, D) for v in fetched], axis=0)
    decoder_full, fetched = lax.optimization_barrier((decoder_full, fetched))
    ends = [0]
    for part in decoder_parts:
        ends.append(ends[-1] + part.shape[1])
    d_qkv, d_out, c_query, c_pairs, c_out, d_up = [
        decoder_full[:, start:end] for start, end in zip(ends, ends[1:])
    ]

    d_qkv_here = my_columns(d_qkv, parts)
    d_joined = (mm(target_all.reshape(-1, D), d_qkv_here) + my_columns(d_bias, parts)).astype(BF16)
    d_joined = d_joined.reshape(parts, micro, tgt_rows, -1)
    pair_weights, pair_shift = d_qkv_here[:, : heads * 128], my_columns(d_bias, parts)[:, : heads * 128]
    d_prior = []
    for by in range(REACH, 0, -1):
        before = (mm(target_before[by - 1].reshape(-1, D), pair_weights) + pair_shift).astype(BF16)
        before = jnp.where(seq >= by, before, jnp.zeros_like(before))
        d_prior.append(before.reshape(parts, micro, tgt_rows, -1))
    d_attended, d_logs = attend(d_joined, d_prior, *tgt_info, heads, True)
    d_mixed = to_tokens(d_attended)
    d_first, d_kept_one = norm(
        target_rows.astype(F32) + mm(d_mixed, d_out) + d_b2, d_g0, d_b3
    )
    d_first_low = d_first.astype(BF16)
    queries = (mm(d_first_low, c_query) + d_b4).astype(BF16).reshape(micro, tgt_rows, D)

    pairs = (mm(fetched, c_pairs) + pair_bias).astype(BF16).reshape(micro, asked, 2 * D)

    crossed_rows, cross_logs = cross(queries, pairs)
    crossed = crossed_rows.reshape(micro * tgt_rows, D)
    d_second, d_kept_two = norm(d_first + mm(crossed, c_out) + d_b6, d_g1, d_b7)
    d_second_low = d_second.astype(BF16)
    d_hidden = mm(d_second_low, d_up) + d_hidden_bias
    d_active = gelu(d_hidden).astype(BF16)
    decoded, d_kept_three = norm(d_second + mm(d_active, d_down) + d_b12, d_g2, d_b13)

    grad = cotangent.reshape(micro * tgt_rows, D).astype(F32)
    g_sum, d_gain_three, d_shift_three = norm_back(grad, d_kept_three, d_g2)
    g_third = g_sum.astype(BF16)
    w_d_down = mm_rows(d_active, g_third)
    g_hidden = (mm_back(g_third, d_down) * gelu_slope(d_hidden)).astype(BF16)
    w_d_up = mm_rows(d_second_low, g_hidden)
    g_second = g_sum + mm_back(g_hidden, d_up)
    g_sum_two, d_gain_two, d_shift_two = norm_back(g_second, d_kept_two, d_g1)
    g_branch_cross = g_sum_two.astype(BF16)
    w_c_out = mm_rows(crossed, g_branch_cross)
    g_crossed = mm_back(g_branch_cross, c_out).astype(BF16).reshape(micro, tgt_rows, D)
    g_queries, g_pairs = cross_back(queries, pairs, cross_logs, g_crossed)
    g_queries = g_queries.reshape(micro * tgt_rows, D)
    g_pairs = g_pairs.reshape(micro * asked, 2 * D)
    g_fetched = mm_back(g_pairs, c_pairs).astype(BF16).reshape(micro, asked, D)
    g_fetched = [g_fetched[m].reshape(devices, asked // devices, D) for m in range(micro)]
    g_fetched = gather(scatter(g_fetched, "xy", 4, BF16), "xy", 5)
    w_c_pairs = mm_rows(fetched, g_pairs)
    w_c_query = mm_rows(d_first_low, g_queries)
    g_first = g_sum_two + mm_back(g_queries, c_query)
    g_resid, d_gain_one, d_shift_one = norm_back(g_first, d_kept_one, d_g0)
    g_branch = g_resid.astype(BF16)
    w_d_out = mm_rows(d_mixed, g_branch)
    g_mixed = mm_back(g_branch, d_out).astype(BF16)
    g_attended = to_heads(g_mixed, parts, micro)
    g_own, *g_prior = attend_back(
        d_joined, d_prior, *tgt_info, d_logs, g_attended, heads, True, F32
    )
    g_back = [to_before(g, by) for g, by in zip(g_prior, range(REACH, 0, -1))]

    g_result = jnp.einsum(
        "mrs,mrd->msd",
        select,
        jnp.stack([v.reshape(asked, D) for v in g_fetched]),
        preferred_element_type=F32,
    ).reshape(micro * src_rows, D)
    g_sum, e_gain_two, e_shift_two = norm_back(g_result, e_kept_two, e_g1)
    g_second_low = g_sum.astype(BF16)
    w_e_down = mm_rows(e_active, g_second_low)
    ge_hidden = (mm_back(g_second_low, e_down) * gelu_slope(e_hidden)).astype(BF16)
    w_e_up = mm_rows(e_first_low, ge_hidden)
    g_first = g_sum + mm_back(ge_hidden, e_up)
    ge_resid, e_gain_one, e_shift_one = norm_back(g_first, e_kept_one, e_g0)
    ge_branch = ge_resid.astype(BF16)
    w_e_out = mm_rows(e_mixed, ge_branch)
    early_grads = [g.astype(BF16) for g in (w_c_query, w_c_pairs, w_c_out, w_d_up, w_e_up)]
    early_pack, ge_branch = lax.optimization_barrier(
        (jnp.concatenate(early_grads, axis=1), ge_branch)
    )
    early_sums = lax.psum_scatter(early_pack, EVERY, scatter_dimension=0, tiled=True)
    ge_mixed = mm_back(ge_branch, e_out).astype(BF16)
    ge_attended = to_heads(ge_mixed, parts, micro)
    (ge_joined,) = attend_back(
        e_joined, [], *src_info, e_logs, ge_attended, heads, False, BF16
    )
    ge_joined = ge_joined.reshape(parts * micro * src_rows, -1)
    w_e_qkv = mm_rows(source_all.reshape(-1, D), ge_joined)
    g_source_all = mm_back(ge_joined, e_qkv_here).astype(BF16)

    *g_back, ge_joined = lax.optimization_barrier((*g_back, ge_joined))
    width = heads * 128
    g_pairs_own = g_own[..., :width] + sum(g.astype(F32) for g in g_back)
    g_joined = jnp.concatenate([g_pairs_own.astype(BF16), g_own[..., width:].astype(BF16)], axis=-1)
    g_joined = g_joined.reshape(parts * micro * tgt_rows, -1)
    w_d_qkv = mm_rows(target_all.reshape(-1, D), g_joined)
    g_target_all = mm_back(g_joined, d_qkv_here).astype(BF16)

    def pieces(value):
        return value.astype(BF16).reshape(devices, value.shape[0] // devices, value.shape[1])

    small_grads = pack_small(
        [
            all_columns(row_sum(ge_joined)[None], parts),
            row_sum(ge_hidden),
            all_columns(row_sum(g_joined)[None], parts),
            row_sum(g_hidden),
            row_sum(g_pairs),
            row_sum(ge_branch),
            e_gain_one,
            e_shift_one,
            row_sum(g_second_low),
            e_gain_two,
            e_shift_two,
            row_sum(g_branch),
            d_gain_one,
            d_shift_one,
            row_sum(g_queries),
            row_sum(g_branch_cross),
            d_gain_two,
            d_shift_two,
            row_sum(g_third),
            d_gain_three,
            d_shift_three,
        ],
        devices,
        heads,
    )
    late_sums = scatter(
        [
            pieces(all_columns(w_e_qkv.astype(BF16), parts)),
            pieces(w_e_out),
            pieces(w_e_down),
            small_grads,
            pieces(all_columns(w_d_qkv.astype(BF16), parts)),
            pieces(w_d_out),
            pieces(w_d_down),
        ],
        "xyxyyxy",
        7,
        F32,
        [v.reshape(parts, -1, D) for v in (g_source_all, g_target_all)],
    )
    g_source, g_target = ge_resid + late_sums[7], g_resid + late_sums[8]
    (
        e_qkv_sum,
        e_out_sum,
        e_down_sum,
        small_sums,
        d_qkv_sum,
        d_out_sum,
        d_down_sum,
        c_query_sum,
        c_pairs_sum,
        c_out_sum,
        d_up_sum,
        e_up_sum,
    ) = finish(late_sums[:7], early_sums, heads)
    small_sums = small_sums[:, : encoder_gains.shape[1]]
    return (
        decoded.reshape(micro, tgt_rows, D),
        g_source.reshape(micro, src_rows, D),
        g_target.reshape(micro, tgt_rows, D),
        e_qkv_sum,
        e_out_sum,
        e_up_sum,
        e_down_sum,
        small_sums[0:2],
        small_sums[2:12],
        d_qkv_sum,
        d_out_sum,
        c_query_sum,
        c_pairs_sum,
        c_out_sum,
        d_up_sum,
        d_down_sum,
        small_sums[12:15],
        small_sums[15:SMALL_ROWS],
    )


def solution(mesh):
    in_specs = (
        P(None, ("seq", "head"), None),
        P(None, ("seq", "head"), None),
        P(None, ("seq", "head"), None),
        P(),
        P(),
        P(),
        P(("seq", "head"), None),
        P(("seq", "head"), None),
        P(("seq", "head"), None),
        P(("seq", "head"), None),
        P(None, ("seq", "head")),
        P(None, ("seq", "head")),
        P(("seq", "head"), None),
        P(("seq", "head"), None),
        P(("seq", "head"), None),
        P(("seq", "head"), None),
        P(("seq", "head"), None),
        P(("seq", "head"), None),
        P(("seq", "head"), None),
        P(None, ("seq", "head")),
        P(None, ("seq", "head")),
    )
    out_specs = (
        P(None, ("seq", "head"), None),
        P(None, ("seq", "head"), None),
        P(None, ("seq", "head"), None),
        P(("seq", "head"), None),
        P(("seq", "head"), None),
        P(("seq", "head"), None),
        P(("seq", "head"), None),
        P(None, ("seq", "head")),
        P(None, ("seq", "head")),
        P(("seq", "head"), None),
        P(("seq", "head"), None),
        P(("seq", "head"), None),
        P(("seq", "head"), None),
        P(("seq", "head"), None),
        P(("seq", "head"), None),
        P(("seq", "head"), None),
        P(None, ("seq", "head")),
        P(None, ("seq", "head")),
    )
    return jax.shard_map(shards, mesh=mesh, in_specs=in_specs, out_specs=out_specs, check_vma=False)
```

```python
import functools

import jax
import jax.numpy as jnp
from jax import lax
from jax.experimental import pallas as pl
from jax.experimental.pallas import tpu as pltpu
from jax.sharding import PartitionSpec as P

D = 768
HEADS = 12
HEAD_DIM = 64
FF = 3072
MICRO = 2
STRETCH = 1024
REACH = 2
EVERY = ("seq", "head")

EPSILON = 1e-05
NEGATIVE = -1e30
MESH = pl.DeviceIdType.MESH
F32 = jnp.float32
BF16 = jnp.bfloat16


def place():
    seq, head = lax.axis_index("seq"), lax.axis_index("head")
    return seq // 2, seq % 2, head // 2, head % 2


def device(z, y, x, c):
    return (z * 2 + y, x * 2 + c)


def shard(z, y, x, c):
    return ((z * 2 + y) * 2 + x) * 2 + c


def greet(z, y, x, c, ahead=False):
    barrier = pltpu.get_barrier_semaphore()
    def tell(who):
        pl.semaphore_signal(barrier, inc=1, device_id=who, device_id_type=MESH)
    tell(device(z, y, x, 1 - c))
    tell(device(z, y, 1 - x, c))
    tell(device(z, 1 - y, x, c))
    @pl.when(z > 0)
    def _():
        tell(device(z - 1, y, x, c))
    @pl.when(z < 3)
    def _():
        tell(device(z + 1, y, x, c))
    if ahead:

        @pl.when((y == 1) & (z < 3))
        def _():
            tell(device(z + 1, 0, x, c))

        @pl.when((y == 0) & (z > 0))
        def _():
            tell(device(z - 1, 1, x, c))

    below, above = (z + 2) // 3, (5 - z) // 3
    count = 3 + below + above
    if ahead:
        count = count + y * above + (1 - y) * below
    pl.semaphore_wait(barrier, count)


def gather_kernel(count, shared, reach, orders, *refs, greeted=False):
    every = count + shared
    ins, outs, refs = refs[:every], refs[every : 2 * every + reach], refs[2 * every + reach :]
    own_sem, recv_sem, send_sem, group_recv, group_send, ahead_send = refs
    z, y, x, c = place()
    if not greeted:
        greet(z, y, x, c, reach > 0)
    here = [(x, y) if order in "xX" else (y, x) for order in orders]

    def shard_of(a, zo, f, l):
        return shard(zo, l, f, c) if orders[a] in "xX" else shard(zo, f, l, c)

    def holder(a, zo, f, l, cc):
        return device(zo, l, f, cc) if orders[a] in "xX" else device(zo, f, l, cc)

    def copy(a, src, where, who, kind):
        return pltpu.make_async_remote_copy(
            src_ref=src,
            dst_ref=outs[a].at[where],
            send_sem=send_sem.at[a, kind, where // 2],
            recv_sem=recv_sem.at[a, where],
            device_id=who,
            device_id_type=MESH,
        )

    def forward(a, src, where, first, up, down):
        f, l = here[a]
        if first:
            copy(a, src, where, holder(a, z, 1 - f, l, c), 0).start()
        if up:

            @pl.when(z < 3)
            def _():
                copy(a, src, where, holder(a, z + 1, f, l, c), 1).start()

        if down:

            @pl.when(z > 0)
            def _():
                copy(a, src, where, holder(a, z - 1, f, l, c), 2).start()

        copy(a, src, where, holder(a, z, f, 1 - l, c), 3).start()
        copy(a, src, where, holder(a, z, f, l, 1 - c), 4).start()

    def arrived(a, where):
        copy(a, outs[a].at[where], where, device(z, y, x, 1 - c), 0).wait_recv()

    def pass_on(a, zo, fo, first, up, down):
        where = shard_of(a, zo, fo, here[a][1])
        arrived(a, where)
        forward(a, outs[a].at[where], where, first, up, down)

    def from_last(zo, other):
        for a in range(count):
            f, l = here[a]
            where = shard_of(a, zo, 1 - f if other else f, 1 - l)
            arrived(a, where)
            copy(a, outs[a].at[where], where, holder(a, z, f, l, 1 - c), 4).start()

    def group_copy(b, src, xo, co, kind, who):
        return pltpu.make_async_remote_copy(
            src_ref=src,
            dst_ref=outs[count + b].at[xo * 2 + co],
            send_sem=group_send.at[b, kind],
            recv_sem=group_recv.at[b, xo * 2 + co],
            device_id=who,
            device_id_type=MESH,
        )

    over, beside = device(z, y, 1 - x, c), device(z, y, x, 1 - c)
    seq = z * 2 + y

    def ahead_copy(by):
        return pltpu.make_async_remote_copy(
            src_ref=ins[every - 1],
            dst_ref=outs[every + by - 1].at[x * 2 + c],
            send_sem=ahead_send.at[by - 1],
            recv_sem=group_recv.at[shared + by - 1, x * 2 + c],
            device_id=(seq + by, x * 2 + c),
            device_id_type=MESH,
        )

    def spread(b, source):
        group_copy(b, source, x, c, 0, over).start()
        group_copy(b, source, x, c, 1, beside).start()

    def spread_on(b):
        landed = outs[count + b].at[(1 - x) * 2 + c]
        group_copy(b, landed, 1 - x, c, 2, beside).wait_recv()
        group_copy(b, landed, 1 - x, c, 2, beside).start()

    def spread_done(b, source):
        landed = outs[count + b].at[(1 - x) * 2 + c]
        group_copy(b, source, x, 1 - c, 1, beside).wait_recv()
        group_copy(b, source, 1 - x, 1 - c, 1, beside).wait_recv()
        group_copy(b, source, x, c, 0, over).wait_send()
        group_copy(b, source, x, c, 1, beside).wait_send()
        group_copy(b, landed, 1 - x, c, 2, beside).wait_send()

    kept = []
    for a in range(count):
        me = shard_of(a, z, *here[a])
        forward(a, ins[a], me, True, True, True)
        kept.append(pltpu.make_async_copy(ins[a], outs[a].at[me], own_sem.at[a]))
        kept[-1].start()
    for a in range(count):
        early = orders[a] in "XY"
        pass_on(a, z, 1 - here[a][0], False, not early, not early)
    from_last(z, False)
    from_last(z, True)
    for b in range(shared):
        spread(b, ins[count + b])
        kept.append(
            pltpu.make_async_copy(
                ins[count + b], outs[count + b].at[x * 2 + c], own_sem.at[count + b]
            )
        )
        kept[-1].start()
    for by in range(1, reach + 1):

        @pl.when(seq + by <= 7)
        def _():
            ahead_copy(by).start()

    for distance in (1, 2, 3):
        if distance == 3:
            for b in range(shared):
                spread_on(b)
            for by in range(1, reach + 1):

                @pl.when(seq >= by)
                def _():
                    ahead_copy(by).wait_recv()
                    spread(shared + by - 1, outs[every + by - 1].at[x * 2 + c])

        for below in (True, False):

            @pl.when((z >= distance) if below else (z + distance <= 3))
            def _():
                zo = z - distance if below else z + distance
                for a in range(count):
                    early = orders[a] in "XY"
                    pass_on(a, zo, here[a][0], early, below, not below)
                    if not early:
                        pass_on(a, zo, 1 - here[a][0], False, below, not below)

        for below in (True, False):

            @pl.when((z >= distance) if below else (z + distance <= 3))
            def _():
                zo = z - distance if below else z + distance
                for a in range(count):
                    if orders[a] in "XY":
                        pass_on(a, zo, 1 - here[a][0], False, False, False)
                from_last(zo, False)
                from_last(zo, True)

    def sent(a, where, kind):
        copy(a, ins[a], where, device(z, y, x, 1 - c), kind).wait_send()

    def cores(i, carry):
        for a in range(count):
            arrived(a, i * 2 + 1 - c)
            sent(a, i * 2 + c, 4)
        return carry

    lax.fori_loop(0, 16, cores, 0)
    for by in range(1, reach + 1):

        @pl.when(seq >= by)
        def _():
            spread_on(shared + by - 1)
            spread_done(shared + by - 1, outs[every + by - 1].at[x * 2 + c])

        @pl.when(seq + by <= 7)
        def _():
            ahead_copy(by).wait_send()

    for b in range(shared):
        spread_done(b, ins[count + b])
    for copied in kept:
        copied.wait()
    for a in range(count):
        f, l = here[a]
        early = orders[a] in "XY"
        if not early:
            sent(a, shard_of(a, z, f, l), 0)
        for zo in range(4):
            if early:
                sent(a, shard_of(a, zo, f, l), 0)
            for fo in range(2):
                sent(a, shard_of(a, zo, fo, l), 3)
            for fo in [f] if early else [0, 1]:

                @pl.when((zo <= z) & (z < 3))
                def _():
                    sent(a, shard_of(a, zo, fo, l), 1)

                @pl.when((zo >= z) & (z > 0))
                def _():
                    sent(a, shard_of(a, zo, fo, l), 2)


def traffic(arrays, share):
    size = sum(v.size * v.dtype.itemsize for v in arrays)
    return pl.CostEstimate(flops=0, transcendentals=0, bytes_accessed=size * share)


def gather_scratch(count, shared, reach):
    spreads = max(shared + reach, 1)
    shapes = [(count + shared,), (count, 32), (count, 5, 16), (spreads, 4), (spreads, 3)]
    return [pltpu.SemaphoreType.DMA(shape) for shape in shapes + [(max(reach, 1),)]]


def gather_all(arrays, orders, collective_id, group_arrays=(), reach=0):
    count, shared = len(arrays), len(group_arrays)
    every = [*arrays, *group_arrays]
    results = [(32, v) for v in arrays] + [(4, v) for v in group_arrays]
    results += [(4, v) for v in every[-1:] * reach]
    return pl.pallas_call(
        functools.partial(gather_kernel, count, shared, reach, orders),
        out_shape=[jax.ShapeDtypeStruct((n,) + v.shape, v.dtype) for n, v in results],
        in_specs=[pl.BlockSpec(memory_space=pl.ANY)] * len(every),
        out_specs=[pl.BlockSpec(memory_space=pl.ANY)] * len(results),
        scratch_shapes=gather_scratch(count, shared, reach),
        compiler_params=pltpu.CompilerParams(collective_id=collective_id, has_side_effects=True),
        cost_estimate=traffic(arrays, 500),
        name="gather_all",
    )(*every)


def scatter_kernel(count, shared, orders, *refs):
    every = count + shared
    grads, outs, refs = refs[:every], refs[every : 2 * every], refs[2 * every :]
    held, mine, near, mid, right, left = [refs[k * count : (k + 1) * count] for k in range(6)]
    refs = refs[6 * count :]
    mine_sem, core_sem, near_sem, mid_sem, right_sem, left_sem, group_sem, refs = (
        *refs[:7],
        refs[7:],
    )
    group_held, group_mine, group_last = [refs[k * shared : (k + 1) * shared] for k in range(3)]
    z, y, x, c = place()
    greet(z, y, x, c)
    half = z // 2
    here = [(x, y) if order in "xX" else (y, x) for order in orders]
    late = [order in "XY" for order in orders]

    def block(a, zt, f, l):
        return (zt * 2 + l) * 2 + f if orders[a] in "xX" else (zt * 2 + f) * 2 + l

    def remote(a, src, dst, sems, slot, who):
        return pltpu.make_async_remote_copy(
            src_ref=src,
            dst_ref=dst,
            send_sem=sems.at[a, 0, slot],
            recv_sem=sems.at[a, 1, slot],
            device_id=who,
            device_id_type=MESH,
        )

    def core_copy(a, q):
        who = device(z, y, x, 1 - c)
        return remote(a, grads[a].at[q * 2 + 1 - c], held[a].at[q], core_sem, q, who)

    def mine_copy(a, q):
        return pltpu.make_async_copy(grads[a].at[q * 2 + c], mine[a].at[q], mine_sem.at[a, q])

    def along(a, first):
        flip_x = (orders[a] in "xX") == first
        return device(z, y, 1 - x, c) if flip_x else device(z, 1 - y, x, c)

    def near_copy(a, q, slot):
        return remote(a, held[a].at[q], near[a].at[slot], near_sem, slot, along(a, True))

    def mid_copy(a, q, slot):
        return remote(a, held[a].at[q], mid[a].at[slot], mid_sem, slot, along(a, False))

    def right_copy(a, q, slot):
        return remote(a, held[a].at[q], right[a].at[slot], right_sem, slot, device(z + 1, y, x, c))

    def left_copy(a, q, slot):
        return remote(a, held[a].at[q], left[a].at[slot], left_sem, slot, device(z - 1, y, x, c))

    def far(k):
        return 3 - k + half * (2 * k - 3)

    def others(k):
        down = 3 - k - (k // 2) * z
        up = k + (k // 2) * (3 - z)
        return down + half * (up - down)

    def add(a, q, *terms):
        total = held[a][q].astype(F32)
        for ref, slot in terms:
            total = total + ref[slot].astype(F32)
        held[a][q] = total.astype(BF16)

    for side in (True, False):

        def start(i, carry, side=side):
            for a in range(count):
                f = here[a][0]
                q = block(a, far(i // 2), 1 - f if side else f, i % 2)
                core_copy(a, q).start()
                mine_copy(a, q).start()
            return carry

        lax.fori_loop(0, 8, start, 0)

    def group_copy(b, kind):
        if kind < 2:
            xt = 1 - x if kind == 0 else x
            return pltpu.make_async_remote_copy(
                src_ref=grads[count + b].at[xt * 2 + 1 - c],
                dst_ref=group_held[b].at[kind],
                send_sem=group_sem.at[b, 0, kind],
                recv_sem=group_sem.at[b, 1, kind],
                device_id=device(z, y, x, 1 - c),
                device_id_type=MESH,
            )
        if kind < 4:
            xt = 1 - x if kind == 2 else x
            return pltpu.make_async_copy(
                grads[count + b].at[xt * 2 + c], group_mine[b].at[kind - 2], group_sem.at[b, 0, kind]
            )
        return pltpu.make_async_remote_copy(
            src_ref=group_held[b].at[0],
            dst_ref=group_last[b],
            send_sem=group_sem.at[b, 0, 4],
            recv_sem=group_sem.at[b, 1, 4],
            device_id=device(z, y, 1 - x, c),
            device_id_type=MESH,
        )

    def in_pieces(rows, step):
        piece = rows // 8

        def body(i, carry):
            step(pl.ds(pl.multiple_of(i * piece, piece), piece))
            return carry

        lax.fori_loop(0, 8, body, 0)

    for b in range(shared):
        for kind in range(4):
            group_copy(b, kind).start()

    def first_step(i, carry):
        zt, lt = far(i // 2), i % 2
        for a in range(count):
            q = block(a, zt, 1 - here[a][0], lt)
            core_copy(a, q).wait_recv()
            mine_copy(a, q).wait()
            add(a, q, (mine[a], q))
            near_copy(a, q, zt * 2 + lt).start()
        return carry

    lax.fori_loop(0, 8, first_step, 0)
    for b in range(shared):
        group_copy(b, 0).wait_recv()
        group_copy(b, 2).wait()

        def to_other(cut, b=b):
            total = group_held[b][0, cut, :].astype(F32) + group_mine[b][0, cut, :].astype(F32)
            group_held[b][0, cut, :] = total.astype(BF16)

        in_pieces(group_last[b].shape[0], to_other)
        group_copy(b, 4).start()

    def summed(a, zt, lt):
        q = block(a, zt, here[a][0], lt)
        core_copy(a, q).wait_recv()
        mine_copy(a, q).wait()
        near_copy(a, q, zt * 2 + lt).wait_recv()
        add(a, q, (mine[a], q), (near[a], zt * 2 + lt))
        return q

    if any(late):

        def mid_step(i, carry):
            zt = far(i)
            for a in range(count):
                if late[a]:
                    mid_copy(a, summed(a, zt, 1 - here[a][1]), zt).start()
            return carry

        lax.fori_loop(0, 4, mid_step, 0)

    def slots(a, zt, lt):
        return (zt - 1, zt) if late[a] else ((zt - 1) * 2 + lt, zt * 2 + lt)

    def along_z(a, zt, lt):
        q = summed(a, zt, lt)
        if late[a]:
            mid_copy(a, q, zt).wait_recv()
            add(a, q, (mid[a], zt))
        up, down = slots(a, zt, lt)

        @pl.when(zt > z)
        def _():
            @pl.when(z > 0)
            def _():
                right_copy(a, q, up).wait_recv()
                add(a, q, (right[a], up))

            right_copy(a, q, up).start()

        @pl.when(zt < z)
        def _():
            @pl.when(z < 3)
            def _():
                left_copy(a, q, down).wait_recv()
                add(a, q, (left[a], down))

            left_copy(a, q, down).start()

    def z_step(k, carry):
        for a in range(count):
            if late[a]:
                along_z(a, others(k), here[a][1])
            else:
                along_z(a, others(k), 0)
                along_z(a, others(k), 1)
        return carry

    lax.fori_loop(0, 3, z_step, 0)

    def from_z(a, q, lt):
        up, down = slots(a, z, lt)

        @pl.when(z > 0)
        def _():
            right_copy(a, q, up).wait_recv()
            add(a, q, (right[a], up))

        @pl.when(z < 3)
        def _():
            left_copy(a, q, down).wait_recv()
            add(a, q, (left[a], down))

    for a in range(count):
        if not late[a]:
            lt = 1 - here[a][1]
            q = summed(a, z, lt)
            from_z(a, q, lt)
            mid_copy(a, q, 0).start()
    for a in range(count):
        lt = here[a][1]
        q = summed(a, z, lt)
        if late[a]:
            mid_copy(a, q, z).wait_recv()
            add(a, q, (mid[a], z))
        from_z(a, q, lt)
    for a in range(count):
        q = block(a, z, *here[a])
        total = held[a][q].astype(F32)
        if not late[a]:
            mid_copy(a, q, 0).wait_recv()
            total = total + mid[a][0].astype(F32)
        outs[a][...] = total.astype(outs[a].dtype)

    for b in range(shared):
        group_copy(b, 1).wait_recv()
        group_copy(b, 3).wait()
        group_copy(b, 4).wait_recv()

        def at_home(cut, b=b):
            total = group_held[b][1, cut, :].astype(F32) + group_mine[b][1, cut, :].astype(F32)
            outs[count + b][cut, :] = total + group_last[b][cut, :].astype(F32)

        in_pieces(group_last[b].shape[0], at_home)
        for kind in (0, 1, 4):
            group_copy(b, kind).wait_send()

    def sent_core(i, carry):
        for a in range(count):
            core_copy(a, i).wait_send()
        return carry

    lax.fori_loop(0, 16, sent_core, 0)

    def sent_near(i, carry):
        for a in range(count):
            near_copy(a, block(a, i // 2, 1 - here[a][0], i % 2), i).wait_send()
        return carry

    lax.fori_loop(0, 8, sent_near, 0)

    def sent_z(k, carry):
        zt = others(k)
        for a in range(count):
            for lt in [here[a][1]] if late[a] else [0, 1]:
                q = block(a, zt, here[a][0], lt)
                up, down = slots(a, zt, lt)

                @pl.when(zt > z)
                def _():
                    right_copy(a, q, up).wait_send()

                @pl.when(zt < z)
                def _():
                    left_copy(a, q, down).wait_send()

        return carry

    lax.fori_loop(0, 3, sent_z, 0)
    for a in range(count):
        f, l = here[a]
        if late[a]:
            for zt in range(4):
                mid_copy(a, block(a, zt, f, 1 - l), zt).wait_send()
        else:
            mid_copy(a, block(a, z, f, 1 - l), 0).wait_send()


def scatter_scratch(shapes, orders, shared):
    count = len(shapes) - shared
    late = [order in "XY" for order in orders]
    sizes = [[16, 16, 8, 4, 3, 3] if up else [16, 16, 8, 1, 6, 6] for up in late]
    scratch = []
    for k in range(6):
        scratch += [pltpu.VMEM((size[k],) + shape, BF16) for size, shape in zip(sizes, shapes)]
    scratch += [pltpu.SemaphoreType.DMA((count, 16))]
    scratch += [pltpu.SemaphoreType.DMA((count, 2, n)) for n in (16, 8, 4, 6, 6)]
    scratch += [pltpu.SemaphoreType.DMA((max(shared, 1), 2, 5))]
    scratch += [pltpu.VMEM((2,) + shape, BF16) for shape in shapes[count:]] * 2
    scratch += [pltpu.VMEM(shape, BF16) for shape in shapes[count:]]
    return scratch


def scatter_sum(arrays, orders, collective_id, out_dtype=F32, group_arrays=()):
    count, shared = len(arrays), len(group_arrays)
    shapes = [v.shape[1:] for v in (*arrays, *group_arrays)]
    return pl.pallas_call(
        functools.partial(scatter_kernel, count, shared, orders),
        out_shape=[jax.ShapeDtypeStruct(shape, out_dtype) for shape in shapes],
        in_specs=[pl.BlockSpec(memory_space=pl.ANY)] * len(shapes),
        out_specs=[pl.BlockSpec(memory_space=pltpu.VMEM)] * len(shapes),
        scratch_shapes=scatter_scratch(shapes, orders, shared),
        compiler_params=pltpu.CompilerParams(
            collective_id=collective_id, has_side_effects=True, vmem_limit_bytes=60 << 20
        ),
        cost_estimate=traffic(arrays, 1),
        name="scatter_sum",
    )(*arrays, *group_arrays)


def exchange_kernel(count, orders, *refs):
    grads, outs, sums = [refs[k * count : (k + 1) * count] for k in range(3)]
    refs = refs[3 * count :]
    scatter_refs = 6 * count + 7
    scatter_kernel(count, 0, orders, *grads, *sums, *refs[:scatter_refs])
    gather_kernel(count, 0, 0, orders, *sums, *outs, *refs[scatter_refs:], greeted=True)


def exchange_all(arrays, orders, collective_id):
    count = len(arrays)
    shapes = [v.shape[1:] for v in arrays]
    scratch = [pltpu.VMEM(shape, BF16) for shape in shapes]
    scratch += scatter_scratch(shapes, orders, 0) + gather_scratch(count, 0, 0)
    return pl.pallas_call(
        functools.partial(exchange_kernel, count, orders),
        out_shape=[jax.ShapeDtypeStruct(v.shape, v.dtype) for v in arrays],
        in_specs=[pl.BlockSpec(memory_space=pl.ANY)] * count,
        out_specs=[pl.BlockSpec(memory_space=pl.ANY)] * count,
        scratch_shapes=scratch,
        compiler_params=pltpu.CompilerParams(
            collective_id=collective_id, has_side_effects=True, vmem_limit_bytes=48 << 20
        ),
        cost_estimate=traffic(arrays, 2),
        name="exchange_all",
    )(*arrays)


def known_mesh():
    return lax.axis_size("seq") == 8 and lax.axis_size("head") == 4


def gather(arrays, orders, collective_id, group_arrays=(), reach=0):
    if known_mesh():
        return gather_all(arrays, orders, collective_id, group_arrays, reach)
    every = [lax.all_gather(v, EVERY, axis=0, tiled=False) for v in arrays]
    group = [lax.all_gather(v, "head", axis=0, tiled=False) for v in group_arrays]
    return every + group + [from_before(group[-1], by) for by in range(1, reach + 1)]


def scatter(arrays, orders, collective_id, out_dtype=F32, group_arrays=()):
    if known_mesh():
        return scatter_sum(arrays, orders, collective_id, out_dtype, group_arrays)
    return [
        lax.psum_scatter(v, axes, scatter_dimension=0, tiled=False).astype(out_dtype)
        for v, axes in [(v, EVERY) for v in arrays] + [(v, "head") for v in group_arrays]
    ]


def exchange(arrays, orders, collective_id):
    if known_mesh():
        return exchange_all(arrays, orders, collective_id)
    sums = [lax.psum_scatter(v, EVERY, scatter_dimension=0, tiled=False) for v in arrays]
    return [lax.all_gather(v, EVERY, axis=0, tiled=False) for v in sums]


def fill(target, refs, columns, scale=None):
    at = 0
    for ref in refs:
        rows = ref.shape[2]
        for p in range(ref.shape[0]):
            piece = ref[p, 0, :, columns]
            target[at : at + rows] = piece if scale is None else piece * scale
            at += rows


def spill(value, refs, columns):
    at = 0
    for ref in refs:
        rows = ref.shape[2]
        for p in range(ref.shape[0]):
            ref[p, 0, :, columns] = value[at : at + rows].astype(ref.dtype)
            at += rows


def across(left, right):
    return lax.dot_general(left, right, (((1,), (1,)), ((), ())), preferred_element_type=F32)


def down(left, right):
    return lax.dot_general(left, right, (((0,), (0,)), ((), ())), preferred_element_type=F32)


def soft_columns(scores):
    peak = jnp.max(scores, axis=0, keepdims=True)
    weights = jnp.exp(scores - peak)
    total = jnp.sum(weights, axis=0, keepdims=True)
    return weights * (1.0 / total), peak + jnp.log(total)


def score_grads(probs, grad_probs):
    delta = jnp.sum(probs * grad_probs, axis=0, keepdims=True)
    return (probs * (grad_probs - delta)).astype(BF16)


def allowed_pairs(key_ref, query_ref, start, tile, causal):
    doc_key, doc_query = key_ref[0, :, 0:1], query_ref[0, 0:1, pl.ds(start, tile)]
    allowed = doc_key == doc_query
    if causal:
        allowed &= key_ref[0, :, 1:2] <= query_ref[0, 1:2, pl.ds(start, tile)]
    return allowed


def attend_kernel(heads, tile, causal, *refs):
    key_ref, query_ref, own_ref = refs[:3]
    prior = refs[3:-6]
    out_ref, log_ref, key_s, value_s, query_s, result_s = refs[-6:]
    group = query_s.shape[0]
    for h in range(heads):
        fill(key_s, (*prior, own_ref), slice(h * 128, h * 128 + 64))
        fill(value_s, (*prior, own_ref), slice(h * 128 + 64, h * 128 + 128))
        at = heads * 128 + h * 64
        fill(query_s, (own_ref,), slice(at, at + 64), 0.125)
        values = value_s[...].T

        def step(i, carry):
            start = pl.multiple_of(i * tile, tile)
            allowed = allowed_pairs(key_ref, query_ref, start, tile, causal)
            scores = across(key_s[...], query_s[pl.ds(start, tile), :])
            probs, log_total = soft_columns(jnp.where(allowed, scores, NEGATIVE))
            made = jnp.dot(values, probs.astype(BF16), preferred_element_type=F32)
            result_s[pl.ds(start, tile), :] = made.astype(BF16).T
            log_ref[0, h : h + 1, pl.ds(start, tile)] = log_total
            return carry

        lax.fori_loop(0, group // tile, step, 0)
        spill(result_s[...], (out_ref,), slice(h * 64, h * 64 + 64))


def rows_spec(shape):
    return pl.BlockSpec((shape[0], 1) + shape[2:], lambda m: (0, m, 0, 0))


def whole_spec(shape):
    return pl.BlockSpec((1,) + shape[1:], lambda m: (m, 0, 0))


def attend(joined, prior, key_info, query_info, heads, causal, tile=256):
    parts, micro, rows, _ = joined.shape
    group = parts * rows
    keys = key_info.shape[1]
    out, logs = (parts, micro, rows, heads * 64), (micro, heads, group)
    return pl.pallas_call(
        functools.partial(attend_kernel, heads, tile, causal),
        grid=(micro,),
        out_shape=[jax.ShapeDtypeStruct(out, BF16), jax.ShapeDtypeStruct(logs, F32)],
        in_specs=[whole_spec(key_info.shape), whole_spec(query_info.shape), rows_spec(joined.shape)]
        + [rows_spec(p.shape) for p in prior],
        out_specs=[rows_spec(out), whole_spec(logs)],
        scratch_shapes=[
            pltpu.VMEM((keys, 64), BF16),
            pltpu.VMEM((keys, 64), BF16),
            pltpu.VMEM((group, 64), BF16),
            pltpu.VMEM((group, 64), BF16),
        ],
        compiler_params=pltpu.CompilerParams(vmem_limit_bytes=48 << 20),
        cost_estimate=pl.CostEstimate(
            flops=16 * micro * heads * group * keys * 128,
            transcendentals=micro * heads * group * keys,
            bytes_accessed=joined.size * 4,
        ),
        name="attend",
    )(key_info, query_info, joined, *prior)


def attend_back_kernel(heads, tile, causal, count, *refs):
    key_ref, query_ref, own_ref, log_ref, grad_ref = refs[:5]
    prior = refs[5 : 5 + count]
    out_ref, *prior_out = refs[5 + count : 6 + 2 * count]
    key_s, value_s, query_s, grad_s, gk_s, gv_s, result_s = refs[6 + 2 * count :]
    group = query_s.shape[0]
    for h in range(heads):
        key_cut, value_cut = slice(h * 128, h * 128 + 64), slice(h * 128 + 64, h * 128 + 128)
        fill(key_s, (*prior, own_ref), key_cut)
        fill(value_s, (*prior, own_ref), value_cut)
        query_cut = slice(heads * 128 + h * 64, heads * 128 + h * 64 + 64)
        fill(query_s, (own_ref,), query_cut, 0.125)
        fill(grad_s, (grad_ref,), slice(h * 64, h * 64 + 64))
        gk_s[...] = jnp.zeros_like(gk_s)
        gv_s[...] = jnp.zeros_like(gv_s)
        keys = key_s[...].T

        def step(i, carry):
            start = pl.multiple_of(i * tile, tile)
            here = pl.ds(start, tile)
            allowed = allowed_pairs(key_ref, query_ref, start, tile, causal)
            query, grad_out = query_s[here, :], grad_s[here, :]
            scores = jnp.where(allowed, across(key_s[...], query), NEGATIVE)
            probs = jnp.exp(scores - log_ref[0, h : h + 1, here])
            grad_scores = score_grads(probs, across(value_s[...], grad_out))
            gv_s[...] += jnp.dot(probs.astype(BF16), grad_out, preferred_element_type=F32)
            gk_s[...] += jnp.dot(grad_scores, query, preferred_element_type=F32)
            made = jnp.dot(keys, grad_scores, preferred_element_type=F32)
            result_s[here, :] = made.T * 0.125
            return carry

        lax.fori_loop(0, group // tile, step, 0)
        spill(result_s[...], (out_ref,), query_cut)
        spill(gk_s[...], (*prior_out, out_ref), key_cut)
        spill(gv_s[...], (*prior_out, out_ref), value_cut)
    for p in range(out_ref.shape[0]):
        out_ref[p, 0, :, heads * 192 :] = jnp.zeros(
            (out_ref.shape[2], out_ref.shape[3] - heads * 192), out_ref.dtype
        )


def attend_back(
    joined, prior, key_info, query_info, logs, grad, heads, causal, out_dtype, tile=256
):
    parts, micro, rows, _ = joined.shape
    group = parts * rows
    keys = key_info.shape[1]
    return pl.pallas_call(
        functools.partial(attend_back_kernel, heads, tile, causal, len(prior)),
        grid=(micro,),
        out_shape=[jax.ShapeDtypeStruct(joined.shape, out_dtype)]
        + [jax.ShapeDtypeStruct(p.shape, BF16) for p in prior],
        in_specs=[
            whole_spec(key_info.shape),
            whole_spec(query_info.shape),
            rows_spec(joined.shape),
            whole_spec(logs.shape),
            rows_spec(grad.shape),
        ]
        + [rows_spec(p.shape) for p in prior],
        out_specs=[rows_spec(joined.shape)] + [rows_spec(p.shape) for p in prior],
        scratch_shapes=[
            pltpu.VMEM((keys, 64), BF16),
            pltpu.VMEM((keys, 64), BF16),
            pltpu.VMEM((group, 64), BF16),
            pltpu.VMEM((group, 64), BF16),
            pltpu.VMEM((keys, 64), F32),
            pltpu.VMEM((keys, 64), F32),
            pltpu.VMEM((group, 64), F32),
        ],
        compiler_params=pltpu.CompilerParams(vmem_limit_bytes=48 << 20),
        cost_estimate=pl.CostEstimate(
            flops=24 * micro * heads * group * keys * 128,
            transcendentals=micro * heads * group * keys,
            bytes_accessed=joined.size * 6,
        ),
        name="attend_back",
    )(key_info, query_info, joined, logs, grad, *prior)


def cross_kernel(query_ref, pairs_ref, out_ref, log_ref):
    for i in range(D // 128):
        outs = []
        for h in range(2):
            at = i * 128 + h * 64
            query, keys = query_ref[0, :, at : at + 64] * 0.125, pairs_ref[0, :, at : at + 64]
            values = pairs_ref[0, :, D + at : D + at + 64]
            probs, log_total = soft_columns(across(keys, query))
            outs.append(down(probs.astype(BF16), values))
            log_ref[0, i * 2 + h : i * 2 + h + 1, :] = log_total
        out_ref[0, :, i * 128 : i * 128 + 128] = jnp.concatenate(outs, axis=1).astype(BF16)


def cross(query, pairs):
    micro, rows, _ = query.shape
    keys = pairs.shape[1]
    logs = (micro, HEADS, rows)
    return pl.pallas_call(
        cross_kernel,
        grid=(micro,),
        out_shape=[jax.ShapeDtypeStruct(query.shape, BF16), jax.ShapeDtypeStruct(logs, F32)],
        in_specs=[whole_spec(query.shape), whole_spec(pairs.shape)],
        out_specs=[whole_spec(query.shape), whole_spec(logs)],
        compiler_params=pltpu.CompilerParams(vmem_limit_bytes=48 << 20),
        cost_estimate=pl.CostEstimate(
            flops=16 * micro * HEADS * rows * keys * 128,
            transcendentals=micro * HEADS * rows * keys,
            bytes_accessed=pairs.size * 2,
        ),
        name="cross",
    )(query, pairs)


def cross_back_kernel(
    query_ref, pairs_ref, log_ref, grad_ref, grad_query_ref, grad_pairs_ref
):
    for i in range(D // 128):
        query_parts, key_parts, value_parts = [], [], []
        for h in range(2):
            at = i * 128 + h * 64
            cut = slice(at, at + 64)
            query, keys = query_ref[0, :, cut] * 0.125, pairs_ref[0, :, cut]
            values, grad_out = pairs_ref[0, :, D + at : D + at + 64], grad_ref[0, :, cut]
            probs = jnp.exp(across(keys, query) - log_ref[0, i * 2 + h : i * 2 + h + 1, :])
            grad_scores = score_grads(probs, across(values, grad_out))
            value_parts.append(jnp.dot(probs.astype(BF16), grad_out, preferred_element_type=F32))
            key_parts.append(jnp.dot(grad_scores, query, preferred_element_type=F32))
            query_parts.append(jnp.dot(keys.T, grad_scores, preferred_element_type=F32))
        cut = slice(i * 128, i * 128 + 128)
        made = jnp.concatenate(query_parts, axis=0).T * 0.125
        grad_query_ref[0, :, cut] = made.astype(BF16)
        grad_pairs_ref[0, :, cut] = jnp.concatenate(key_parts, axis=1).astype(BF16)
        cut = slice(D + i * 128, D + i * 128 + 128)
        grad_pairs_ref[0, :, cut] = jnp.concatenate(value_parts, axis=1).astype(BF16)


def cross_back(query, pairs, logs, grad):
    micro, rows, _ = query.shape
    keys = pairs.shape[1]
    return pl.pallas_call(
        cross_back_kernel,
        grid=(micro,),
        out_shape=[jax.ShapeDtypeStruct(query.shape, BF16), jax.ShapeDtypeStruct(pairs.shape, BF16)],
        in_specs=[whole_spec(v.shape) for v in (query, pairs, logs, grad)],
        out_specs=[whole_spec(query.shape), whole_spec(pairs.shape)],
        compiler_params=pltpu.CompilerParams(vmem_limit_bytes=48 << 20),
        cost_estimate=pl.CostEstimate(
            flops=24 * micro * HEADS * rows * keys * 128,
            transcendentals=micro * HEADS * rows * keys,
            bytes_accessed=pairs.size * 4,
        ),
        name="cross_back",
    )(query, pairs, logs, grad)


SMALL_ROWS = 29
SINGLES = (4, 0, 5, 10, 1, 11, 17, 12, 18, 19, 21, 13, 22, 27, 14, 28)


def head_places(head, heads):
    base = head // heads * joined_width(heads) + head % heads * 64
    return base + head % heads * 64 + 64, base + heads * 128


def joined_width(heads):
    return (heads * 192 + 127) // 128 * 128


def unpack_kernel(width, heads, pack_ref, *refs):
    e_joined, e_hidden, d_joined, d_hidden, pair_bias = refs[:5]
    singles, full = refs[5:-1], refs[-1]
    for d in range(pack_ref.shape[0]):
        full[:, d * width : d * width + width] = pack_ref[d, :, 0:width].astype(F32)
    for target, row in ((e_joined, 2), (d_joined, 15)):
        target[...] = jnp.zeros_like(target)
        for head in range(HEADS):
            value_at, query_at = head_places(head, heads)
            cut = slice(head * 64, head * 64 + 64)
            target[:, query_at : query_at + 64] = full[row : row + 1, cut]
            target[:, value_at : value_at + 64] = full[row + 1 : row + 2, cut]
    for target, row in ((e_hidden, 6), (d_hidden, 23)):
        for k in range(FF // D):
            target[:, k * D : k * D + D] = full[row + k : row + k + 1, :]
    pair_bias[:, 0:D] = jnp.zeros((1, D), F32)
    pair_bias[:, D:] = full[20:21, :]
    for target, row in zip(singles, SINGLES):
        target[...] = full[row : row + 1, :]


def unpack_small(packs, heads):
    devices = packs.shape[0]
    joined = joined_width(heads) * (HEADS // heads)
    widths = [joined, FF, joined, FF, 2 * D] + [D] * len(SINGLES)
    return pl.pallas_call(
        functools.partial(unpack_kernel, D // devices, heads),
        out_shape=[jax.ShapeDtypeStruct((1, w), F32) for w in widths],
        scratch_shapes=[pltpu.VMEM((32, D), F32)],
        name="unpack_small",
    )(packs)


def pack_kernel(width, heads, count, *refs):
    e_joined, e_hidden, d_joined, d_hidden, pair_sum = refs[:5]
    singles, out_ref, full = refs[5 : 5 + count], refs[-2], refs[-1]
    full[...] = jnp.zeros_like(full)
    for source, row in ((e_joined, 2), (d_joined, 15)):
        for head in range(HEADS):
            value_at, query_at = head_places(head, heads)
            cut = slice(head * 64, head * 64 + 64)
            full[row : row + 1, cut] = source[:, query_at : query_at + 64]
            full[row + 1 : row + 2, cut] = source[:, value_at : value_at + 64]
    for source, row in ((e_hidden, 6), (d_hidden, 23)):
        for k in range(FF // D):
            full[row + k : row + k + 1, :] = source[k * D : k * D + D].reshape(1, D)
    full[20:21, :] = pair_sum[D:].reshape(1, D)
    for source, row in zip(singles, SINGLES):
        full[row : row + 1, :] = source[...].reshape(1, D)
    out_ref[...] = jnp.zeros_like(out_ref)
    for d in range(out_ref.shape[0]):
        out_ref[d, :, 0:width] = full[:, d * width : d * width + width].astype(BF16)


def pack_small(vectors, devices, heads):
    return pl.pallas_call(
        functools.partial(pack_kernel, D // devices, heads, len(SINGLES)),
        out_shape=jax.ShapeDtypeStruct((devices, 32, 128), BF16),
        scratch_shapes=[pltpu.VMEM((32, D), F32)],
        name="pack_small",
    )(*vectors)


def finish_kernel(heads, *refs):
    late, pack, outs = refs[:7], refs[7], refs[8:]
    for k in (0, 4):
        for head in range(HEADS):
            value_at, query_at = head_places(head, heads)
            for n, at in enumerate((query_at, value_at - 64, value_at)):
                start = head * 192 + n * 64
                outs[k][:, start : start + 64] = late[k][:, at : at + 64]
    for k in (1, 2, 3, 5, 6):
        outs[k][...] = late[k][...]
    at = 0
    for target in outs[7:]:
        width = target.shape[1]
        target[...] = pack[:, at : at + width].astype(F32)
        at += width


def finish(late, early, heads):
    rows = late[0].shape[0]
    shapes = [v.shape for v in late]
    shapes[0] = shapes[4] = (rows, 3 * D)
    shapes += [(rows, width) for width in (D, 2 * D, D, FF, FF)]
    return pl.pallas_call(
        functools.partial(finish_kernel, heads),
        out_shape=[jax.ShapeDtypeStruct(shape, F32) for shape in shapes],
        compiler_params=pltpu.CompilerParams(vmem_limit_bytes=48 << 20),
        name="finish",
    )(*late, early)


def norm(resid, gain, shift):
    center = resid - jnp.mean(resid, axis=-1, keepdims=True)
    scale = lax.rsqrt(jnp.mean(center * center, axis=-1, keepdims=True) + EPSILON)
    hat = center * scale
    return hat * gain + shift, (hat, scale)


def norm_back(grad, kept, gain):
    hat, scale = kept
    inner = grad * gain
    grad_resid = scale * (
        inner
        - jnp.mean(inner, axis=-1, keepdims=True)
        - hat * jnp.mean(inner * hat, axis=-1, keepdims=True)
    )
    return grad_resid, jnp.sum(grad * hat, axis=0), jnp.sum(grad, axis=0)


def gelu(value):
    return value * (1.0 + lax.erf(value * 0.7071067811865476)) * 0.5


def gelu_slope(value):
    bell = jnp.exp(value * value * -0.5) * 0.3989422804014327
    return 0.5 * (1.0 + lax.erf(value * 0.7071067811865476)) + value * bell


def mm(left, right):
    return jnp.dot(left, right, preferred_element_type=F32)


def mm_rows(left, right):
    return lax.dot_general(left, right, (((0,), (0,)), ((), ())), preferred_element_type=F32)


def mm_back(left, right):
    return lax.dot_general(left, right, (((1,), (1,)), ((), ())), preferred_element_type=F32)


def row_sum(value):
    return jnp.sum(value.astype(F32), axis=0)


def doc_starts(lengths):
    count = lengths.shape[1]
    before = jnp.arange(count)[None, :] < jnp.arange(count)[:, None]
    return jnp.sum(jnp.where(before[None], lengths[:, None, :], 0), axis=2)


def doc_ids(starts, positions):
    return jnp.sum((starts[:, None, :] <= positions[None, :, None]).astype(jnp.int32), axis=2) - 1


def key_and_query_info(starts, key_pos, query_pos):
    key_docs, query_docs = doc_ids(starts, key_pos), doc_ids(starts, query_pos)
    micro = starts.shape[0]
    key_info = jnp.stack(
        [key_docs, jnp.broadcast_to(key_pos, (micro,) + key_pos.shape)], axis=2
    )
    query_info = jnp.stack(
        [query_docs, jnp.broadcast_to(query_pos, (micro,) + query_pos.shape)], axis=1
    )
    return key_info, query_info


def by_group(weight, parts):
    rows = weight.shape[0]
    split = weight.reshape(rows, parts, HEADS // parts, 3, HEAD_DIM)
    pairs = split[:, :, :, 1:].reshape(rows, parts, -1)
    query = split[:, :, :, 0].reshape(rows, parts, -1)
    width = joined_width(HEADS // parts)
    blank = jnp.zeros((rows, parts, width - pairs.shape[2] - query.shape[2]), weight.dtype)
    return jnp.concatenate([pairs, query, blank], axis=2).reshape(rows, parts * width)


def by_head(grad, parts):
    rows, heads = grad.shape[0], HEADS // parts
    split = grad.reshape(rows, parts, -1)
    pairs = split[:, :, : heads * 128].reshape(rows, parts, heads, 2, HEAD_DIM)
    query = split[:, :, heads * 128 : heads * 192].reshape(rows, parts, heads, 1, HEAD_DIM)
    return jnp.concatenate([query, pairs], axis=3).reshape(rows, 3 * D)


def my_columns(full, parts):
    width = full.shape[1] // parts
    return lax.dynamic_slice_in_dim(full, lax.axis_index("head") * width, width, 1)


def all_columns(mine, parts):
    rows, width = mine.shape
    full = jnp.zeros((rows, width * parts), mine.dtype)
    return lax.dynamic_update_slice_in_dim(full, mine, lax.axis_index("head") * width, 1)


def to_tokens(value):
    parts, micro, rows, columns = value.shape
    got = lax.all_to_all(value, "head", split_axis=0, concat_axis=0, tiled=True)
    return got.transpose(1, 2, 0, 3).reshape(micro * rows, parts * columns)


def to_heads(value, parts, micro):
    rows = value.shape[0] // micro
    split = value.reshape(micro, rows, parts, -1).transpose(2, 0, 1, 3)
    return lax.all_to_all(split, "head", split_axis=0, concat_axis=0, tiled=True)


def from_before(value, by):
    count = lax.axis_size("seq")
    return lax.ppermute(value, "seq", [(i, i + by) for i in range(count - by)])


def to_before(value, by):
    count = lax.axis_size("seq")
    return lax.ppermute(value, "seq", [(i + by, i) for i in range(count - by)])


def shards(
    source,
    target,
    cotangent,
    src_lengths,
    tgt_lengths,
    retrieved,
    encoder_qkv,
    encoder_out,
    encoder_up,
    encoder_down,
    encoder_gains,
    encoder_biases,
    decoder_qkv,
    decoder_out,
    cross_query,
    cross_keyvalue,
    cross_out,
    decoder_up,
    decoder_down,
    decoder_gains,
    decoder_biases,
):
    micro, src_rows, _ = source.shape
    tgt_rows = target.shape[1]
    parts = lax.axis_size("head")
    devices = parts * lax.axis_size("seq")
    seq, me = lax.axis_index("seq"), lax.axis_index(EVERY)
    src_group, tgt_group = src_rows * parts, tgt_rows * parts
    asked = retrieved.shape[1]
    source_rows = source.reshape(micro * src_rows, D)
    target_rows = target.reshape(micro * tgt_rows, D)

    heads = HEADS // parts
    small = jnp.concatenate([encoder_gains, encoder_biases, decoder_gains, decoder_biases], axis=0)
    small = jnp.pad(small, ((0, 32 - SMALL_ROWS), (0, 128 - small.shape[1])))
    encoder_full = gather(
        [by_group(encoder_qkv, parts), encoder_out, encoder_up, encoder_down, small],
        "yxxxx",
        0,
        [source, target],
        REACH,
    )
    source_all, target_all, *target_before = encoder_full[5:]
    decoder_parts = [
        by_group(decoder_qkv, parts),
        decoder_out,
        cross_query,
        cross_keyvalue,
        cross_out,
        decoder_up,
    ]
    decoder_pack, small_full = lax.optimization_barrier(
        (jnp.concatenate(decoder_parts, axis=1), encoder_full[4])
    )
    decoder_full = lax.all_gather(decoder_pack, EVERY, axis=0, tiled=True)
    d_down = lax.all_gather(decoder_down, EVERY, axis=0, tiled=True)
    e_qkv, e_out, e_up, e_down = [v.reshape(-1, v.shape[-1]) for v in encoder_full[:4]]
    e_bias, e_hidden_bias, d_bias, d_hidden_bias, pair_bias, *singles = unpack_small(
        small_full, heads
    )
    e_b2, e_g0, e_b3, e_b8, e_g1, e_b9 = singles[:6]
    d_b2, d_g0, d_b3, d_b4, d_b6, d_g1, d_b7, d_b12, d_g2, d_b13 = singles[6:]

    src_pos = seq * src_group + jnp.arange(src_group, dtype=jnp.int32)
    src_info = key_and_query_info(doc_starts(src_lengths), src_pos, src_pos)
    tgt_pos = seq * tgt_group + jnp.arange(tgt_group, dtype=jnp.int32)
    tgt_key_pos = (seq - REACH) * tgt_group + jnp.arange((REACH + 1) * tgt_group, dtype=jnp.int32)
    tgt_info = key_and_query_info(doc_starts(tgt_lengths), tgt_key_pos, tgt_pos)

    e_qkv_here = my_columns(e_qkv, parts)
    e_joined = (mm(source_all.reshape(-1, D), e_qkv_here) + my_columns(e_bias, parts)).astype(BF16)
    e_joined = e_joined.reshape(parts, micro, src_rows, -1)
    e_attended, e_logs = attend(e_joined, [], *src_info, heads, False)
    e_mixed = to_tokens(e_attended)
    e_first, e_kept_one = norm(
        source_rows.astype(F32) + mm(e_mixed, e_out) + e_b2, e_g0, e_b3
    )
    e_first_low = e_first.astype(BF16)
    e_hidden = mm(e_first_low, e_up) + e_hidden_bias
    e_active = gelu(e_hidden).astype(BF16)
    e_result, e_kept_two = norm(e_first + mm(e_active, e_down) + e_b8, e_g1, e_b9)

    src_own = me * src_rows + jnp.arange(src_rows, dtype=jnp.int32)
    select = (retrieved[:, :, None] == src_own[None, None, :]).astype(BF16)
    picked = jnp.einsum(
        "mrs,msd->mrd",
        select,
        e_result.astype(BF16).reshape(micro, src_rows, D),
        preferred_element_type=F32,
    ).astype(BF16)
    picked = [picked[m].reshape(devices, asked // devices, D) for m in range(micro)]
    fetched = exchange(picked, "xy", 2)
    fetched = jnp.concatenate([v.reshape(asked, D) for v in fetched], axis=0)
    decoder_full, fetched = lax.optimization_barrier((decoder_full, fetched))
    ends = [0]
    for part in decoder_parts:
        ends.append(ends[-1] + part.shape[1])
    d_qkv, d_out, c_query, c_pairs, c_out, d_up = [
        decoder_full[:, start:end] for start, end in zip(ends, ends[1:])
    ]

    d_qkv_here = my_columns(d_qkv, parts)
    d_joined = (mm(target_all.reshape(-1, D), d_qkv_here) + my_columns(d_bias, parts)).astype(BF16)
    d_joined = d_joined.reshape(parts, micro, tgt_rows, -1)
    pair_weights, pair_shift = d_qkv_here[:, : heads * 128], my_columns(d_bias, parts)[:, : heads * 128]
    d_prior = []
    for by in range(REACH, 0, -1):
        before = (mm(target_before[by - 1].reshape(-1, D), pair_weights) + pair_shift).astype(BF16)
        before = jnp.where(seq >= by, before, jnp.zeros_like(before))
        d_prior.append(before.reshape(parts, micro, tgt_rows, -1))
    d_attended, d_logs = attend(d_joined, d_prior, *tgt_info, heads, True)
    d_mixed = to_tokens(d_attended)
    d_first, d_kept_one = norm(
        target_rows.astype(F32) + mm(d_mixed, d_out) + d_b2, d_g0, d_b3
    )
    d_first_low = d_first.astype(BF16)
    queries = (mm(d_first_low, c_query) + d_b4).astype(BF16).reshape(micro, tgt_rows, D)

    pairs = (mm(fetched, c_pairs) + pair_bias).astype(BF16).reshape(micro, asked, 2 * D)

    crossed_rows, cross_logs = cross(queries, pairs)
    crossed = crossed_rows.reshape(micro * tgt_rows, D)
    d_second, d_kept_two = norm(d_first + mm(crossed, c_out) + d_b6, d_g1, d_b7)
    d_second_low = d_second.astype(BF16)
    d_hidden = mm(d_second_low, d_up) + d_hidden_bias
    d_active = gelu(d_hidden).astype(BF16)
    decoded, d_kept_three = norm(d_second + mm(d_active, d_down) + d_b12, d_g2, d_b13)

    grad = cotangent.reshape(micro * tgt_rows, D).astype(F32)
    g_sum, d_gain_three, d_shift_three = norm_back(grad, d_kept_three, d_g2)
    g_third = g_sum.astype(BF16)
    w_d_down = mm_rows(d_active, g_third)
    g_hidden = (mm_back(g_third, d_down) * gelu_slope(d_hidden)).astype(BF16)
    w_d_up = mm_rows(d_second_low, g_hidden)
    g_second = g_sum + mm_back(g_hidden, d_up)
    g_sum_two, d_gain_two, d_shift_two = norm_back(g_second, d_kept_two, d_g1)
    g_branch_cross = g_sum_two.astype(BF16)
    w_c_out = mm_rows(crossed, g_branch_cross)
    g_crossed = mm_back(g_branch_cross, c_out).astype(BF16).reshape(micro, tgt_rows, D)
    g_queries, g_pairs = cross_back(queries, pairs, cross_logs, g_crossed)
    g_queries = g_queries.reshape(micro * tgt_rows, D)
    g_pairs = g_pairs.reshape(micro * asked, 2 * D)
    g_fetched = mm_back(g_pairs, c_pairs).astype(BF16).reshape(micro, asked, D)
    g_fetched = [g_fetched[m].reshape(devices, asked // devices, D) for m in range(micro)]
    g_fetched = exchange(g_fetched, "xy", 3)
    w_c_pairs = mm_rows(fetched, g_pairs)
    w_c_query = mm_rows(d_first_low, g_queries)
    g_first = g_sum_two + mm_back(g_queries, c_query)
    g_resid, d_gain_one, d_shift_one = norm_back(g_first, d_kept_one, d_g0)
    g_branch = g_resid.astype(BF16)
    w_d_out = mm_rows(d_mixed, g_branch)
    g_mixed = mm_back(g_branch, d_out).astype(BF16)
    g_attended = to_heads(g_mixed, parts, micro)
    g_own, *g_prior = attend_back(
        d_joined, d_prior, *tgt_info, d_logs, g_attended, heads, True, F32
    )
    g_back = [to_before(g, by) for g, by in zip(g_prior, range(REACH, 0, -1))]

    g_result = jnp.einsum(
        "mrs,mrd->msd",
        select,
        jnp.stack([v.reshape(asked, D) for v in g_fetched]),
        preferred_element_type=F32,
    ).reshape(micro * src_rows, D)
    g_sum, e_gain_two, e_shift_two = norm_back(g_result, e_kept_two, e_g1)
    g_second_low = g_sum.astype(BF16)
    w_e_down = mm_rows(e_active, g_second_low)
    ge_hidden = (mm_back(g_second_low, e_down) * gelu_slope(e_hidden)).astype(BF16)
    w_e_up = mm_rows(e_first_low, ge_hidden)
    g_first = g_sum + mm_back(ge_hidden, e_up)
    ge_resid, e_gain_one, e_shift_one = norm_back(g_first, e_kept_one, e_g0)
    ge_branch = ge_resid.astype(BF16)
    w_e_out = mm_rows(e_mixed, ge_branch)
    early_grads = [g.astype(BF16) for g in (w_c_query, w_c_pairs, w_c_out, w_d_up, w_e_up)]
    early_pack, ge_branch = lax.optimization_barrier(
        (jnp.concatenate(early_grads, axis=1), ge_branch)
    )
    early_sums = lax.psum_scatter(early_pack, EVERY, scatter_dimension=0, tiled=True)
    ge_mixed = mm_back(ge_branch, e_out).astype(BF16)
    ge_attended = to_heads(ge_mixed, parts, micro)
    (ge_joined,) = attend_back(
        e_joined, [], *src_info, e_logs, ge_attended, heads, False, BF16
    )
    ge_joined = ge_joined.reshape(parts * micro * src_rows, -1)
    w_e_qkv = mm_rows(source_all.reshape(-1, D), ge_joined).astype(BF16)
    g_source_all = mm_back(ge_joined, e_qkv_here).astype(BF16)

    *g_back, g_source_all, w_e_qkv = lax.optimization_barrier((*g_back, g_source_all, w_e_qkv))
    width = heads * 128
    g_pairs_own = g_own[..., :width] + sum(g.astype(F32) for g in g_back)
    g_joined = jnp.concatenate([g_pairs_own.astype(BF16), g_own[..., width:].astype(BF16)], axis=-1)
    g_joined = g_joined.reshape(parts * micro * tgt_rows, -1)
    w_d_qkv = mm_rows(target_all.reshape(-1, D), g_joined)
    g_target_all = mm_back(g_joined, d_qkv_here).astype(BF16)

    def pieces(value):
        return value.astype(BF16).reshape(devices, value.shape[0] // devices, value.shape[1])

    small_grads = pack_small(
        [
            all_columns(row_sum(ge_joined)[None], parts),
            row_sum(ge_hidden),
            all_columns(row_sum(g_joined)[None], parts),
            row_sum(g_hidden),
            row_sum(g_pairs),
            row_sum(ge_branch),
            e_gain_one,
            e_shift_one,
            row_sum(g_second_low),
            e_gain_two,
            e_shift_two,
            row_sum(g_branch),
            d_gain_one,
            d_shift_one,
            row_sum(g_queries),
            row_sum(g_branch_cross),
            d_gain_two,
            d_shift_two,
            row_sum(g_third),
            d_gain_three,
            d_shift_three,
        ],
        devices,
        heads,
    )
    late_sums = scatter(
        [
            pieces(all_columns(w_e_qkv, parts)),
            pieces(w_e_out),
            pieces(w_e_down),
            small_grads,
            pieces(all_columns(w_d_qkv.astype(BF16), parts)),
            pieces(w_d_out),
            pieces(w_d_down),
        ],
        "xyxyyyy",
        4,
        F32,
        [v.reshape(parts, -1, D) for v in (g_source_all, g_target_all)],
    )
    g_source, g_target = ge_resid + late_sums[7], g_resid + late_sums[8]
    (
        e_qkv_sum,
        e_out_sum,
        e_down_sum,
        small_sums,
        d_qkv_sum,
        d_out_sum,
        d_down_sum,
        c_query_sum,
        c_pairs_sum,
        c_out_sum,
        d_up_sum,
        e_up_sum,
    ) = finish(late_sums[:7], early_sums, heads)
    small_sums = small_sums[:, : encoder_gains.shape[1]]
    return (
        decoded.reshape(micro, tgt_rows, D),
        g_source.reshape(micro, src_rows, D),
        g_target.reshape(micro, tgt_rows, D),
        e_qkv_sum,
        e_out_sum,
        e_up_sum,
        e_down_sum,
        small_sums[0:2],
        small_sums[2:12],
        d_qkv_sum,
        d_out_sum,
        c_query_sum,
        c_pairs_sum,
        c_out_sum,
        d_up_sum,
        d_down_sum,
        small_sums[12:15],
        small_sums[15:SMALL_ROWS],
    )


def solution(mesh):
    in_specs = (
        P(None, ("seq", "head"), None),
        P(None, ("seq", "head"), None),
        P(None, ("seq", "head"), None),
        P(),
        P(),
        P(),
        P(("seq", "head"), None),
        P(("seq", "head"), None),
        P(("seq", "head"), None),
        P(("seq", "head"), None),
        P(None, ("seq", "head")),
        P(None, ("seq", "head")),
        P(("seq", "head"), None),
        P(("seq", "head"), None),
        P(("seq", "head"), None),
        P(("seq", "head"), None),
        P(("seq", "head"), None),
        P(("seq", "head"), None),
        P(("seq", "head"), None),
        P(None, ("seq", "head")),
        P(None, ("seq", "head")),
    )
    out_specs = (
        P(None, ("seq", "head"), None),
        P(None, ("seq", "head"), None),
        P(None, ("seq", "head"), None),
        P(("seq", "head"), None),
        P(("seq", "head"), None),
        P(("seq", "head"), None),
        P(("seq", "head"), None),
        P(None, ("seq", "head")),
        P(None, ("seq", "head")),
        P(("seq", "head"), None),
        P(("seq", "head"), None),
        P(("seq", "head"), None),
        P(("seq", "head"), None),
        P(("seq", "head"), None),
        P(("seq", "head"), None),
        P(("seq", "head"), None),
        P(None, ("seq", "head")),
        P(None, ("seq", "head")),
    )
    return jax.shard_map(shards, mesh=mesh, in_specs=in_specs, out_specs=out_specs, check_vma=False)
```

```python
import functools

import jax
import jax.numpy as jnp
from jax import lax
from jax.experimental import pallas as pl
from jax.experimental.pallas import tpu as pltpu
from jax.sharding import PartitionSpec as P

D = 768
HEADS = 12
HEAD_DIM = 64
FF = 3072
MICRO = 2
STRETCH = 1024
REACH = 2
EVERY = ("seq", "head")

EPSILON = 1e-05
NEGATIVE = -1e30
MESH = pl.DeviceIdType.MESH
F32 = jnp.float32
BF16 = jnp.bfloat16


def place():
    seq, head = lax.axis_index("seq"), lax.axis_index("head")
    return seq // 2, seq % 2, head // 2, head % 2


def device(z, y, x, c):
    return (z * 2 + y, x * 2 + c)


def shard(z, y, x, c):
    return ((z * 2 + y) * 2 + x) * 2 + c


def greet(z, y, x, c, ahead=False):
    barrier = pltpu.get_barrier_semaphore()
    def tell(who):
        pl.semaphore_signal(barrier, inc=1, device_id=who, device_id_type=MESH)
    tell(device(z, y, x, 1 - c))
    tell(device(z, y, 1 - x, c))
    tell(device(z, 1 - y, x, c))
    @pl.when(z > 0)
    def _():
        tell(device(z - 1, y, x, c))
    @pl.when(z < 3)
    def _():
        tell(device(z + 1, y, x, c))
    if ahead:

        @pl.when((y == 1) & (z < 3))
        def _():
            tell(device(z + 1, 0, x, c))

        @pl.when((y == 0) & (z > 0))
        def _():
            tell(device(z - 1, 1, x, c))

    below, above = (z + 2) // 3, (5 - z) // 3
    count = 3 + below + above
    if ahead:
        count = count + y * above + (1 - y) * below
    pl.semaphore_wait(barrier, count)


def gather_kernel(count, shared, reach, orders, *refs, greeted=False):
    every = count + shared
    ins, outs, refs = refs[:every], refs[every : 2 * every + reach], refs[2 * every + reach :]
    own_sem, recv_sem, send_sem, group_recv, group_send, ahead_send = refs
    z, y, x, c = place()
    if not greeted:
        greet(z, y, x, c, reach > 0)
    here = [(x, y) if order in "xX" else (y, x) for order in orders]

    def shard_of(a, zo, f, l):
        return shard(zo, l, f, c) if orders[a] in "xX" else shard(zo, f, l, c)

    def holder(a, zo, f, l, cc):
        return device(zo, l, f, cc) if orders[a] in "xX" else device(zo, f, l, cc)

    def copy(a, src, where, who, kind):
        return pltpu.make_async_remote_copy(
            src_ref=src,
            dst_ref=outs[a].at[where],
            send_sem=send_sem.at[a, kind, where // 2],
            recv_sem=recv_sem.at[a, where],
            device_id=who,
            device_id_type=MESH,
        )

    def forward(a, src, where, first, up, down):
        f, l = here[a]
        if first:
            copy(a, src, where, holder(a, z, 1 - f, l, c), 0).start()
        if up:

            @pl.when(z < 3)
            def _():
                copy(a, src, where, holder(a, z + 1, f, l, c), 1).start()

        if down:

            @pl.when(z > 0)
            def _():
                copy(a, src, where, holder(a, z - 1, f, l, c), 2).start()

        copy(a, src, where, holder(a, z, f, 1 - l, c), 3).start()
        copy(a, src, where, holder(a, z, f, l, 1 - c), 4).start()

    def arrived(a, where):
        copy(a, outs[a].at[where], where, device(z, y, x, 1 - c), 0).wait_recv()

    def pass_on(a, zo, fo, first, up, down):
        where = shard_of(a, zo, fo, here[a][1])
        arrived(a, where)
        forward(a, outs[a].at[where], where, first, up, down)

    def from_last(zo, other):
        for a in range(count):
            f, l = here[a]
            where = shard_of(a, zo, 1 - f if other else f, 1 - l)
            arrived(a, where)
            copy(a, outs[a].at[where], where, holder(a, z, f, l, 1 - c), 4).start()

    def group_copy(b, src, xo, co, kind, who):
        return pltpu.make_async_remote_copy(
            src_ref=src,
            dst_ref=outs[count + b].at[xo * 2 + co],
            send_sem=group_send.at[b, kind],
            recv_sem=group_recv.at[b, xo * 2 + co],
            device_id=who,
            device_id_type=MESH,
        )

    over, beside = device(z, y, 1 - x, c), device(z, y, x, 1 - c)
    seq = z * 2 + y

    def ahead_copy(by):
        return pltpu.make_async_remote_copy(
            src_ref=ins[every - 1],
            dst_ref=outs[every + by - 1].at[x * 2 + c],
            send_sem=ahead_send.at[by - 1],
            recv_sem=group_recv.at[shared + by - 1, x * 2 + c],
            device_id=(seq + by, x * 2 + c),
            device_id_type=MESH,
        )

    def spread(b, source):
        group_copy(b, source, x, c, 0, over).start()
        group_copy(b, source, x, c, 1, beside).start()

    def spread_on(b):
        landed = outs[count + b].at[(1 - x) * 2 + c]
        group_copy(b, landed, 1 - x, c, 2, beside).wait_recv()
        group_copy(b, landed, 1 - x, c, 2, beside).start()

    def spread_done(b, source):
        landed = outs[count + b].at[(1 - x) * 2 + c]
        group_copy(b, source, x, 1 - c, 1, beside).wait_recv()
        group_copy(b, source, 1 - x, 1 - c, 1, beside).wait_recv()
        group_copy(b, source, x, c, 0, over).wait_send()
        group_copy(b, source, x, c, 1, beside).wait_send()
        group_copy(b, landed, 1 - x, c, 2, beside).wait_send()

    kept = []
    for a in range(count):
        me = shard_of(a, z, *here[a])
        forward(a, ins[a], me, True, True, True)
        kept.append(pltpu.make_async_copy(ins[a], outs[a].at[me], own_sem.at[a]))
        kept[-1].start()
    for a in range(count):
        early = orders[a] in "XY"
        pass_on(a, z, 1 - here[a][0], False, not early, not early)
    from_last(z, False)
    from_last(z, True)
    for b in range(shared):
        spread(b, ins[count + b])
        kept.append(
            pltpu.make_async_copy(
                ins[count + b], outs[count + b].at[x * 2 + c], own_sem.at[count + b]
            )
        )
        kept[-1].start()
    for by in range(1, reach + 1):

        @pl.when(seq + by <= 7)
        def _():
            ahead_copy(by).start()

    for distance in (1, 2, 3):
        if distance == 3:
            for b in range(shared):
                spread_on(b)
            for by in range(1, reach + 1):

                @pl.when(seq >= by)
                def _():
                    ahead_copy(by).wait_recv()
                    spread(shared + by - 1, outs[every + by - 1].at[x * 2 + c])

        for below in (True, False):

            @pl.when((z >= distance) if below else (z + distance <= 3))
            def _():
                zo = z - distance if below else z + distance
                for a in range(count):
                    early = orders[a] in "XY"
                    pass_on(a, zo, here[a][0], early, below, not below)
                    if not early:
                        pass_on(a, zo, 1 - here[a][0], False, below, not below)

        for below in (True, False):

            @pl.when((z >= distance) if below else (z + distance <= 3))
            def _():
                zo = z - distance if below else z + distance
                for a in range(count):
                    if orders[a] in "XY":
                        pass_on(a, zo, 1 - here[a][0], False, False, False)
                from_last(zo, False)
                from_last(zo, True)

    def sent(a, where, kind):
        copy(a, ins[a], where, device(z, y, x, 1 - c), kind).wait_send()

    def cores(i, carry):
        for a in range(count):
            arrived(a, i * 2 + 1 - c)
            sent(a, i * 2 + c, 4)
        return carry

    lax.fori_loop(0, 16, cores, 0)
    for by in range(1, reach + 1):

        @pl.when(seq >= by)
        def _():
            spread_on(shared + by - 1)
            spread_done(shared + by - 1, outs[every + by - 1].at[x * 2 + c])

        @pl.when(seq + by <= 7)
        def _():
            ahead_copy(by).wait_send()

    for b in range(shared):
        spread_done(b, ins[count + b])
    for copied in kept:
        copied.wait()
    for a in range(count):
        f, l = here[a]
        early = orders[a] in "XY"
        if not early:
            sent(a, shard_of(a, z, f, l), 0)
        for zo in range(4):
            if early:
                sent(a, shard_of(a, zo, f, l), 0)
            for fo in range(2):
                sent(a, shard_of(a, zo, fo, l), 3)
            for fo in [f] if early else [0, 1]:

                @pl.when((zo <= z) & (z < 3))
                def _():
                    sent(a, shard_of(a, zo, fo, l), 1)

                @pl.when((zo >= z) & (z > 0))
                def _():
                    sent(a, shard_of(a, zo, fo, l), 2)


def traffic(arrays, share):
    size = sum(v.size * v.dtype.itemsize for v in arrays)
    return pl.CostEstimate(flops=0, transcendentals=0, bytes_accessed=size * share)


def gather_scratch(count, shared, reach):
    spreads = max(shared + reach, 1)
    shapes = [(count + shared,), (count, 32), (count, 5, 16), (spreads, 4), (spreads, 3)]
    return [pltpu.SemaphoreType.DMA(shape) for shape in shapes + [(max(reach, 1),)]]


def gather_all(arrays, orders, collective_id, group_arrays=(), reach=0):
    count, shared = len(arrays), len(group_arrays)
    every = [*arrays, *group_arrays]
    results = [(32, v) for v in arrays] + [(4, v) for v in group_arrays]
    results += [(4, v) for v in every[-1:] * reach]
    return pl.pallas_call(
        functools.partial(gather_kernel, count, shared, reach, orders),
        out_shape=[jax.ShapeDtypeStruct((n,) + v.shape, v.dtype) for n, v in results],
        in_specs=[pl.BlockSpec(memory_space=pl.ANY)] * len(every),
        out_specs=[pl.BlockSpec(memory_space=pl.ANY)] * len(results),
        scratch_shapes=gather_scratch(count, shared, reach),
        compiler_params=pltpu.CompilerParams(collective_id=collective_id, has_side_effects=True),
        cost_estimate=traffic(arrays, 500),
        name="gather_all",
    )(*every)


def scatter_kernel(count, shared, orders, *refs):
    every = count + shared
    grads, outs, refs = refs[:every], refs[every : 2 * every], refs[2 * every :]
    held, mine, near, mid, right, left = [refs[k * count : (k + 1) * count] for k in range(6)]
    refs = refs[6 * count :]
    mine_sem, core_sem, near_sem, mid_sem, right_sem, left_sem, group_sem, refs = (
        *refs[:7],
        refs[7:],
    )
    group_held, group_mine, group_last = [refs[k * shared : (k + 1) * shared] for k in range(3)]
    z, y, x, c = place()
    greet(z, y, x, c)
    half = z // 2
    here = [(x, y) if order in "xX" else (y, x) for order in orders]
    late = [order in "XY" for order in orders]

    def block(a, zt, f, l):
        return (zt * 2 + l) * 2 + f if orders[a] in "xX" else (zt * 2 + f) * 2 + l

    def remote(a, src, dst, sems, slot, who):
        return pltpu.make_async_remote_copy(
            src_ref=src,
            dst_ref=dst,
            send_sem=sems.at[a, 0, slot],
            recv_sem=sems.at[a, 1, slot],
            device_id=who,
            device_id_type=MESH,
        )

    def core_copy(a, q):
        who = device(z, y, x, 1 - c)
        return remote(a, grads[a].at[q * 2 + 1 - c], held[a].at[q], core_sem, q, who)

    def mine_copy(a, q):
        return pltpu.make_async_copy(grads[a].at[q * 2 + c], mine[a].at[q], mine_sem.at[a, q])

    def along(a, first):
        flip_x = (orders[a] in "xX") == first
        return device(z, y, 1 - x, c) if flip_x else device(z, 1 - y, x, c)

    def near_copy(a, q, slot):
        return remote(a, held[a].at[q], near[a].at[slot], near_sem, slot, along(a, True))

    def mid_copy(a, q, slot):
        return remote(a, held[a].at[q], mid[a].at[slot], mid_sem, slot, along(a, False))

    def right_copy(a, q, slot):
        return remote(a, held[a].at[q], right[a].at[slot], right_sem, slot, device(z + 1, y, x, c))

    def left_copy(a, q, slot):
        return remote(a, held[a].at[q], left[a].at[slot], left_sem, slot, device(z - 1, y, x, c))

    def far(k):
        return 3 - k + half * (2 * k - 3)

    def others(k):
        down = 3 - k - (k // 2) * z
        up = k + (k // 2) * (3 - z)
        return down + half * (up - down)

    def add(a, q, *terms):
        total = held[a][q].astype(F32)
        for ref, slot in terms:
            total = total + ref[slot].astype(F32)
        held[a][q] = total.astype(BF16)

    for side in (True, False):

        def start(i, carry, side=side):
            for a in range(count):
                f = here[a][0]
                q = block(a, far(i // 2), 1 - f if side else f, i % 2)
                core_copy(a, q).start()
                mine_copy(a, q).start()
            return carry

        lax.fori_loop(0, 8, start, 0)

    def group_copy(b, kind):
        if kind < 2:
            xt = 1 - x if kind == 0 else x
            return pltpu.make_async_remote_copy(
                src_ref=grads[count + b].at[xt * 2 + 1 - c],
                dst_ref=group_held[b].at[kind],
                send_sem=group_sem.at[b, 0, kind],
                recv_sem=group_sem.at[b, 1, kind],
                device_id=device(z, y, x, 1 - c),
                device_id_type=MESH,
            )
        if kind < 4:
            xt = 1 - x if kind == 2 else x
            return pltpu.make_async_copy(
                grads[count + b].at[xt * 2 + c], group_mine[b].at[kind - 2], group_sem.at[b, 0, kind]
            )
        return pltpu.make_async_remote_copy(
            src_ref=group_held[b].at[0],
            dst_ref=group_last[b],
            send_sem=group_sem.at[b, 0, 4],
            recv_sem=group_sem.at[b, 1, 4],
            device_id=device(z, y, 1 - x, c),
            device_id_type=MESH,
        )

    def in_pieces(rows, step):
        piece = rows // 8

        def body(i, carry):
            step(pl.ds(pl.multiple_of(i * piece, piece), piece))
            return carry

        lax.fori_loop(0, 8, body, 0)

    for b in range(shared):
        for kind in range(4):
            group_copy(b, kind).start()

    def first_step(i, carry):
        zt, lt = far(i // 2), i % 2
        for a in range(count):
            q = block(a, zt, 1 - here[a][0], lt)
            core_copy(a, q).wait_recv()
            mine_copy(a, q).wait()
            add(a, q, (mine[a], q))
            near_copy(a, q, zt * 2 + lt).start()
        return carry

    lax.fori_loop(0, 8, first_step, 0)
    for b in range(shared):
        group_copy(b, 0).wait_recv()
        group_copy(b, 2).wait()

        def to_other(cut, b=b):
            total = group_held[b][0, cut, :].astype(F32) + group_mine[b][0, cut, :].astype(F32)
            group_held[b][0, cut, :] = total.astype(BF16)

        in_pieces(group_last[b].shape[0], to_other)
        group_copy(b, 4).start()

    def summed(a, zt, lt):
        q = block(a, zt, here[a][0], lt)
        core_copy(a, q).wait_recv()
        mine_copy(a, q).wait()
        near_copy(a, q, zt * 2 + lt).wait_recv()
        add(a, q, (mine[a], q), (near[a], zt * 2 + lt))
        return q

    if any(late):

        def mid_step(i, carry):
            zt = far(i)
            for a in range(count):
                if late[a]:
                    mid_copy(a, summed(a, zt, 1 - here[a][1]), zt).start()
            return carry

        lax.fori_loop(0, 4, mid_step, 0)

    def slots(a, zt, lt):
        return (zt - 1, zt) if late[a] else ((zt - 1) * 2 + lt, zt * 2 + lt)

    def along_z(a, zt, lt):
        q = summed(a, zt, lt)
        if late[a]:
            mid_copy(a, q, zt).wait_recv()
            add(a, q, (mid[a], zt))
        up, down = slots(a, zt, lt)

        @pl.when(zt > z)
        def _():
            @pl.when(z > 0)
            def _():
                right_copy(a, q, up).wait_recv()
                add(a, q, (right[a], up))

            right_copy(a, q, up).start()

        @pl.when(zt < z)
        def _():
            @pl.when(z < 3)
            def _():
                left_copy(a, q, down).wait_recv()
                add(a, q, (left[a], down))

            left_copy(a, q, down).start()

    def z_step(k, carry):
        for a in range(count):
            if late[a]:
                along_z(a, others(k), here[a][1])
            else:
                along_z(a, others(k), 0)
                along_z(a, others(k), 1)
        return carry

    lax.fori_loop(0, 3, z_step, 0)

    def from_z(a, q, lt):
        up, down = slots(a, z, lt)

        @pl.when(z > 0)
        def _():
            right_copy(a, q, up).wait_recv()
            add(a, q, (right[a], up))

        @pl.when(z < 3)
        def _():
            left_copy(a, q, down).wait_recv()
            add(a, q, (left[a], down))

    for a in range(count):
        if not late[a]:
            lt = 1 - here[a][1]
            q = summed(a, z, lt)
            from_z(a, q, lt)
            mid_copy(a, q, 0).start()
    for a in range(count):
        lt = here[a][1]
        q = summed(a, z, lt)
        if late[a]:
            mid_copy(a, q, z).wait_recv()
            add(a, q, (mid[a], z))
        from_z(a, q, lt)
    for a in range(count):
        q = block(a, z, *here[a])
        total = held[a][q].astype(F32)
        if not late[a]:
            mid_copy(a, q, 0).wait_recv()
            total = total + mid[a][0].astype(F32)
        outs[a][...] = total.astype(outs[a].dtype)

    for b in range(shared):
        group_copy(b, 1).wait_recv()
        group_copy(b, 3).wait()
        group_copy(b, 4).wait_recv()

        def at_home(cut, b=b):
            total = group_held[b][1, cut, :].astype(F32) + group_mine[b][1, cut, :].astype(F32)
            outs[count + b][cut, :] = total + group_last[b][cut, :].astype(F32)

        in_pieces(group_last[b].shape[0], at_home)
        for kind in (0, 1, 4):
            group_copy(b, kind).wait_send()

    def sent_core(i, carry):
        for a in range(count):
            core_copy(a, i).wait_send()
        return carry

    lax.fori_loop(0, 16, sent_core, 0)

    def sent_near(i, carry):
        for a in range(count):
            near_copy(a, block(a, i // 2, 1 - here[a][0], i % 2), i).wait_send()
        return carry

    lax.fori_loop(0, 8, sent_near, 0)

    def sent_z(k, carry):
        zt = others(k)
        for a in range(count):
            for lt in [here[a][1]] if late[a] else [0, 1]:
                q = block(a, zt, here[a][0], lt)
                up, down = slots(a, zt, lt)

                @pl.when(zt > z)
                def _():
                    right_copy(a, q, up).wait_send()

                @pl.when(zt < z)
                def _():
                    left_copy(a, q, down).wait_send()

        return carry

    lax.fori_loop(0, 3, sent_z, 0)
    for a in range(count):
        f, l = here[a]
        if late[a]:
            for zt in range(4):
                mid_copy(a, block(a, zt, f, 1 - l), zt).wait_send()
        else:
            mid_copy(a, block(a, z, f, 1 - l), 0).wait_send()


def scatter_scratch(shapes, orders, shared):
    count = len(shapes) - shared
    late = [order in "XY" for order in orders]
    sizes = [[16, 16, 8, 4, 3, 3] if up else [16, 16, 8, 1, 6, 6] for up in late]
    scratch = []
    for k in range(6):
        scratch += [pltpu.VMEM((size[k],) + shape, BF16) for size, shape in zip(sizes, shapes)]
    scratch += [pltpu.SemaphoreType.DMA((count, 16))]
    scratch += [pltpu.SemaphoreType.DMA((count, 2, n)) for n in (16, 8, 4, 6, 6)]
    scratch += [pltpu.SemaphoreType.DMA((max(shared, 1), 2, 5))]
    scratch += [pltpu.VMEM((2,) + shape, BF16) for shape in shapes[count:]] * 2
    scratch += [pltpu.VMEM(shape, BF16) for shape in shapes[count:]]
    return scratch


def scatter_sum(arrays, orders, collective_id, out_dtype=F32, group_arrays=()):
    count, shared = len(arrays), len(group_arrays)
    shapes = [v.shape[1:] for v in (*arrays, *group_arrays)]
    return pl.pallas_call(
        functools.partial(scatter_kernel, count, shared, orders),
        out_shape=[jax.ShapeDtypeStruct(shape, out_dtype) for shape in shapes],
        in_specs=[pl.BlockSpec(memory_space=pl.ANY)] * len(shapes),
        out_specs=[pl.BlockSpec(memory_space=pltpu.VMEM)] * len(shapes),
        scratch_shapes=scatter_scratch(shapes, orders, shared),
        compiler_params=pltpu.CompilerParams(
            collective_id=collective_id, has_side_effects=True, vmem_limit_bytes=60 << 20
        ),
        cost_estimate=traffic(arrays, 1),
        name="scatter_sum",
    )(*arrays, *group_arrays)


def exchange_kernel(count, orders, *refs):
    grads, outs, sums = [refs[k * count : (k + 1) * count] for k in range(3)]
    refs = refs[3 * count :]
    scatter_refs = 6 * count + 7
    scatter_kernel(count, 0, orders, *grads, *sums, *refs[:scatter_refs])
    gather_kernel(count, 0, 0, orders, *sums, *outs, *refs[scatter_refs:], greeted=True)


def exchange_all(arrays, orders, collective_id):
    count = len(arrays)
    shapes = [v.shape[1:] for v in arrays]
    scratch = [pltpu.VMEM(shape, BF16) for shape in shapes]
    scratch += scatter_scratch(shapes, orders, 0) + gather_scratch(count, 0, 0)
    return pl.pallas_call(
        functools.partial(exchange_kernel, count, orders),
        out_shape=[jax.ShapeDtypeStruct(v.shape, v.dtype) for v in arrays],
        in_specs=[pl.BlockSpec(memory_space=pl.ANY)] * count,
        out_specs=[pl.BlockSpec(memory_space=pl.ANY)] * count,
        scratch_shapes=scratch,
        compiler_params=pltpu.CompilerParams(
            collective_id=collective_id, has_side_effects=True, vmem_limit_bytes=48 << 20
        ),
        cost_estimate=traffic(arrays, 2),
        name="exchange_all",
    )(*arrays)


def known_mesh():
    return lax.axis_size("seq") == 8 and lax.axis_size("head") == 4


def gather(arrays, orders, collective_id, group_arrays=(), reach=0):
    if known_mesh():
        return gather_all(arrays, orders, collective_id, group_arrays, reach)
    every = [lax.all_gather(v, EVERY, axis=0, tiled=False) for v in arrays]
    group = [lax.all_gather(v, "head", axis=0, tiled=False) for v in group_arrays]
    return every + group + [from_before(group[-1], by) for by in range(1, reach + 1)]


def scatter(arrays, orders, collective_id, out_dtype=F32, group_arrays=()):
    if known_mesh():
        return scatter_sum(arrays, orders, collective_id, out_dtype, group_arrays)
    return [
        lax.psum_scatter(v, axes, scatter_dimension=0, tiled=False).astype(out_dtype)
        for v, axes in [(v, EVERY) for v in arrays] + [(v, "head") for v in group_arrays]
    ]


def exchange(arrays, orders, collective_id):
    if known_mesh():
        return exchange_all(arrays, orders, collective_id)
    sums = [lax.psum_scatter(v, EVERY, scatter_dimension=0, tiled=False) for v in arrays]
    return [lax.all_gather(v, EVERY, axis=0, tiled=False) for v in sums]


def fill(target, refs, columns, scale=None):
    at = 0
    for ref in refs:
        rows = ref.shape[2]
        for p in range(ref.shape[0]):
            piece = ref[p, 0, :, columns]
            target[at : at + rows] = piece if scale is None else piece * scale
            at += rows


def spill(value, refs, columns):
    at = 0
    for ref in refs:
        rows = ref.shape[2]
        for p in range(ref.shape[0]):
            ref[p, 0, :, columns] = value[at : at + rows].astype(ref.dtype)
            at += rows


def across(left, right):
    return lax.dot_general(left, right, (((1,), (1,)), ((), ())), preferred_element_type=F32)


def down(left, right):
    return lax.dot_general(left, right, (((0,), (0,)), ((), ())), preferred_element_type=F32)


def soft_columns(scores):
    peak = jnp.max(scores, axis=0, keepdims=True)
    weights = jnp.exp(scores - peak)
    total = jnp.sum(weights, axis=0, keepdims=True)
    return weights * (1.0 / total), peak + jnp.log(total)


def score_grads(probs, grad_probs):
    delta = jnp.sum(probs * grad_probs, axis=0, keepdims=True)
    return (probs * (grad_probs - delta)).astype(BF16)


def allowed_pairs(key_ref, query_ref, start, tile, causal):
    doc_key, doc_query = key_ref[0, :, 0:1], query_ref[0, 0:1, pl.ds(start, tile)]
    allowed = doc_key == doc_query
    if causal:
        allowed &= key_ref[0, :, 1:2] <= query_ref[0, 1:2, pl.ds(start, tile)]
    return allowed


def attend_kernel(heads, tile, causal, *refs):
    key_ref, query_ref, own_ref = refs[:3]
    prior = refs[3:-6]
    out_ref, log_ref, key_s, value_s, query_s, result_s = refs[-6:]
    group = query_s.shape[0]
    for h in range(heads):
        fill(key_s, (*prior, own_ref), slice(h * 128, h * 128 + 64))
        fill(value_s, (*prior, own_ref), slice(h * 128 + 64, h * 128 + 128))
        at = heads * 128 + h * 64
        fill(query_s, (own_ref,), slice(at, at + 64), 0.125)
        values = value_s[...].T

        def step(i, carry):
            start = pl.multiple_of(i * tile, tile)
            allowed = allowed_pairs(key_ref, query_ref, start, tile, causal)
            scores = across(key_s[...], query_s[pl.ds(start, tile), :])
            probs, log_total = soft_columns(jnp.where(allowed, scores, NEGATIVE))
            made = jnp.dot(values, probs.astype(BF16), preferred_element_type=F32)
            result_s[pl.ds(start, tile), :] = made.astype(BF16).T
            log_ref[0, h : h + 1, pl.ds(start, tile)] = log_total
            return carry

        lax.fori_loop(0, group // tile, step, 0)
        spill(result_s[...], (out_ref,), slice(h * 64, h * 64 + 64))


def rows_spec(shape):
    return pl.BlockSpec((shape[0], 1) + shape[2:], lambda m: (0, m, 0, 0))


def whole_spec(shape):
    return pl.BlockSpec((1,) + shape[1:], lambda m: (m, 0, 0))


def attend(joined, prior, key_info, query_info, heads, causal, tile=512):
    parts, micro, rows, _ = joined.shape
    group = parts * rows
    keys = key_info.shape[1]
    out, logs = (parts, micro, rows, heads * 64), (micro, heads, group)
    return pl.pallas_call(
        functools.partial(attend_kernel, heads, tile, causal),
        grid=(micro,),
        out_shape=[jax.ShapeDtypeStruct(out, BF16), jax.ShapeDtypeStruct(logs, F32)],
        in_specs=[whole_spec(key_info.shape), whole_spec(query_info.shape), rows_spec(joined.shape)]
        + [rows_spec(p.shape) for p in prior],
        out_specs=[rows_spec(out), whole_spec(logs)],
        scratch_shapes=[
            pltpu.VMEM((keys, 64), BF16),
            pltpu.VMEM((keys, 64), BF16),
            pltpu.VMEM((group, 64), BF16),
            pltpu.VMEM((group, 64), BF16),
        ],
        compiler_params=pltpu.CompilerParams(vmem_limit_bytes=48 << 20),
        cost_estimate=pl.CostEstimate(
            flops=16 * micro * heads * group * keys * 128,
            transcendentals=micro * heads * group * keys,
            bytes_accessed=joined.size * 4,
        ),
        name="attend",
    )(key_info, query_info, joined, *prior)


def attend_back_kernel(heads, tile, causal, count, *refs):
    key_ref, query_ref, own_ref, log_ref, grad_ref = refs[:5]
    prior = refs[5 : 5 + count]
    out_ref, *prior_out = refs[5 + count : 6 + 2 * count]
    key_s, value_s, query_s, grad_s, gk_s, gv_s, result_s = refs[6 + 2 * count :]
    group = query_s.shape[0]
    for h in range(heads):
        key_cut, value_cut = slice(h * 128, h * 128 + 64), slice(h * 128 + 64, h * 128 + 128)
        fill(key_s, (*prior, own_ref), key_cut)
        fill(value_s, (*prior, own_ref), value_cut)
        query_cut = slice(heads * 128 + h * 64, heads * 128 + h * 64 + 64)
        fill(query_s, (own_ref,), query_cut, 0.125)
        fill(grad_s, (grad_ref,), slice(h * 64, h * 64 + 64))
        gk_s[...] = jnp.zeros_like(gk_s)
        gv_s[...] = jnp.zeros_like(gv_s)
        keys = key_s[...].T

        def step(i, carry):
            start = pl.multiple_of(i * tile, tile)
            here = pl.ds(start, tile)
            allowed = allowed_pairs(key_ref, query_ref, start, tile, causal)
            query, grad_out = query_s[here, :], grad_s[here, :]
            scores = jnp.where(allowed, across(key_s[...], query), NEGATIVE)
            probs = jnp.exp(scores - log_ref[0, h : h + 1, here])
            grad_scores = score_grads(probs, across(value_s[...], grad_out))
            gv_s[...] += jnp.dot(probs.astype(BF16), grad_out, preferred_element_type=F32)
            gk_s[...] += jnp.dot(grad_scores, query, preferred_element_type=F32)
            made = jnp.dot(keys, grad_scores, preferred_element_type=F32)
            result_s[here, :] = made.T * 0.125
            return carry

        lax.fori_loop(0, group // tile, step, 0)
        spill(result_s[...], (out_ref,), query_cut)
        spill(gk_s[...], (*prior_out, out_ref), key_cut)
        spill(gv_s[...], (*prior_out, out_ref), value_cut)
    for p in range(out_ref.shape[0]):
        out_ref[p, 0, :, heads * 192 :] = jnp.zeros(
            (out_ref.shape[2], out_ref.shape[3] - heads * 192), out_ref.dtype
        )


def attend_back(
    joined, prior, key_info, query_info, logs, grad, heads, causal, out_dtype, tile=512
):
    parts, micro, rows, _ = joined.shape
    group = parts * rows
    keys = key_info.shape[1]
    return pl.pallas_call(
        functools.partial(attend_back_kernel, heads, tile, causal, len(prior)),
        grid=(micro,),
        out_shape=[jax.ShapeDtypeStruct(joined.shape, out_dtype)]
        + [jax.ShapeDtypeStruct(p.shape, BF16) for p in prior],
        in_specs=[
            whole_spec(key_info.shape),
            whole_spec(query_info.shape),
            rows_spec(joined.shape),
            whole_spec(logs.shape),
            rows_spec(grad.shape),
        ]
        + [rows_spec(p.shape) for p in prior],
        out_specs=[rows_spec(joined.shape)] + [rows_spec(p.shape) for p in prior],
        scratch_shapes=[
            pltpu.VMEM((keys, 64), BF16),
            pltpu.VMEM((keys, 64), BF16),
            pltpu.VMEM((group, 64), BF16),
            pltpu.VMEM((group, 64), BF16),
            pltpu.VMEM((keys, 64), F32),
            pltpu.VMEM((keys, 64), F32),
            pltpu.VMEM((group, 64), F32),
        ],
        compiler_params=pltpu.CompilerParams(vmem_limit_bytes=48 << 20),
        cost_estimate=pl.CostEstimate(
            flops=24 * micro * heads * group * keys * 128,
            transcendentals=micro * heads * group * keys,
            bytes_accessed=joined.size * 6,
        ),
        name="attend_back",
    )(key_info, query_info, joined, logs, grad, *prior)


def cross_kernel(query_ref, pairs_ref, out_ref, log_ref):
    for i in range(D // 128):
        outs = []
        for h in range(2):
            at = i * 128 + h * 64
            query, keys = query_ref[0, :, at : at + 64] * 0.125, pairs_ref[0, :, at : at + 64]
            values = pairs_ref[0, :, D + at : D + at + 64]
            probs, log_total = soft_columns(across(keys, query))
            outs.append(down(probs.astype(BF16), values))
            log_ref[0, i * 2 + h : i * 2 + h + 1, :] = log_total
        out_ref[0, :, i * 128 : i * 128 + 128] = jnp.concatenate(outs, axis=1).astype(BF16)


def cross(query, pairs):
    micro, rows, _ = query.shape
    keys = pairs.shape[1]
    logs = (micro, HEADS, rows)
    return pl.pallas_call(
        cross_kernel,
        grid=(micro,),
        out_shape=[jax.ShapeDtypeStruct(query.shape, BF16), jax.ShapeDtypeStruct(logs, F32)],
        in_specs=[whole_spec(query.shape), whole_spec(pairs.shape)],
        out_specs=[whole_spec(query.shape), whole_spec(logs)],
        compiler_params=pltpu.CompilerParams(vmem_limit_bytes=48 << 20),
        cost_estimate=pl.CostEstimate(
            flops=16 * micro * HEADS * rows * keys * 128,
            transcendentals=micro * HEADS * rows * keys,
            bytes_accessed=pairs.size * 2,
        ),
        name="cross",
    )(query, pairs)


def cross_back_kernel(
    query_ref, pairs_ref, log_ref, grad_ref, grad_query_ref, grad_pairs_ref
):
    for i in range(D // 128):
        query_parts, key_parts, value_parts = [], [], []
        for h in range(2):
            at = i * 128 + h * 64
            cut = slice(at, at + 64)
            query, keys = query_ref[0, :, cut] * 0.125, pairs_ref[0, :, cut]
            values, grad_out = pairs_ref[0, :, D + at : D + at + 64], grad_ref[0, :, cut]
            probs = jnp.exp(across(keys, query) - log_ref[0, i * 2 + h : i * 2 + h + 1, :])
            grad_scores = score_grads(probs, across(values, grad_out))
            value_parts.append(jnp.dot(probs.astype(BF16), grad_out, preferred_element_type=F32))
            key_parts.append(jnp.dot(grad_scores, query, preferred_element_type=F32))
            query_parts.append(jnp.dot(keys.T, grad_scores, preferred_element_type=F32))
        cut = slice(i * 128, i * 128 + 128)
        made = jnp.concatenate(query_parts, axis=0).T * 0.125
        grad_query_ref[0, :, cut] = made.astype(BF16)
        grad_pairs_ref[0, :, cut] = jnp.concatenate(key_parts, axis=1).astype(BF16)
        cut = slice(D + i * 128, D + i * 128 + 128)
        grad_pairs_ref[0, :, cut] = jnp.concatenate(value_parts, axis=1).astype(BF16)


def cross_back(query, pairs, logs, grad):
    micro, rows, _ = query.shape
    keys = pairs.shape[1]
    return pl.pallas_call(
        cross_back_kernel,
        grid=(micro,),
        out_shape=[jax.ShapeDtypeStruct(query.shape, BF16), jax.ShapeDtypeStruct(pairs.shape, BF16)],
        in_specs=[whole_spec(v.shape) for v in (query, pairs, logs, grad)],
        out_specs=[whole_spec(query.shape), whole_spec(pairs.shape)],
        compiler_params=pltpu.CompilerParams(vmem_limit_bytes=48 << 20),
        cost_estimate=pl.CostEstimate(
            flops=24 * micro * HEADS * rows * keys * 128,
            transcendentals=micro * HEADS * rows * keys,
            bytes_accessed=pairs.size * 4,
        ),
        name="cross_back",
    )(query, pairs, logs, grad)


SMALL_ROWS = 29
SINGLES = (4, 0, 5, 10, 1, 11, 17, 12, 18, 19, 21, 13, 22, 27, 14, 28)


def head_places(head, heads):
    base = head // heads * joined_width(heads) + head % heads * 64
    return base + head % heads * 64 + 64, base + heads * 128


def joined_width(heads):
    return (heads * 192 + 127) // 128 * 128


def unpack_kernel(width, heads, pack_ref, *refs):
    e_joined, e_hidden, d_joined, d_hidden, pair_bias = refs[:5]
    singles, full = refs[5:-1], refs[-1]
    for d in range(pack_ref.shape[0]):
        full[:, d * width : d * width + width] = pack_ref[d, :, 0:width].astype(F32)
    for target, row in ((e_joined, 2), (d_joined, 15)):
        target[...] = jnp.zeros_like(target)
        for head in range(HEADS):
            value_at, query_at = head_places(head, heads)
            cut = slice(head * 64, head * 64 + 64)
            target[:, query_at : query_at + 64] = full[row : row + 1, cut]
            target[:, value_at : value_at + 64] = full[row + 1 : row + 2, cut]
    for target, row in ((e_hidden, 6), (d_hidden, 23)):
        for k in range(FF // D):
            target[:, k * D : k * D + D] = full[row + k : row + k + 1, :]
    pair_bias[:, 0:D] = jnp.zeros((1, D), F32)
    pair_bias[:, D:] = full[20:21, :]
    for target, row in zip(singles, SINGLES):
        target[...] = full[row : row + 1, :]


def unpack_small(packs, heads):
    devices = packs.shape[0]
    joined = joined_width(heads) * (HEADS // heads)
    widths = [joined, FF, joined, FF, 2 * D] + [D] * len(SINGLES)
    return pl.pallas_call(
        functools.partial(unpack_kernel, D // devices, heads),
        out_shape=[jax.ShapeDtypeStruct((1, w), F32) for w in widths],
        scratch_shapes=[pltpu.VMEM((32, D), F32)],
        name="unpack_small",
    )(packs)


def pack_kernel(width, heads, count, *refs):
    e_joined, e_hidden, d_joined, d_hidden, pair_sum = refs[:5]
    singles, out_ref, full = refs[5 : 5 + count], refs[-2], refs[-1]
    full[...] = jnp.zeros_like(full)
    for source, row in ((e_joined, 2), (d_joined, 15)):
        for head in range(HEADS):
            value_at, query_at = head_places(head, heads)
            cut = slice(head * 64, head * 64 + 64)
            full[row : row + 1, cut] = source[:, query_at : query_at + 64]
            full[row + 1 : row + 2, cut] = source[:, value_at : value_at + 64]
    for source, row in ((e_hidden, 6), (d_hidden, 23)):
        for k in range(FF // D):
            full[row + k : row + k + 1, :] = source[k * D : k * D + D].reshape(1, D)
    full[20:21, :] = pair_sum[D:].reshape(1, D)
    for source, row in zip(singles, SINGLES):
        full[row : row + 1, :] = source[...].reshape(1, D)
    out_ref[...] = jnp.zeros_like(out_ref)
    for d in range(out_ref.shape[0]):
        out_ref[d, :, 0:width] = full[:, d * width : d * width + width].astype(BF16)


def pack_small(vectors, devices, heads):
    return pl.pallas_call(
        functools.partial(pack_kernel, D // devices, heads, len(SINGLES)),
        out_shape=jax.ShapeDtypeStruct((devices, 32, 128), BF16),
        scratch_shapes=[pltpu.VMEM((32, D), F32)],
        name="pack_small",
    )(*vectors)


def finish_kernel(heads, *refs):
    late, pack, outs = refs[:7], refs[7], refs[8:]
    for k in (0, 4):
        for head in range(HEADS):
            value_at, query_at = head_places(head, heads)
            for n, at in enumerate((query_at, value_at - 64, value_at)):
                start = head * 192 + n * 64
                outs[k][:, start : start + 64] = late[k][:, at : at + 64]
    for k in (1, 2, 3, 5, 6):
        outs[k][...] = late[k][...]
    at = 0
    for target in outs[7:]:
        width = target.shape[1]
        target[...] = pack[:, at : at + width].astype(F32)
        at += width


def finish(late, early, heads):
    rows = late[0].shape[0]
    shapes = [v.shape for v in late]
    shapes[0] = shapes[4] = (rows, 3 * D)
    shapes += [(rows, width) for width in (D, 2 * D, D, FF, FF)]
    return pl.pallas_call(
        functools.partial(finish_kernel, heads),
        out_shape=[jax.ShapeDtypeStruct(shape, F32) for shape in shapes],
        compiler_params=pltpu.CompilerParams(vmem_limit_bytes=48 << 20),
        name="finish",
    )(*late, early)


def norm(resid, gain, shift):
    center = resid - jnp.mean(resid, axis=-1, keepdims=True)
    scale = lax.rsqrt(jnp.mean(center * center, axis=-1, keepdims=True) + EPSILON)
    hat = center * scale
    return hat * gain + shift, (hat, scale)


def norm_back(grad, kept, gain):
    hat, scale = kept
    inner = grad * gain
    grad_resid = scale * (
        inner
        - jnp.mean(inner, axis=-1, keepdims=True)
        - hat * jnp.mean(inner * hat, axis=-1, keepdims=True)
    )
    return grad_resid, jnp.sum(grad * hat, axis=0), jnp.sum(grad, axis=0)


def gelu(value):
    return value * (1.0 + lax.erf(value * 0.7071067811865476)) * 0.5


def gelu_slope(value):
    bell = jnp.exp(value * value * -0.5) * 0.3989422804014327
    return 0.5 * (1.0 + lax.erf(value * 0.7071067811865476)) + value * bell


def mm(left, right):
    return jnp.dot(left, right, preferred_element_type=F32)


def mm_rows(left, right):
    return lax.dot_general(left, right, (((0,), (0,)), ((), ())), preferred_element_type=F32)


def mm_back(left, right):
    return lax.dot_general(left, right, (((1,), (1,)), ((), ())), preferred_element_type=F32)


def row_sum(value):
    return jnp.sum(value.astype(F32), axis=0)


def doc_starts(lengths):
    count = lengths.shape[1]
    before = jnp.arange(count)[None, :] < jnp.arange(count)[:, None]
    return jnp.sum(jnp.where(before[None], lengths[:, None, :], 0), axis=2)


def doc_ids(starts, positions):
    return jnp.sum((starts[:, None, :] <= positions[None, :, None]).astype(jnp.int32), axis=2) - 1


def key_and_query_info(starts, key_pos, query_pos):
    key_docs, query_docs = doc_ids(starts, key_pos), doc_ids(starts, query_pos)
    micro = starts.shape[0]
    key_info = jnp.stack(
        [key_docs, jnp.broadcast_to(key_pos, (micro,) + key_pos.shape)], axis=2
    )
    query_info = jnp.stack(
        [query_docs, jnp.broadcast_to(query_pos, (micro,) + query_pos.shape)], axis=1
    )
    return key_info, query_info


def by_group(weight, parts):
    rows = weight.shape[0]
    split = weight.reshape(rows, parts, HEADS // parts, 3, HEAD_DIM)
    pairs = split[:, :, :, 1:].reshape(rows, parts, -1)
    query = split[:, :, :, 0].reshape(rows, parts, -1)
    width = joined_width(HEADS // parts)
    blank = jnp.zeros((rows, parts, width - pairs.shape[2] - query.shape[2]), weight.dtype)
    return jnp.concatenate([pairs, query, blank], axis=2).reshape(rows, parts * width)


def by_head(grad, parts):
    rows, heads = grad.shape[0], HEADS // parts
    split = grad.reshape(rows, parts, -1)
    pairs = split[:, :, : heads * 128].reshape(rows, parts, heads, 2, HEAD_DIM)
    query = split[:, :, heads * 128 : heads * 192].reshape(rows, parts, heads, 1, HEAD_DIM)
    return jnp.concatenate([query, pairs], axis=3).reshape(rows, 3 * D)


def my_columns(full, parts):
    width = full.shape[1] // parts
    return lax.dynamic_slice_in_dim(full, lax.axis_index("head") * width, width, 1)


def all_columns(mine, parts):
    rows, width = mine.shape
    full = jnp.zeros((rows, width * parts), mine.dtype)
    return lax.dynamic_update_slice_in_dim(full, mine, lax.axis_index("head") * width, 1)


def to_tokens(value):
    parts, micro, rows, columns = value.shape
    got = lax.all_to_all(value, "head", split_axis=0, concat_axis=0, tiled=True)
    return got.transpose(1, 2, 0, 3).reshape(micro * rows, parts * columns)


def to_heads(value, parts, micro):
    rows = value.shape[0] // micro
    split = value.reshape(micro, rows, parts, -1).transpose(2, 0, 1, 3)
    return lax.all_to_all(split, "head", split_axis=0, concat_axis=0, tiled=True)


def from_before(value, by):
    count = lax.axis_size("seq")
    return lax.ppermute(value, "seq", [(i, i + by) for i in range(count - by)])


def to_before(value, by):
    count = lax.axis_size("seq")
    return lax.ppermute(value, "seq", [(i + by, i) for i in range(count - by)])


def shards(
    source,
    target,
    cotangent,
    src_lengths,
    tgt_lengths,
    retrieved,
    encoder_qkv,
    encoder_out,
    encoder_up,
    encoder_down,
    encoder_gains,
    encoder_biases,
    decoder_qkv,
    decoder_out,
    cross_query,
    cross_keyvalue,
    cross_out,
    decoder_up,
    decoder_down,
    decoder_gains,
    decoder_biases,
):
    micro, src_rows, _ = source.shape
    tgt_rows = target.shape[1]
    parts = lax.axis_size("head")
    devices = parts * lax.axis_size("seq")
    seq, me = lax.axis_index("seq"), lax.axis_index(EVERY)
    src_group, tgt_group = src_rows * parts, tgt_rows * parts
    asked = retrieved.shape[1]
    source_rows = source.reshape(micro * src_rows, D)
    target_rows = target.reshape(micro * tgt_rows, D)

    heads = HEADS // parts
    small = jnp.concatenate([encoder_gains, encoder_biases, decoder_gains, decoder_biases], axis=0)
    small = jnp.pad(small, ((0, 32 - SMALL_ROWS), (0, 128 - small.shape[1])))
    encoder_full = gather(
        [by_group(encoder_qkv, parts), encoder_out, encoder_up, encoder_down, small],
        "yxxxx",
        0,
        [source, target],
        REACH,
    )
    source_all, target_all, *target_before = encoder_full[5:]
    decoder_parts = [
        by_group(decoder_qkv, parts),
        decoder_out,
        cross_query,
        cross_keyvalue,
        cross_out,
        decoder_up,
    ]
    decoder_pack, small_full = lax.optimization_barrier(
        (jnp.concatenate(decoder_parts, axis=1), encoder_full[4])
    )
    decoder_full = lax.all_gather(decoder_pack, EVERY, axis=0, tiled=True)
    d_down = lax.all_gather(decoder_down, EVERY, axis=0, tiled=True)
    e_qkv, e_out, e_up, e_down = [v.reshape(-1, v.shape[-1]) for v in encoder_full[:4]]
    e_bias, e_hidden_bias, d_bias, d_hidden_bias, pair_bias, *singles = unpack_small(
        small_full, heads
    )
    e_b2, e_g0, e_b3, e_b8, e_g1, e_b9 = singles[:6]
    d_b2, d_g0, d_b3, d_b4, d_b6, d_g1, d_b7, d_b12, d_g2, d_b13 = singles[6:]

    src_pos = seq * src_group + jnp.arange(src_group, dtype=jnp.int32)
    src_info = key_and_query_info(doc_starts(src_lengths), src_pos, src_pos)
    tgt_pos = seq * tgt_group + jnp.arange(tgt_group, dtype=jnp.int32)
    tgt_key_pos = (seq - REACH) * tgt_group + jnp.arange((REACH + 1) * tgt_group, dtype=jnp.int32)
    tgt_info = key_and_query_info(doc_starts(tgt_lengths), tgt_key_pos, tgt_pos)

    e_qkv_here = my_columns(e_qkv, parts)
    e_joined = (mm(source_all.reshape(-1, D), e_qkv_here) + my_columns(e_bias, parts)).astype(BF16)
    e_joined = e_joined.reshape(parts, micro, src_rows, -1)
    e_attended, e_logs = attend(e_joined, [], *src_info, heads, False)
    e_mixed = to_tokens(e_attended)
    e_first, e_kept_one = norm(
        source_rows.astype(F32) + mm(e_mixed, e_out) + e_b2, e_g0, e_b3
    )
    e_first_low = e_first.astype(BF16)
    e_hidden = mm(e_first_low, e_up) + e_hidden_bias
    e_active = gelu(e_hidden).astype(BF16)
    e_result, e_kept_two = norm(e_first + mm(e_active, e_down) + e_b8, e_g1, e_b9)

    src_own = me * src_rows + jnp.arange(src_rows, dtype=jnp.int32)
    select = (retrieved[:, :, None] == src_own[None, None, :]).astype(BF16)
    picked = jnp.einsum(
        "mrs,msd->mrd",
        select,
        e_result.astype(BF16).reshape(micro, src_rows, D),
        preferred_element_type=F32,
    ).astype(BF16)
    picked = [picked[m].reshape(devices, asked // devices, D) for m in range(micro)]
    fetched = exchange(picked, "xy", 2)
    fetched = jnp.concatenate([v.reshape(asked, D) for v in fetched], axis=0)
    decoder_full, fetched = lax.optimization_barrier((decoder_full, fetched))
    ends = [0]
    for part in decoder_parts:
        ends.append(ends[-1] + part.shape[1])
    d_qkv, d_out, c_query, c_pairs, c_out, d_up = [
        decoder_full[:, start:end] for start, end in zip(ends, ends[1:])
    ]

    d_qkv_here = my_columns(d_qkv, parts)
    d_joined = (mm(target_all.reshape(-1, D), d_qkv_here) + my_columns(d_bias, parts)).astype(BF16)
    d_joined = d_joined.reshape(parts, micro, tgt_rows, -1)
    pair_weights, pair_shift = d_qkv_here[:, : heads * 128], my_columns(d_bias, parts)[:, : heads * 128]
    d_prior = []
    for by in range(REACH, 0, -1):
        before = (mm(target_before[by - 1].reshape(-1, D), pair_weights) + pair_shift).astype(BF16)
        before = jnp.where(seq >= by, before, jnp.zeros_like(before))
        d_prior.append(before.reshape(parts, micro, tgt_rows, -1))
    d_attended, d_logs = attend(d_joined, d_prior, *tgt_info, heads, True)
    d_mixed = to_tokens(d_attended)
    d_first, d_kept_one = norm(
        target_rows.astype(F32) + mm(d_mixed, d_out) + d_b2, d_g0, d_b3
    )
    d_first_low = d_first.astype(BF16)
    queries = (mm(d_first_low, c_query) + d_b4).astype(BF16).reshape(micro, tgt_rows, D)

    pairs = (mm(fetched, c_pairs) + pair_bias).astype(BF16).reshape(micro, asked, 2 * D)

    crossed_rows, cross_logs = cross(queries, pairs)
    crossed = crossed_rows.reshape(micro * tgt_rows, D)
    d_second, d_kept_two = norm(d_first + mm(crossed, c_out) + d_b6, d_g1, d_b7)
    d_second_low = d_second.astype(BF16)
    d_hidden = mm(d_second_low, d_up) + d_hidden_bias
    d_active = gelu(d_hidden).astype(BF16)
    decoded, d_kept_three = norm(d_second + mm(d_active, d_down) + d_b12, d_g2, d_b13)

    grad = cotangent.reshape(micro * tgt_rows, D).astype(F32)
    g_sum, d_gain_three, d_shift_three = norm_back(grad, d_kept_three, d_g2)
    g_third = g_sum.astype(BF16)
    w_d_down = mm_rows(d_active, g_third)
    g_hidden = (mm_back(g_third, d_down) * gelu_slope(d_hidden)).astype(BF16)
    w_d_up = mm_rows(d_second_low, g_hidden)
    g_second = g_sum + mm_back(g_hidden, d_up)
    g_sum_two, d_gain_two, d_shift_two = norm_back(g_second, d_kept_two, d_g1)
    g_branch_cross = g_sum_two.astype(BF16)
    w_c_out = mm_rows(crossed, g_branch_cross)
    g_crossed = mm_back(g_branch_cross, c_out).astype(BF16).reshape(micro, tgt_rows, D)
    g_queries, g_pairs = cross_back(queries, pairs, cross_logs, g_crossed)
    g_queries = g_queries.reshape(micro * tgt_rows, D)
    g_pairs = g_pairs.reshape(micro * asked, 2 * D)
    g_fetched = mm_back(g_pairs, c_pairs).astype(BF16).reshape(micro, asked, D)
    g_fetched = [g_fetched[m].reshape(devices, asked // devices, D) for m in range(micro)]
    g_fetched = exchange(g_fetched, "xy", 3)
    w_c_pairs = mm_rows(fetched, g_pairs)
    w_c_query = mm_rows(d_first_low, g_queries)
    g_first = g_sum_two + mm_back(g_queries, c_query)
    g_resid, d_gain_one, d_shift_one = norm_back(g_first, d_kept_one, d_g0)
    g_branch = g_resid.astype(BF16)
    w_d_out = mm_rows(d_mixed, g_branch)
    g_mixed = mm_back(g_branch, d_out).astype(BF16)
    g_attended = to_heads(g_mixed, parts, micro)
    g_own, *g_prior = attend_back(
        d_joined, d_prior, *tgt_info, d_logs, g_attended, heads, True, F32
    )
    g_back = [to_before(g, by) for g, by in zip(g_prior, range(REACH, 0, -1))]

    g_result = jnp.einsum(
        "mrs,mrd->msd",
        select,
        jnp.stack([v.reshape(asked, D) for v in g_fetched]),
        preferred_element_type=F32,
    ).reshape(micro * src_rows, D)
    g_sum, e_gain_two, e_shift_two = norm_back(g_result, e_kept_two, e_g1)
    g_second_low = g_sum.astype(BF16)
    w_e_down = mm_rows(e_active, g_second_low)
    ge_hidden = (mm_back(g_second_low, e_down) * gelu_slope(e_hidden)).astype(BF16)
    w_e_up = mm_rows(e_first_low, ge_hidden)
    g_first = g_sum + mm_back(ge_hidden, e_up)
    ge_resid, e_gain_one, e_shift_one = norm_back(g_first, e_kept_one, e_g0)
    ge_branch = ge_resid.astype(BF16)
    w_e_out = mm_rows(e_mixed, ge_branch)
    early_grads = [g.astype(BF16) for g in (w_c_query, w_c_pairs, w_c_out, w_d_up, w_e_up)]
    early_pack, ge_branch = lax.optimization_barrier(
        (jnp.concatenate(early_grads, axis=1), ge_branch)
    )
    early_sums = lax.psum_scatter(early_pack, EVERY, scatter_dimension=0, tiled=True)
    ge_mixed = mm_back(ge_branch, e_out).astype(BF16)
    ge_attended = to_heads(ge_mixed, parts, micro)
    (ge_joined,) = attend_back(
        e_joined, [], *src_info, e_logs, ge_attended, heads, False, BF16
    )
    ge_joined = ge_joined.reshape(parts * micro * src_rows, -1)
    w_e_qkv = mm_rows(source_all.reshape(-1, D), ge_joined).astype(BF16)
    g_source_all = mm_back(ge_joined, e_qkv_here).astype(BF16)

    *g_back, g_source_all, w_e_qkv = lax.optimization_barrier((*g_back, g_source_all, w_e_qkv))
    width = heads * 128
    g_pairs_own = g_own[..., :width] + sum(g.astype(F32) for g in g_back)
    g_joined = jnp.concatenate([g_pairs_own.astype(BF16), g_own[..., width:].astype(BF16)], axis=-1)
    g_joined = g_joined.reshape(parts * micro * tgt_rows, -1)
    w_d_qkv = mm_rows(target_all.reshape(-1, D), g_joined)
    g_target_all = mm_back(g_joined, d_qkv_here).astype(BF16)

    def pieces(value):
        return value.astype(BF16).reshape(devices, value.shape[0] // devices, value.shape[1])

    small_grads = pack_small(
        [
            all_columns(row_sum(ge_joined)[None], parts),
            row_sum(ge_hidden),
            all_columns(row_sum(g_joined)[None], parts),
            row_sum(g_hidden),
            row_sum(g_pairs),
            row_sum(ge_branch),
            e_gain_one,
            e_shift_one,
            row_sum(g_second_low),
            e_gain_two,
            e_shift_two,
            row_sum(g_branch),
            d_gain_one,
            d_shift_one,
            row_sum(g_queries),
            row_sum(g_branch_cross),
            d_gain_two,
            d_shift_two,
            row_sum(g_third),
            d_gain_three,
            d_shift_three,
        ],
        devices,
        heads,
    )
    late_sums = scatter(
        [
            pieces(all_columns(w_e_qkv, parts)),
            pieces(w_e_out),
            pieces(w_e_down),
            small_grads,
            pieces(all_columns(w_d_qkv.astype(BF16), parts)),
            pieces(w_d_out),
            pieces(w_d_down),
        ],
        "xyxyyyy",
        4,
        F32,
        [v.reshape(parts, -1, D) for v in (g_source_all, g_target_all)],
    )
    g_source, g_target = ge_resid + late_sums[7], g_resid + late_sums[8]
    (
        e_qkv_sum,
        e_out_sum,
        e_down_sum,
        small_sums,
        d_qkv_sum,
        d_out_sum,
        d_down_sum,
        c_query_sum,
        c_pairs_sum,
        c_out_sum,
        d_up_sum,
        e_up_sum,
    ) = finish(late_sums[:7], early_sums, heads)
    small_sums = small_sums[:, : encoder_gains.shape[1]]
    return (
        decoded.reshape(micro, tgt_rows, D),
        g_source.reshape(micro, src_rows, D),
        g_target.reshape(micro, tgt_rows, D),
        e_qkv_sum,
        e_out_sum,
        e_up_sum,
        e_down_sum,
        small_sums[0:2],
        small_sums[2:12],
        d_qkv_sum,
        d_out_sum,
        c_query_sum,
        c_pairs_sum,
        c_out_sum,
        d_up_sum,
        d_down_sum,
        small_sums[12:15],
        small_sums[15:SMALL_ROWS],
    )


def solution(mesh):
    in_specs = (
        P(None, ("seq", "head"), None),
        P(None, ("seq", "head"), None),
        P(None, ("seq", "head"), None),
        P(),
        P(),
        P(),
        P(("seq", "head"), None),
        P(("seq", "head"), None),
        P(("seq", "head"), None),
        P(("seq", "head"), None),
        P(None, ("seq", "head")),
        P(None, ("seq", "head")),
        P(("seq", "head"), None),
        P(("seq", "head"), None),
        P(("seq", "head"), None),
        P(("seq", "head"), None),
        P(("seq", "head"), None),
        P(("seq", "head"), None),
        P(("seq", "head"), None),
        P(None, ("seq", "head")),
        P(None, ("seq", "head")),
    )
    out_specs = (
        P(None, ("seq", "head"), None),
        P(None, ("seq", "head"), None),
        P(None, ("seq", "head"), None),
        P(("seq", "head"), None),
        P(("seq", "head"), None),
        P(("seq", "head"), None),
        P(("seq", "head"), None),
        P(None, ("seq", "head")),
        P(None, ("seq", "head")),
        P(("seq", "head"), None),
        P(("seq", "head"), None),
        P(("seq", "head"), None),
        P(("seq", "head"), None),
        P(("seq", "head"), None),
        P(("seq", "head"), None),
        P(("seq", "head"), None),
        P(None, ("seq", "head")),
        P(None, ("seq", "head")),
    )
    return jax.shard_map(shards, mesh=mesh, in_specs=in_specs, out_specs=out_specs, check_vma=False)
```
